32 devices in a mesh: dp: 4 (over z), ctx: 2 (over x), tp: 4 (over y, core).
Axes of the slice: x: 2, y: 2, z: 4, core: 2. Of those that a mesh axis runs over, the one named last changes fastest.
Arguments:
- image_tokens: bfloat16 [4, 1024, 1536], P('dp', 'ctx'), may hold values from -6 to 6
- text_tokens: bfloat16 [4, 154, 1536], P('dp', 'ctx'), may hold values from -6 to 6
- conditioning: bfloat16 [4, 1536], P(None, ('dp', 'ctx')), may hold values from -5 to 5
- ada_weight: bfloat16 [2, 1536, 6, 1536], P(None, ('dp', 'ctx'), None, 'tp'), may hold values from -0.15625 to 0.15625
- ada_bias: bfloat16 [2, 6, 1536], P(None, None, 'tp'), may hold values from -1.5 to 1.5
- qkv_weight: bfloat16 [2, 1536, 3, 1536], P(None, ('dp', 'ctx'), None, 'tp'), may hold values from -0.15625 to 0.15625
- qv_bias: bfloat16 [2, 2, 1536], P(None, None, 'tp'), may hold values from -1.5 to 1.5
- out_weight: bfloat16 [2, 1536, 1536], P(None, ('dp', 'ctx'), 'tp'), may hold values from -0.875 to 0.875
- out_bias: bfloat16 [2, 1536], P(None, ('dp', 'ctx')), may hold values from -1.5 to 1.5
- up_weight: bfloat16 [2, 1536, 6144], P(None, ('dp', 'ctx'), 'tp'), may hold values from -0.15625 to 0.15625
- up_bias: bfloat16 [2, 6144], P(None, 'tp'), may hold values from -1.5 to 1.5
- down_weight: bfloat16 [2, 1536, 6144], P(None, ('dp', 'ctx'), 'tp'), may hold values from -0.078125 to 0.078125
- down_bias: bfloat16 [2, 1536], P(None, ('dp', 'ctx')), may hold values from -1.5 to 1.5
- image_cotangent: bfloat16 [4, 1024, 1536], P('dp', 'ctx'), may hold values from -6 to 6
- text_cotangent: bfloat16 [4, 154, 1536], P('dp', 'ctx'), may hold values from -6 to 6
Outputs:
- image_out: bfloat16 [4, 1024, 1536], P('dp', 'ctx')
- text_out: bfloat16 [4, 154, 1536], P('dp', 'ctx')
- image_grad: bfloat16 [4, 1024, 1536], P('dp', 'ctx')
- text_grad: bfloat16 [4, 154, 1536], P('dp', 'ctx')
- cond_grad: float32 [4, 1536], P(None, ('dp', 'ctx'))
- ada_weight_grad: float32 [2, 1536, 6, 1536], P(None, ('dp', 'ctx'), None, 'tp')
- ada_bias_grad: float32 [2, 6, 1536], P(None, None, 'tp')
- qkv_weight_grad: float32 [2, 1536, 3, 1536], P(None, ('dp', 'ctx'), None, 'tp')
- qv_bias_grad: float32 [2, 2, 1536], P(None, None, 'tp')
- out_weight_grad: float32 [2, 1536, 1536], P(None, ('dp', 'ctx'), 'tp')
- out_bias_grad: float32 [2, 1536], P(None, ('dp', 'ctx'))
- up_weight_grad: float32 [2, 1536, 6144], P(None, ('dp', 'ctx'), 'tp')
- up_bias_grad: float32 [2, 6144], P(None, 'tp')
- down_weight_grad: float32 [2, 1536, 6144], P(None, ('dp', 'ctx'), 'tp')
- down_bias_grad: float32 [2, 1536], P(None, ('dp', 'ctx'))
- root_means: float32 [6], replicated
The draws below stay inside these ranges and needn't reach their ends.
All inputs are finite; a program needn't handle non-finite values.
Results may differ from the reference program's by a relative error of at most 0.013.
Values may be sent and summed in bfloat16 or wider, within the bound.
A program may use at most 192 MiB of HBM per device.

```python
import jax
import jax.numpy as jnp
from jax import lax

D = 1536
HEADS = 24
HEAD_DIM = 64
FF = 6144
LI = 1024
LT = 154
SEQS = 4


def scaled_rows(key, length):
    position = jnp.arange(SEQS, dtype=jnp.float32) / max(SEQS - 1, 1)
    sample = jnp.clip(jax.random.normal(key, (SEQS, length, D), jnp.float32), -4.0, 4.0)
    factor = 0.5 * 3.0 ** position
    return (sample * factor[:, None, None]).astype(jnp.bfloat16)


def draw_image_tokens(key, part):
    return scaled_rows(key, LI)


def draw_text_tokens(key, part):
    return scaled_rows(jax.random.fold_in(key, 7), LT)


def levels(stream_key, dims, cuts, least, top_value):
    factor_of = 1.0
    for dim, shards_of in cuts:
        heights = jax.random.uniform(jax.random.fold_in(jax.random.fold_in(stream_key, 6), dim), (shards_of,), jnp.float32, least / len(cuts), top_value / len(cuts))
        factor_of = factor_of * jnp.repeat(jnp.exp(heights), dims[dim] // shards_of).reshape((-1,) + (1,) * (len(dims) - 1 - dim))
    return factor_of


def bell_draw(key, shape, scale, bound, shards=(), kind=jnp.bfloat16):
    values = scale * jax.random.normal(key, shape, jnp.float32)
    if shards:
        values = values * levels(key, shape, shards, -0.22, 0.18)
    return jnp.clip(values, -bound, bound).astype(kind)


def setup_inputs(seed: int = 0) -> dict:
    seeds = jax.random.split(jax.random.key(seed), 16)
    return {
        "image_tokens": draw_image_tokens(jax.random.fold_in(seeds[15], 71), 0),
        "text_tokens": draw_text_tokens(jax.random.fold_in(seeds[15], 71), 0),
        "conditioning": bell_draw(seeds[2], (SEQS, D), 1.0, 5.0, ((1, 8),)),
        "ada_weight": bell_draw(seeds[3], (2, D, 6, D), D ** -0.5, 0.15625, ((1, 8), (3, 4))),
        "ada_bias": bell_draw(seeds[4], (2, 6, D), 0.3, 1.5, ((2, 4),)),
        "qkv_weight": bell_draw(seeds[5], (2, D, 3, D), D ** -0.5, 0.15625, ((1, 8), (3, 4))),
        "qv_bias": bell_draw(seeds[6], (2, 2, D), 0.3, 1.5, ((2, 4),)),
        "out_weight": bell_draw(seeds[7], (2, D, D), (D // 32) ** -0.5, 0.875, ((1, 8), (2, 4))),
        "out_bias": bell_draw(seeds[8], (2, D), 0.3, 1.5, ((1, 8),)),
        "up_weight": bell_draw(seeds[9], (2, D, FF), D ** -0.5, 0.15625, ((1, 8), (2, 4))),
        "up_bias": bell_draw(seeds[10], (2, FF), 0.3, 1.5, ((1, 4),)),
        "down_weight": bell_draw(seeds[11], (2, D, FF), FF ** -0.5, 0.078125, ((1, 8), (2, 4))),
        "down_bias": bell_draw(seeds[12], (2, D), 0.3, 1.5, ((1, 8),)),
        "image_cotangent": bell_draw(seeds[13], (SEQS, LI, D), 1.0, 6.0, ((0, 4), (1, 2))),
        "text_cotangent": bell_draw(seeds[14], (SEQS, LT, D), 1.0, 6.0, ((0, 4), (1, 2))),
    }


@jax.custom_vjp
def low(v):
    return lax.optimization_barrier(v.astype(jnp.bfloat16)).astype(jnp.float32)

@jax.custom_vjp
def low_back(v):
    return v

def low_keep(v):
    return (low(v), None)

def low_pass(kept, grad):
    return (grad,)

def back_keep(v):
    return (v, None)

def back_low(kept, grad):
    return (low(grad),)
low.defvjp(low_keep, low_pass)
low_back.defvjp(back_keep, back_low)
PRECISE = lax.Precision.HIGHEST

def rounded_both(values):
    return low_back(low(values))

def modulate(inputs, shift_by, scale_by):
    centred = inputs - lax.optimization_barrier(jnp.mean(inputs, axis=-1, keepdims=True))
    spread = lax.optimization_barrier(jnp.mean(centred * centred, axis=-1, keepdims=True))
    return centred * lax.rsqrt(spread + 1e-06) * (1.0 + scale_by) + shift_by

def sequence_forward(params, image_rows, text_rows, conditions):
    ada_weight, ada_bias, qkv_weight, qv_bias, out_weight, out_bias, up_weight, up_bias, down_weight, down_bias = params
    activated = low(jax.nn.silu(conditions))
    modulation = low_back(jnp.einsum('d,adkf->akf', activated, ada_weight, precision=PRECISE) + ada_bias)
    streams = (image_rows, text_rows)
    queries = []
    key_list = []
    value_list = []
    for stream in range(2):
        normed = low(modulate(streams[stream], modulation[stream, 0], modulation[stream, 1]))
        projected = jnp.einsum('rd,dkf->rkf', normed, qkv_weight[stream], precision=PRECISE)
        queries.append(rounded_both(projected[:, 0] + qv_bias[stream, 0]))
        key_list.append(rounded_both(projected[:, 1]))
        value_list.append(rounded_both(projected[:, 2] + qv_bias[stream, 1]))
    length = LI + LT
    query_heads = jnp.concatenate(queries, 0).reshape(length, HEADS, HEAD_DIM)
    key_heads = jnp.concatenate(key_list, 0).reshape(length, HEADS, HEAD_DIM)
    value_heads = jnp.concatenate(value_list, 0).reshape(length, HEADS, HEAD_DIM)
    scores = low_back(jnp.einsum('qhe,khe->hqk', query_heads, key_heads, precision=PRECISE) * HEAD_DIM ** (-0.5))
    weights = low(jax.nn.softmax(scores, axis=-1))
    attended = rounded_both(jnp.einsum('hqk,khe->qhe', weights, value_heads, precision=PRECISE).reshape(length, D))
    pieces = (attended[:LI], attended[LI:])
    results = []
    squares = []
    for stream in range(2):
        attention = low_back(jnp.einsum('rf,df->rd', pieces[stream], out_weight[stream], precision=PRECISE) + out_bias[stream])
        gated_attention = modulation[stream, 2] * attention
        middle = streams[stream] + gated_attention
        second = low(modulate(middle, modulation[stream, 3], modulation[stream, 4]))
        hidden = low_back(jnp.dot(second, up_weight[stream], precision=PRECISE, preferred_element_type=jnp.float32) + up_bias[stream])
        gelu_out = low(jax.nn.gelu(hidden, approximate=True))
        feed = low_back(jnp.einsum('rf,df->rd', gelu_out, down_weight[stream], precision=PRECISE) + down_bias[stream])
        gated_feed = modulation[stream, 5] * feed
        result = middle + gated_feed
        results.append(result)
        squares.append((jnp.sum(result * result), jnp.sum(gated_attention * gated_attention), jnp.sum(gated_feed * gated_feed)))
    statistic = jnp.stack([squares[0][0], squares[1][0], squares[0][1], squares[1][1], squares[0][2], squares[1][2]])
    return ((results[0], results[1]), statistic)

def reference(image_tokens, text_tokens, conditioning, ada_weight, ada_bias, qkv_weight, qv_bias, out_weight, out_bias, up_weight, up_bias, down_weight, down_bias, image_cotangent, text_cotangent):
    params = tuple((weight.astype(jnp.float32) for weight in (ada_weight, ada_bias, qkv_weight, qv_bias, out_weight, out_bias, up_weight, up_bias, down_weight, down_bias)))

    def advance(running, inputs):
        totals, sums_so_far = running
        image_seq, text_seq, cond_seq, image_cot, text_cot = inputs
        results, pullback, statistic = jax.vjp(sequence_forward, params, image_seq.astype(jnp.float32), text_seq.astype(jnp.float32), cond_seq.astype(jnp.float32), has_aux=True)
        gradients = pullback((image_cot.astype(jnp.float32), text_cot.astype(jnp.float32)))
        totals = jax.tree.map(jnp.add, totals, gradients[0])
        emitted = (results[0].astype(jnp.bfloat16), results[1].astype(jnp.bfloat16), gradients[1].astype(jnp.bfloat16), gradients[2].astype(jnp.bfloat16), gradients[3])
        return ((totals, sums_so_far + statistic), emitted)
    initial = (jax.tree.map(jnp.zeros_like, params), jnp.zeros((6,), jnp.float32))
    (totals, statistic), emitted = lax.scan(advance, initial, (image_tokens, text_tokens, conditioning, image_cotangent, text_cotangent))
    counts = jnp.array([SEQS * LI * D, SEQS * LT * D] * 3, jnp.float32)
    root_means = jnp.sqrt(statistic / counts)
    return (emitted[0], emitted[1], emitted[2], emitted[3], emitted[4], totals[0], totals[1], totals[2], totals[3], totals[4], totals[5], totals[6], totals[7], totals[8], totals[9], root_means)
```

```python
import functools

import jax
import jax.numpy as jnp
from jax import lax
from jax.experimental import pallas as pl
from jax.experimental.pallas import tpu as pltpu
from jax.sharding import PartitionSpec as P

HEAD_DIM = 64
F32 = jnp.float32
BF16 = jnp.bfloat16
VMEM_LIMIT = 60 * 1024 * 1024
PLANE = ("ctx", "tp")
TEXT_SLOTS = 128
QUERY_BLOCK = 256


def dot(left, right, dims=((1,), (0,))):
    return lax.dot_general(left, right, (dims, ((), ())), preferred_element_type=F32)


def key_bias(rows, image_rows, text_rows):
    slot = lax.broadcasted_iota(jnp.int32, (rows, 1), 0)
    masked = jnp.logical_and(slot >= image_rows, lax.rem(slot - image_rows, TEXT_SLOTS) >= text_rows)
    return jnp.where(masked, -1e30, 0.0).astype(F32)


def attend_forward_kernel(heads, image_rows, text_rows, q_ref, k_ref, v_ref, o_ref, lse_ref, vt_ref):
    @pl.when(pl.program_id(0) == 0)
    def _():
        vt_ref[...] = v_ref[...].T

    rows = k_ref.shape[0]
    bias = key_bias(rows, image_rows, text_rows)
    queries_t = (q_ref[...] * HEAD_DIM ** (-0.5)).T
    outs = []
    for head in range(heads):
        span = slice(head * HEAD_DIM, (head + 1) * HEAD_DIM)
        scores = dot(k_ref[:, span], queries_t[span]) + bias
        top = jnp.max(scores, axis=0, keepdims=True)
        grown = jnp.exp(scores - top)
        total = jnp.sum(grown, axis=0, keepdims=True)
        lse_ref[head : head + 1] = top + jnp.log(total)
        outs.append(dot(vt_ref[span], grown.astype(BF16)) * (1.0 / total))
    o_ref[...] = jnp.concatenate(outs, 0).T.astype(BF16)


def attend_forward(q, k, v, image_rows, text_rows):
    rows, wide = q.shape
    heads = wide // HEAD_DIM
    whole = pl.BlockSpec((rows, wide), lambda i: (0, 0))
    block = pl.BlockSpec((QUERY_BLOCK, wide), lambda i: (i, 0))
    return pl.pallas_call(
        functools.partial(attend_forward_kernel, heads, image_rows, text_rows),
        grid=(rows // QUERY_BLOCK,),
        in_specs=[block, whole, whole],
        out_specs=[block, pl.BlockSpec((heads, QUERY_BLOCK), lambda i: (0, i))],
        out_shape=[
            jax.ShapeDtypeStruct((rows, wide), BF16),
            jax.ShapeDtypeStruct((heads, rows), F32),
        ],
        scratch_shapes=[pltpu.VMEM((wide, rows), BF16)],
        compiler_params=pltpu.CompilerParams(vmem_limit_bytes=VMEM_LIMIT),
        cost_estimate=pl.CostEstimate(
            flops=4 * rows * rows * wide, bytes_accessed=8 * rows * wide, transcendentals=heads * rows * rows
        ),
        name="attend_forward",
    )(q, k, v)


def attend_backward_kernel(
    heads, image_rows, text_rows, q_ref, k_ref, v_ref, g_ref, lse_ref, dq_ref, dk_ref, dv_ref, kt_ref, dk_sum, dv_sum
):
    step = pl.program_id(0)

    @pl.when(step == 0)
    def _():
        kt_ref[...] = k_ref[...].T
        dk_sum[...] = jnp.zeros_like(dk_sum)
        dv_sum[...] = jnp.zeros_like(dv_sum)

    rows = k_ref.shape[0]
    bias = key_bias(rows, image_rows, text_rows)
    queries = q_ref[...] * HEAD_DIM ** (-0.5)
    queries_t = queries.T
    grads = g_ref[...]
    grads_t = grads.T
    outs = []
    for head in range(heads):
        span = slice(head * HEAD_DIM, (head + 1) * HEAD_DIM)
        scores = dot(k_ref[:, span], queries_t[span]) + bias
        prob = jnp.exp(scores - lse_ref[head : head + 1])
        grad_prob = dot(v_ref[:, span], grads_t[span])
        weighted = prob * grad_prob
        inner = jnp.sum(weighted, axis=0, keepdims=True)
        grad_score = (weighted - prob * inner).astype(BF16)
        dv_sum[head] += dot(prob.astype(BF16), grads[:, span])
        dk_sum[head] += dot(grad_score, queries[:, span])
        outs.append(dot(kt_ref[span], grad_score) * HEAD_DIM ** (-0.5))
    dq_ref[...] = jnp.concatenate(outs, 0).T.astype(BF16)

    @pl.when(step == pl.num_programs(0) - 1)
    def _():
        dk_ref[...] = jnp.concatenate([dk_sum[head] for head in range(heads)], 1).astype(BF16)
        dv_ref[...] = jnp.concatenate([dv_sum[head] for head in range(heads)], 1).astype(BF16)


def attend_backward(q, k, v, grad, lse, image_rows, text_rows):
    rows, wide = q.shape
    heads = wide // HEAD_DIM
    whole = pl.BlockSpec((rows, wide), lambda i: (0, 0))
    block = pl.BlockSpec((QUERY_BLOCK, wide), lambda i: (i, 0))
    return pl.pallas_call(
        functools.partial(attend_backward_kernel, heads, image_rows, text_rows),
        grid=(rows // QUERY_BLOCK,),
        in_specs=[block, whole, whole, block, pl.BlockSpec((heads, QUERY_BLOCK), lambda i: (0, i))],
        out_specs=[block, whole, whole],
        out_shape=[jax.ShapeDtypeStruct((rows, wide), BF16)] * 3,
        scratch_shapes=[
            pltpu.VMEM((wide, rows), BF16),
            pltpu.VMEM((heads, rows, HEAD_DIM), F32),
            pltpu.VMEM((heads, rows, HEAD_DIM), F32),
        ],
        compiler_params=pltpu.CompilerParams(vmem_limit_bytes=VMEM_LIMIT),
        cost_estimate=pl.CostEstimate(
            flops=10 * rows * rows * wide, bytes_accessed=14 * rows * wide, transcendentals=heads * rows * rows
        ),
        name="attend_backward",
    )(q, k, v, grad, lse)


def normalise(inputs):
    centred = inputs - jnp.mean(inputs, axis=-1, keepdims=True)
    spread = lax.rsqrt(jnp.mean(centred * centred, axis=-1, keepdims=True) + 1e-06)
    return centred * spread, spread


def normalise_back(grad_norm, norm, spread):
    return spread * (
        grad_norm
        - jnp.mean(grad_norm, axis=-1, keepdims=True)
        - norm * jnp.mean(grad_norm * norm, axis=-1, keepdims=True)
    )


def gelu_parts(hidden):
    root = 0.7978845608028654
    square = hidden * hidden
    bent = jnp.tanh(hidden * (root + root * 0.044715 * square))
    half = 0.5 * (1.0 + bent)
    slope = half + 0.5 * hidden * (1.0 - bent * bent) * (root + 3.0 * root * 0.044715 * square)
    return hidden * half, slope


def plane_scatter(partial_image, partial_text):
    return tuple(
        lax.psum_scatter(part, PLANE, scatter_dimension=0, tiled=True).astype(F32)
        for part in (partial_image, partial_text)
    )


def plane_gather(own_image, own_text):
    return tuple(lax.all_gather(part, PLANE, axis=0, tiled=True) for part in (own_image, own_text))


def gather_rows(shard):
    mixed = lax.all_to_all(shard, "ctx", split_axis=2, concat_axis=1, tiled=True)[:, :, 0]
    return lax.all_gather(mixed, "dp", axis=1, tiled=True)


def scatter_rows(grad):
    mine = lax.psum_scatter(grad.astype(BF16), "dp", scatter_dimension=1, tiled=True)
    streams, rows, half = mine.shape
    ctx_n = lax.axis_size("ctx")
    split = mine.reshape(streams, ctx_n, rows // ctx_n, 1, half)
    both = lax.all_to_all(split, "ctx", split_axis=1, concat_axis=3, tiled=True)[:, 0]
    return both.astype(F32)


def on_device(
    image_tokens,
    text_tokens,
    conditioning,
    ada_weight,
    ada_bias,
    qkv_weight,
    qv_bias,
    out_weight,
    out_bias,
    up_weight,
    up_bias,
    down_weight,
    down_bias,
    image_cotangent,
    text_cotangent,
):
    ctx_n, tp_n, dp_n = lax.axis_size("ctx"), lax.axis_size("tp"), lax.axis_size("dp")
    dp, ctx, tp = lax.axis_index("dp"), lax.axis_index("ctx"), lax.axis_index("tp")
    image_length, text_length, width = image_tokens.shape[1], text_tokens.shape[1], image_tokens.shape[2]
    slice_width = qkv_weight.shape[3]
    shard_rows = qkv_weight.shape[1]
    half = slice_width // ctx_n
    up_half = up_weight.shape[2] // ctx_n
    image_own, text_own = image_length // tp_n, TEXT_SLOTS // tp_n
    image_all = image_length * ctx_n
    pad = ((0, TEXT_SLOTS - text_length), (0, 0))

    cond_float = conditioning.astype(F32)
    activated_low = jax.nn.silu(cond_float).astype(BF16)
    partial_mod = jnp.einsum("nd,adkf->nakf", activated_low, ada_weight, preferred_element_type=F32)
    mod_slices = lax.psum(partial_mod, ("dp", "ctx")) + ada_bias.astype(F32)
    own_slices = lax.dynamic_slice_in_dim(mod_slices, dp, 1, 0)[0]
    modulation = lax.all_gather(own_slices, "tp", axis=2, tiled=True)

    qkv_full = gather_rows(
        qkv_weight.reshape(2, shard_rows, 3, ctx_n, half)
        .transpose(0, 1, 3, 2, 4)
        .reshape(2, shard_rows, ctx_n, 3 * half)
    )
    out_full = gather_rows(out_weight.reshape(2, shard_rows, ctx_n, half))
    up_full = gather_rows(up_weight.reshape(2, shard_rows, ctx_n, up_half))
    down_full = gather_rows(down_weight.reshape(2, shard_rows, ctx_n, up_half))
    biases = lax.all_gather(
        jnp.concatenate([out_bias, down_bias], 0).astype(F32), ("dp", "ctx"), axis=1, tiled=True
    )
    out_bias_full, down_bias_full = biases[:2], biases[2:]
    qv_own = lax.dynamic_slice_in_dim(qv_bias, ctx * half, half, 2).astype(F32)
    up_bias_own = lax.dynamic_slice_in_dim(up_bias, ctx * up_half, up_half, 1).astype(F32)

    tokens = (image_tokens[0], jnp.pad(text_tokens[0], pad))
    cotangents = (image_cotangent[0], jnp.pad(text_cotangent[0], pad))
    tokens_all = [lax.all_gather(part, "ctx", axis=0, tiled=True) for part in tokens]
    cotangents_all = [lax.all_gather(part, "ctx", axis=0, tiled=True) for part in cotangents]
    own_rows = (image_own, text_own)

    def own(parts):
        return [
            lax.dynamic_slice_in_dim(part, tp * rows, rows, 0).astype(F32)
            for part, rows in zip(parts, own_rows)
        ]

    tokens_own, cotangents_own = own(tokens), own(cotangents)
    text_valid = (tp * text_own + lax.broadcasted_iota(jnp.int32, (text_own, 1), 0)) < text_length
    valid = (jnp.ones((image_own, 1), F32), text_valid.astype(F32))

    normed_low, qkv_parts = [], []
    for stream in range(2):
        norm, _ = normalise(tokens_all[stream].astype(F32))
        normed = (norm * (1.0 + modulation[stream, 1]) + modulation[stream, 0]).astype(BF16)
        normed_low.append(normed)
        bias = jnp.concatenate([qv_own[stream, 0], jnp.zeros((half,), F32), qv_own[stream, 1]])
        qkv_parts.append((dot(normed, qkv_full[stream]) + bias).astype(BF16))
    joint = jnp.concatenate(qkv_parts, 0)
    queries, keys, values = joint[:, :half], joint[:, half : 2 * half], joint[:, 2 * half :]
    blended, lse = attend_forward(queries, keys, values, image_all, text_length)
    blended_parts = (blended[:image_all], blended[image_all:])
    attention_own = plane_scatter(
        *[dot(blended_parts[s], out_full[s], ((1,), (1,))).astype(BF16) for s in range(2)]
    )
    attention, middles, norms2, spreads2, second_own = [], [], [], [], []
    for stream in range(2):
        branch = attention_own[stream] + out_bias_full[stream]
        middle = tokens_own[stream] + modulation[stream, 2] * branch
        norm, spread = normalise(middle)
        attention.append(branch)
        middles.append(middle)
        norms2.append(norm)
        spreads2.append(spread)
        second_own.append((norm * (1.0 + modulation[stream, 4]) + modulation[stream, 3]).astype(BF16))
    second_low = plane_gather(*second_own)

    feed_parts, second_parts = [], []
    down_weight_grads, up_weight_grads, down_bias_grads, up_bias_grads = [], [], [], []
    for stream in range(2):
        hidden = dot(second_low[stream], up_full[stream]) + up_bias_own[stream]
        gelu_out, slope = gelu_parts(hidden)
        gelu_low = gelu_out.astype(BF16)
        feed_parts.append(dot(gelu_low, down_full[stream], ((1,), (1,))).astype(BF16))
        grad_feed = (cotangents_all[stream].astype(F32) * modulation[stream, 5]).astype(BF16)
        down_weight_grads.append(dot(grad_feed, gelu_low, ((0,), (0,))))
        grad_hidden = (dot(grad_feed, down_full[stream]) * slope).astype(BF16)
        up_bias_grads.append(jnp.sum(grad_hidden.astype(F32), axis=0))
        up_weight_grads.append(dot(second_low[stream], grad_hidden, ((0,), (0,))))
        second_parts.append(dot(grad_hidden, up_full[stream], ((1,), (1,))).astype(BF16))
        own_feed = (cotangents[stream].astype(F32) * modulation[stream, 5]).astype(BF16)
        down_bias_grads.append(jnp.sum(own_feed.astype(F32), axis=0))
    feed_own = plane_scatter(*feed_parts)
    grad_second = plane_scatter(*second_parts)
    down_weight_grad = scatter_rows(jnp.stack(down_weight_grads)).reshape(2, shard_rows, -1)
    up_weight_grad = scatter_rows(jnp.stack(up_weight_grads)).reshape(2, shard_rows, -1)

    outputs, squares, mod_grads, grad_middles, attention_grads, out_bias_grads = [], [], [], [], [], []
    for stream in range(2):
        feed = feed_own[stream] + down_bias_full[stream]
        gated_attention = modulation[stream, 2] * attention[stream]
        gated_feed = modulation[stream, 5] * feed
        result = middles[stream] + gated_feed
        outputs.append(result.astype(BF16))
        squares.append(
            [jnp.sum(part * part * valid[stream]) for part in (result, gated_attention, gated_feed)]
        )
        grad_scaled = grad_second[stream] * (1.0 + modulation[stream, 4])
        grad_middle = cotangents_own[stream] + normalise_back(grad_scaled, norms2[stream], spreads2[stream])
        grad_attention = (grad_middle * modulation[stream, 2]).astype(BF16)
        grad_middles.append(grad_middle)
        attention_grads.append(grad_attention)
        out_bias_grads.append(jnp.sum(grad_attention.astype(F32), axis=0))
        mod_grads.append(
            [
                jnp.sum(grad_middle * attention[stream], axis=0),
                jnp.sum(grad_second[stream], axis=0),
                jnp.sum(grad_second[stream] * norms2[stream], axis=0),
                jnp.sum(cotangents_own[stream] * feed, axis=0),
            ]
        )
    attention_grad_all = plane_gather(*attention_grads)

    out_weight_grads, blended_grads = [], []
    for stream in range(2):
        out_weight_grads.append(dot(attention_grad_all[stream], blended_parts[stream], ((0,), (0,))))
        blended_grads.append(dot(attention_grad_all[stream], out_full[stream]).astype(BF16))
    grad_queries, grad_keys, grad_values = attend_backward(
        queries, keys, values, jnp.concatenate(blended_grads, 0), lse, image_all, text_length
    )
    grad_joint = jnp.concatenate([grad_queries, grad_keys, grad_values], 1)
    grad_parts = (grad_joint[:image_all], grad_joint[image_all:])
    qkv_weight_grads, qv_bias_grads, normed_parts = [], [], []
    for stream in range(2):
        sums = jnp.sum(grad_parts[stream].astype(F32), axis=0)
        qv_bias_grads.append(jnp.stack([sums[:half], sums[2 * half :]]))
        qkv_weight_grads.append(dot(normed_low[stream], grad_parts[stream], ((0,), (0,))))
        normed_parts.append(dot(grad_parts[stream], qkv_full[stream], ((1,), (1,))).astype(BF16))
    grad_normed = plane_scatter(*normed_parts)
    out_weight_grad = scatter_rows(jnp.stack(out_weight_grads)).reshape(2, shard_rows, -1)
    qkv_weight_grad = (
        scatter_rows(jnp.stack(qkv_weight_grads))
        .reshape(2, shard_rows, ctx_n, 3, half)
        .transpose(0, 1, 3, 2, 4)
        .reshape(2, shard_rows, 3, slice_width)
    )

    token_grads, mod_streams = [], []
    for stream in range(2):
        norm, spread = normalise(tokens_own[stream])
        grad_scaled = grad_normed[stream] * (1.0 + modulation[stream, 1])
        grad_tokens = grad_middles[stream] + normalise_back(grad_scaled, norm, spread)
        token_grads.append(grad_tokens.astype(BF16))
        mod_streams.append(
            jnp.stack(
                [jnp.sum(grad_normed[stream], axis=0), jnp.sum(grad_normed[stream] * norm, axis=0)]
                + mod_grads[stream]
            )
        )
    finals = [
        lax.all_gather(part, "tp", axis=0, tiled=True) for part in (*outputs, *token_grads)
    ]
    grad_mod = lax.psum_scatter(jnp.stack(mod_streams), "tp", scatter_dimension=2, tiled=True)
    grad_mod = lax.psum(grad_mod, "ctx")
    grad_mod_low = lax.all_gather(grad_mod, "dp", axis=0).astype(BF16)
    ada_bias_grad = jnp.sum(grad_mod_low.astype(F32), axis=0)
    ada_weight_grad = jnp.einsum("nd,nakf->adkf", activated_low, grad_mod_low, preferred_element_type=F32)
    cond_partial = jnp.einsum("nakf,adkf->nd", grad_mod_low, ada_weight, preferred_element_type=F32)
    cond_total = lax.psum(cond_partial, "tp")
    cond_grad = jax.vjp(jax.nn.silu, cond_float)[1](cond_total)[0]

    bias_rows = lax.psum_scatter(
        jnp.concatenate(
            [jnp.stack(down_bias_grads) * (tp == 0).astype(F32), jnp.stack(out_bias_grads)], 0
        ),
        ("dp", "ctx"),
        scatter_dimension=1,
        tiled=True,
    )
    bias_rows = lax.psum(bias_rows, "tp")
    qv_local = lax.dynamic_update_slice_in_dim(
        jnp.zeros((2, 2, slice_width), F32), jnp.stack(qv_bias_grads), ctx * half, 2
    )
    up_local = lax.dynamic_update_slice_in_dim(
        jnp.zeros((2, up_bias.shape[1]), F32), jnp.stack(up_bias_grads), ctx * up_half, 1
    )
    qv_bias_grad, up_bias_grad = lax.psum((qv_local, up_local), ("dp", "ctx"))
    squares_local = jnp.stack([squares[s][term] for term in range(3) for s in range(2)])
    squares_total = lax.psum(squares_local, ("dp", "ctx", "tp"))
    counts = jnp.array([image_length, text_length] * 3, F32) * (dp_n * ctx_n * width)
    root_means = jnp.sqrt(squares_total / counts)
    return (
        finals[0][None],
        finals[1][None, :text_length],
        finals[2][None],
        finals[3][None, :text_length],
        cond_grad,
        ada_weight_grad,
        ada_bias_grad,
        qkv_weight_grad,
        qv_bias_grad,
        out_weight_grad,
        bias_rows[2:],
        up_weight_grad,
        up_bias_grad,
        down_weight_grad,
        bias_rows[:2],
        root_means,
    )


def solution(mesh):
    rows = P(None, ("dp", "ctx"))
    tokens = P("dp", "ctx", None)
    stacked = P(None, ("dp", "ctx"), None, "tp")
    matrix = P(None, ("dp", "ctx"), "tp")
    return jax.shard_map(
        on_device,
        mesh=mesh,
        in_specs=(
            tokens,
            tokens,
            rows,
            stacked,
            P(None, None, "tp"),
            stacked,
            P(None, None, "tp"),
            matrix,
            rows,
            matrix,
            P(None, "tp"),
            matrix,
            rows,
            tokens,
            tokens,
        ),
        out_specs=(
            tokens,
            tokens,
            tokens,
            tokens,
            rows,
            stacked,
            P(None, None, "tp"),
            stacked,
            P(None, None, "tp"),
            matrix,
            rows,
            matrix,
            P(None, "tp"),
            matrix,
            rows,
            P(),
        ),
        check_vma=False,
    )
```

```python
import functools

import jax
import jax.numpy as jnp
from jax import lax
from jax.experimental import pallas as pl
from jax.experimental.pallas import tpu as pltpu
from jax.sharding import PartitionSpec as P

HEAD_DIM = 64
F32 = jnp.float32
BF16 = jnp.bfloat16
VMEM_LIMIT = 60 * 1024 * 1024
PLANE = ("ctx", "tp")
TEXT_SLOTS = 96
JOINT_STEP = 256
QUERY_BLOCK = 256


def dot(left, right, dims=((1,), (0,))):
    return lax.dot_general(left, right, (dims, ((), ())), preferred_element_type=F32)


def key_bias(rows, image_rows, text_rows):
    slot = lax.broadcasted_iota(jnp.int32, (rows, 1), 0)
    text_slot = slot - image_rows
    unused = jnp.logical_or(lax.rem(text_slot, TEXT_SLOTS) >= text_rows, text_slot >= 2 * TEXT_SLOTS)
    masked = jnp.logical_and(text_slot >= 0, unused)
    return jnp.where(masked, -1e30, 0.0).astype(F32)


def attend_forward_kernel(heads, image_rows, text_rows, q_ref, k_ref, v_ref, o_ref, lse_ref, vt_ref):
    @pl.when(pl.program_id(0) == 0)
    def _():
        vt_ref[...] = v_ref[...].T

    rows = k_ref.shape[0]
    bias = key_bias(rows, image_rows, text_rows)
    queries_t = (q_ref[...] * HEAD_DIM ** (-0.5)).T
    outs = []
    for head in range(heads):
        span = slice(head * HEAD_DIM, (head + 1) * HEAD_DIM)
        scores = dot(k_ref[:, span], queries_t[span]) + bias
        top = jnp.max(scores, axis=0, keepdims=True)
        grown = jnp.exp(scores - top)
        total = jnp.sum(grown, axis=0, keepdims=True)
        lse_ref[head : head + 1] = top + jnp.log(total)
        outs.append(dot(vt_ref[span], grown.astype(BF16)) * (1.0 / total))
    o_ref[...] = jnp.concatenate(outs, 0).T.astype(BF16)


def attend_forward(q, k, v, image_rows, text_rows):
    rows, wide = q.shape
    heads = wide // HEAD_DIM
    whole = pl.BlockSpec((rows, wide), lambda i: (0, 0))
    block = pl.BlockSpec((QUERY_BLOCK, wide), lambda i: (i, 0))
    return pl.pallas_call(
        functools.partial(attend_forward_kernel, heads, image_rows, text_rows),
        grid=(rows // QUERY_BLOCK,),
        in_specs=[block, whole, whole],
        out_specs=[block, pl.BlockSpec((heads, QUERY_BLOCK), lambda i: (0, i))],
        out_shape=[
            jax.ShapeDtypeStruct((rows, wide), BF16),
            jax.ShapeDtypeStruct((heads, rows), F32),
        ],
        scratch_shapes=[pltpu.VMEM((wide, rows), BF16)],
        compiler_params=pltpu.CompilerParams(vmem_limit_bytes=VMEM_LIMIT),
        cost_estimate=pl.CostEstimate(
            flops=4 * rows * rows * wide, bytes_accessed=8 * rows * wide, transcendentals=heads * rows * rows
        ),
        name="attend_forward",
    )(q, k, v)


def attend_backward_kernel(
    heads, image_rows, text_rows, q_ref, k_ref, v_ref, g_ref, lse_ref, dq_ref, dk_ref, dv_ref, kt_ref, dk_sum, dv_sum
):
    step = pl.program_id(0)

    @pl.when(step == 0)
    def _():
        kt_ref[...] = k_ref[...].T
        dk_sum[...] = jnp.zeros_like(dk_sum)
        dv_sum[...] = jnp.zeros_like(dv_sum)

    rows = k_ref.shape[0]
    bias = key_bias(rows, image_rows, text_rows)
    queries = q_ref[...] * HEAD_DIM ** (-0.5)
    queries_t = queries.T
    grads = g_ref[...]
    grads_t = grads.T
    outs = []
    for head in range(heads):
        span = slice(head * HEAD_DIM, (head + 1) * HEAD_DIM)
        scores = dot(k_ref[:, span], queries_t[span]) + bias
        prob = jnp.exp(scores - lse_ref[head : head + 1])
        grad_prob = dot(v_ref[:, span], grads_t[span])
        weighted = prob * grad_prob
        inner = jnp.sum(weighted, axis=0, keepdims=True)
        grad_score = (weighted - prob * inner).astype(BF16)
        dv_sum[head] += dot(prob.astype(BF16), grads[:, span])
        dk_sum[head] += dot(grad_score, queries[:, span])
        outs.append(dot(kt_ref[span], grad_score) * HEAD_DIM ** (-0.5))
    dq_ref[...] = jnp.concatenate(outs, 0).T.astype(BF16)

    @pl.when(step == pl.num_programs(0) - 1)
    def _():
        dk_ref[...] = jnp.concatenate([dk_sum[head] for head in range(heads)], 1).astype(BF16)
        dv_ref[...] = jnp.concatenate([dv_sum[head] for head in range(heads)], 1).astype(BF16)


def attend_backward(q, k, v, grad, lse, image_rows, text_rows):
    rows, wide = q.shape
    heads = wide // HEAD_DIM
    whole = pl.BlockSpec((rows, wide), lambda i: (0, 0))
    block = pl.BlockSpec((QUERY_BLOCK, wide), lambda i: (i, 0))
    return pl.pallas_call(
        functools.partial(attend_backward_kernel, heads, image_rows, text_rows),
        grid=(rows // QUERY_BLOCK,),
        in_specs=[block, whole, whole, block, pl.BlockSpec((heads, QUERY_BLOCK), lambda i: (0, i))],
        out_specs=[block, whole, whole],
        out_shape=[jax.ShapeDtypeStruct((rows, wide), BF16)] * 3,
        scratch_shapes=[
            pltpu.VMEM((wide, rows), BF16),
            pltpu.VMEM((heads, rows, HEAD_DIM), F32),
            pltpu.VMEM((heads, rows, HEAD_DIM), F32),
        ],
        compiler_params=pltpu.CompilerParams(vmem_limit_bytes=VMEM_LIMIT),
        cost_estimate=pl.CostEstimate(
            flops=10 * rows * rows * wide, bytes_accessed=14 * rows * wide, transcendentals=heads * rows * rows
        ),
        name="attend_backward",
    )(q, k, v, grad, lse)


def normalise(inputs):
    centred = inputs - jnp.mean(inputs, axis=-1, keepdims=True)
    spread = lax.rsqrt(jnp.mean(centred * centred, axis=-1, keepdims=True) + 1e-06)
    return centred * spread, spread


def normalise_back(grad_norm, norm, spread):
    return spread * (
        grad_norm
        - jnp.mean(grad_norm, axis=-1, keepdims=True)
        - norm * jnp.mean(grad_norm * norm, axis=-1, keepdims=True)
    )


def gelu_parts(hidden):
    root = 0.7978845608028654
    square = hidden * hidden
    bent = jnp.tanh(hidden * (root + root * 0.044715 * square))
    half = 0.5 * (1.0 + bent)
    slope = half + 0.5 * hidden * (1.0 - bent * bent) * (root + 3.0 * root * 0.044715 * square)
    return hidden * half, slope


MESH = pl.DeviceIdType.MESH
VMEM_SPEC = pl.BlockSpec(memory_space=pltpu.VMEM)
ANY_SPEC = pl.BlockSpec(memory_space=pl.ANY)


class Wires:
    def __init__(self, send_sems, recv_sems):
        self.dp, self.x, self.tp = lax.axis_index("dp"), lax.axis_index("ctx"), lax.axis_index("tp")
        self.y, self.k = self.tp // 2, self.tp % 2
        self.x_next = (self.dp, 1 - self.x, self.tp)
        self.y_next = (self.dp, self.x, (1 - self.y) * 2 + self.k)
        self.k_next = (self.dp, self.x, self.y * 2 + 1 - self.k)
        self.send_sems, self.recv_sems, self.used = send_sems, recv_sems, 0
        self.started = []

    def copy(self, source, target, device):
        wire = pltpu.make_async_remote_copy(
            src_ref=source,
            dst_ref=target,
            send_sem=self.send_sems.at[self.used],
            recv_sem=self.recv_sems.at[self.used],
            device_id=device,
            device_id_type=MESH,
        )
        self.used += 1
        wire.start()
        self.started.append(wire)
        return wire

    def meet(self, devices):
        barrier = pltpu.get_barrier_semaphore()
        for device in devices:
            pl.semaphore_signal(barrier, inc=1, device_id=device, device_id_type=MESH)
        pl.semaphore_wait(barrier, len(devices))

    def finish(self):
        for wire in self.started:
            wire.wait_send()


def row_step(rows):
    return 32 if rows % 32 == 0 else rows


def over_rows(rows, body):
    step = row_step(rows)
    if step == rows:
        body(slice(0, rows))
        return

    def one(index, carry):
        body(pl.ds(pl.multiple_of(index * step, step), step))
        return carry

    lax.fori_loop(0, rows // step, one, 0)


def reduce_plane(wires, streams):
    x, y, k = wires.x, wires.y, wires.k
    first = [wires.copy(s["part"].at[:, :, 1 - k], s["core"], wires.k_next) for s in streams]
    second = []
    for s, arrived in zip(streams, first):
        part, core, held = s["part"], s["core"], s["held"]
        rows, width = part.shape[3], part.shape[4]
        cut = width // 2
        arrived.wait_recv()
        for i in range(2):
            for j in range(2):

                def add(span, i=i, j=j):
                    held[i, j, span] = (part[i, j, k, span].astype(F32) + core[i, j, span].astype(F32)).astype(BF16)

                over_rows(rows, add)
        second.append(
            (
                wires.copy(held.at[:, 1 - y, :, pl.ds(0, cut)], s["along_y"], wires.y_next),
                wires.copy(held.at[1 - x, :, :, pl.ds(cut, cut)], s["along_x"], wires.x_next),
            )
        )
    third = []
    for s, (from_y, from_x) in zip(streams, second):
        held, along_y, along_x, out_x, out_y = s["held"], s["along_y"], s["along_x"], s["out_x"], s["out_y"]
        rows, width = held.shape[2], held.shape[3]
        cut = width // 2
        from_y.wait_recv()
        from_x.wait_recv()

        def add(span):
            out_x[span] = (
                held[1 - x, y, span, :cut].astype(F32) + along_y[1 - x, span].astype(F32)
            ).astype(BF16)
            out_y[span] = (
                held[x, 1 - y, span, cut:].astype(F32) + along_x[1 - y, span].astype(F32)
            ).astype(BF16)

        over_rows(rows, add)
        third.append(
            (
                wires.copy(out_x, s["last_x"], wires.x_next),
                wires.copy(out_y, s["last_y"], wires.y_next),
            )
        )
    for s, (from_x, from_y) in zip(streams, third):
        held, along_y, along_x, last_x, last_y, total = (
            s["held"],
            s["along_y"],
            s["along_x"],
            s["last_x"],
            s["last_y"],
            s["total"],
        )
        rows, width = held.shape[2], held.shape[3]
        cut = width // 2
        from_x.wait_recv()
        from_y.wait_recv()

        def add(span):
            total[span, :cut] = (
                held[x, y, span, :cut].astype(F32) + along_y[x, span].astype(F32) + last_x[span].astype(F32)
            )
            total[span, cut:] = (
                held[x, y, span, cut:].astype(F32) + along_x[y, span].astype(F32) + last_y[span].astype(F32)
            )

        over_rows(rows, add)


REDUCE_KEYS = ("core", "held", "along_y", "along_x", "out_x", "out_y", "last_x", "last_y", "total")


def reduce_scratch(rows, width):
    half = width // 2
    return [
        pltpu.VMEM((2, 2, rows, width), BF16),
        pltpu.VMEM((2, 2, rows, width), BF16),
        pltpu.VMEM((2, rows, half), BF16),
        pltpu.VMEM((2, rows, half), BF16),
        pltpu.VMEM((rows, half), BF16),
        pltpu.VMEM((rows, half), BF16),
        pltpu.VMEM((rows, half), BF16),
        pltpu.VMEM((rows, half), BF16),
        pltpu.VMEM((rows, width), F32),
    ]


def spread_plane(wires, blocks):
    x, y, k = wires.x, wires.y, wires.k
    first = []
    for block in blocks:
        cut = block.shape[4] // 2
        low, high = pl.ds(0, cut), pl.ds(cut, cut)
        mine = block.at[x, y, k, :, low], block.at[x, y, k, :, high]
        first.append((wires.copy(mine[0], mine[0], wires.x_next), wires.copy(mine[1], mine[1], wires.y_next)))
    second = []
    for block, (from_x, from_y) in zip(blocks, first):
        cut = block.shape[4] // 2
        low, high = pl.ds(0, cut), pl.ds(cut, cut)
        from_x.wait_recv()
        from_y.wait_recv()
        lows, highs = block.at[:, y, k, :, low], block.at[x, :, k, :, high]
        second.append((wires.copy(lows, lows, wires.y_next), wires.copy(highs, highs, wires.x_next)))
    third = []
    for block, (from_y, from_x) in zip(blocks, second):
        from_y.wait_recv()
        from_x.wait_recv()
        gathered = block.at[:, :, k]
        third.append(wires.copy(gathered, gathered, wires.k_next))
    for arrived in third:
        arrived.wait_recv()


def comm_call(kernel, outs, scratch, wires, collective_id, name, in_specs, out_specs):
    return pl.pallas_call(
        kernel,
        out_shape=outs,
        in_specs=in_specs,
        out_specs=out_specs,
        scratch_shapes=scratch + [pltpu.SemaphoreType.DMA((wires,)), pltpu.SemaphoreType.DMA((wires,))],
        compiler_params=pltpu.CompilerParams(
            collective_id=collective_id, has_side_effects=True, vmem_limit_bytes=VMEM_LIMIT
        ),
        name=name,
    )


def enter_kernel(
    n_dp,
    part_ref,
    bias_ref,
    rows_ref,
    image_ref,
    text_ref,
    mod_ref,
    rows_out,
    image_out,
    text_out,
    mod_in,
    local_sems,
    send_sems,
    recv_sems,
):
    wires = Wires(send_sems, recv_sems)
    dp, x, y, k, tp = wires.dp, wires.x, wires.y, wires.k, wires.tp
    count = n_dp * 2
    me = dp * 2 + x
    peers = [lax.rem(me + offset, count) for offset in range(1, count)]
    others = [(peer // 2, peer % 2, tp) for peer in peers]
    lanes = [lax.rem(tp + offset, 4) for offset in range(1, 4)]
    wires.meet(others + [(dp, x, lane) for lane in lanes])

    keep = [
        pltpu.make_async_copy(image_ref, image_out.at[x], local_sems.at[0]),
        pltpu.make_async_copy(text_ref, text_out.at[x], local_sems.at[1]),
    ]
    streams = ((image_ref, image_out), (text_ref, text_out))
    sums = [wires.copy(part_ref.at[peer // 2], mod_in.at[me], other) for peer, other in zip(peers, others)]
    rows = [wires.copy(rows_ref, rows_out.at[me], other) for other in others]
    along_x = [wires.copy(ref.at[tp], out.at[x, tp], wires.x_next) for ref, out in streams]
    for local in keep:
        local.start()
    mod_in[me] = part_ref[dp]
    rows_out[me] = rows_ref[...]
    for arrived in sums:
        arrived.wait_recv()
    total = bias_ref[...]
    for source in range(count):
        total = total + mod_in[source]
    mod_ref[tp] = total
    mods = [wires.copy(mod_ref.at[tp], mod_ref.at[tp], (dp, x, lane)) for lane in lanes]
    along_y = []
    for (_, out), arrived in zip(streams, along_x):
        arrived.wait_recv()
        block = out.at[1 - x, tp]
        along_y.append(wires.copy(block, block, wires.y_next))
    across = []
    for _, out in streams:
        block = out.at[1 - x, tp]
        across.append(wires.copy(block, block, wires.k_next))
    far = (1 - y) * 2 + k
    for (_, out), arrived in zip(streams, along_y):
        arrived.wait_recv()
        block = out.at[1 - x, far]
        across.append(wires.copy(block, block, wires.k_next))
    for arrived in mods + rows + across:
        arrived.wait_recv()
    for local in keep:
        local.wait()
    wires.finish()


def enter(partial_mod, ada_bias, bias_rows, image, text):
    n_dp, kinds, wide = partial_mod.shape
    count = 2 * n_dp
    tp_n = image.shape[0]
    return comm_call(
        functools.partial(enter_kernel, n_dp),
        [
            jax.ShapeDtypeStruct((tp_n, kinds, wide), F32),
            jax.ShapeDtypeStruct((count,) + bias_rows.shape, F32),
            jax.ShapeDtypeStruct((2,) + image.shape, BF16),
            jax.ShapeDtypeStruct((2,) + text.shape, BF16),
        ],
        [pltpu.VMEM((count, kinds, wide), F32), pltpu.SemaphoreType.DMA((2,))],
        2 * (count - 1) + 3 + 8,
        0,
        "enter",
        [VMEM_SPEC] * 3 + [ANY_SPEC] * 2,
        [VMEM_SPEC] * 2 + [ANY_SPEC] * 2,
    )(partial_mod, ada_bias, bias_rows, image, text)


def middle_kernel(
    image_part,
    text_part,
    image_x,
    text_x,
    mod_ref,
    bias_ref,
    image_attention,
    text_attention,
    image_middle,
    text_middle,
    image_all,
    text_all,
    *scratch,
):
    send_sems, recv_sems = scratch[-2:]
    wires = Wires(send_sems, recv_sems)
    x, y, k = wires.x, wires.y, wires.k
    wires.meet([wires.x_next, wires.y_next, wires.k_next])
    size = len(REDUCE_KEYS)
    streams = [
        dict(zip(("part",) + REDUCE_KEYS, (part,) + scratch[i * size : (i + 1) * size]))
        for i, part in enumerate((image_part, text_part))
    ]
    reduce_plane(wires, streams)
    for i, (tokens, attention, middle, gathered) in enumerate(
        ((image_x, image_attention, image_middle, image_all), (text_x, text_attention, text_middle, text_all))
    ):
        total = streams[i]["total"]

        def finish(span, i=i, tokens=tokens, attention=attention, middle=middle, gathered=gathered, total=total):
            branch = total[span] + bias_ref[i]
            attention[span] = branch
            value = tokens[span].astype(F32) + mod_ref[i, 2] * branch
            middle[span] = value
            norm, _ = normalise(value)
            gathered[x, y, k, span] = (norm * (1.0 + mod_ref[i, 4]) + mod_ref[i, 3]).astype(BF16)

        over_rows(total.shape[0], finish)
    spread_plane(wires, [image_all, text_all])
    wires.finish()


def middle_step(image_part, text_part, image_x, text_x, mod, bias):
    (image_rows, width), text_rows = image_x.shape, text_x.shape[0]
    outs = []
    for _ in range(2):
        outs += [jax.ShapeDtypeStruct((rows, width), F32) for rows in (image_rows, text_rows)]
    outs += [jax.ShapeDtypeStruct(part.shape, BF16) for part in (image_part, text_part)]
    return comm_call(
        middle_kernel,
        outs,
        reduce_scratch(image_rows, width) + reduce_scratch(text_rows, width),
        20,
        1,
        "middle",
        [VMEM_SPEC] * 6,
        [VMEM_SPEC] * 6,
    )(image_part, text_part, image_x, text_x, mod, bias)


def turn_kernel(
    valid_ref,
    image_feed,
    text_feed,
    image_second,
    text_second,
    image_attention,
    text_attention,
    image_middle,
    text_middle,
    image_cot,
    text_cot,
    mod_ref,
    bias_ref,
    image_out,
    text_out,
    image_grad,
    text_grad,
    sums_ref,
    image_all,
    text_all,
    *scratch,
):
    send_sems, recv_sems = scratch[-2:]
    wires = Wires(send_sems, recv_sems)
    x, y, k = wires.x, wires.y, wires.k
    wires.meet([wires.x_next, wires.y_next, wires.k_next])
    size = len(REDUCE_KEYS)
    streams = [
        dict(zip(("part",) + REDUCE_KEYS, (part,) + scratch[i * size : (i + 1) * size]))
        for i, part in enumerate((image_second, text_second, image_feed, text_feed))
    ]
    reduce_plane(wires, streams)
    sums_ref[...] = jnp.zeros_like(sums_ref)
    groups = (
        (image_attention, image_middle, image_cot, image_out, image_grad, image_all),
        (text_attention, text_middle, text_cot, text_out, text_grad, text_all),
    )
    for i, (attention, middle, cot, out, grad, gathered) in enumerate(groups):
        second, feed = streams[i]["total"], streams[2 + i]["total"]

        def finish(span, i=i, attention=attention, middle=middle, cot=cot, out=out, grad=grad, gathered=gathered, second=second, feed=feed):
            branch, value, arriving, pulled = attention[span], middle[span], cot[span].astype(F32), second[span]
            fed = feed[span] + bias_ref[i]
            gated_branch = mod_ref[i, 2] * branch
            gated_feed = mod_ref[i, 5] * fed
            result = value + gated_feed
            out[span] = result.astype(BF16)
            norm, spread = normalise(value)
            grad_middle = arriving + normalise_back(pulled * (1.0 + mod_ref[i, 4]), norm, spread)
            grad[span] = grad_middle
            low = (grad_middle * mod_ref[i, 2]).astype(BF16)
            gathered[x, y, k, span] = low
            if i == 1:
                kept = valid_ref[span]
                result, gated_branch, gated_feed = result * kept, gated_branch * kept, gated_feed * kept
            own_feed = (arriving * mod_ref[i, 5]).astype(BF16).astype(F32)
            terms = (
                grad_middle * branch,
                pulled,
                pulled * norm,
                arriving * fed,
                own_feed,
                low.astype(F32),
                result * result,
                gated_branch * gated_branch,
                gated_feed * gated_feed,
            )
            for t, term in enumerate(terms):
                sums_ref[i, t : t + 1] += jnp.sum(term, axis=0, keepdims=True)

        over_rows(second.shape[0], finish)
    spread_plane(wires, [image_all, text_all])
    wires.finish()


def turn_step(valid, feeds, seconds, attentions, middles, cots, mod, bias):
    width = middles[0].shape[1]
    rows = [part.shape[0] for part in middles]
    outs = [jax.ShapeDtypeStruct((r, width), BF16) for r in rows]
    outs += [jax.ShapeDtypeStruct((r, width), F32) for r in rows]
    outs += [jax.ShapeDtypeStruct((2, 16, width), F32)]
    outs += [jax.ShapeDtypeStruct(part.shape, BF16) for part in feeds]
    scratch = []
    for _ in range(2):
        for r in rows:
            scratch += reduce_scratch(r, width)
    return comm_call(
        turn_kernel, outs, scratch, 30, 2, "turn", [VMEM_SPEC] * 13, [VMEM_SPEC] * 7
    )(valid, *feeds, *seconds, *attentions, *middles, *cots, mod, bias)


PACKED = 24


def leave_kernel(
    n_dp,
    image_part,
    text_part,
    image_x,
    text_x,
    image_grad,
    text_grad,
    image_out,
    text_out,
    sums_ref,
    mod_ref,
    halves_ref,
    image_outs,
    text_outs,
    image_grads,
    text_grads,
    packed_out,
    halves_out,
    *scratch,
):
    send_sems, recv_sems = scratch[-2:]
    packed, packed_in, own_sums, both_halves, local_sums = scratch[-7:-2]
    wires = Wires(send_sems, recv_sems)
    dp, x, y, k, tp = wires.dp, wires.x, wires.y, wires.k, wires.tp
    me = x * 4 + tp
    peers = [lax.rem(me + offset, 8) for offset in range(1, 8)]
    planes = [lax.rem(dp + offset, n_dp) for offset in range(1, n_dp)]
    wires.meet([(dp, peer // 4, peer % 4) for peer in peers] + [(plane, x, tp) for plane in planes])

    image_outs[tp] = image_out[...]
    text_outs[tp] = text_out[...]
    both_halves[x] = halves_ref[...]
    halves = wires.copy(both_halves.at[x], both_halves.at[x], wires.x_next)
    size = len(REDUCE_KEYS)
    streams = [
        dict(zip(("part",) + REDUCE_KEYS, (part,) + scratch[i * size : (i + 1) * size]))
        for i, part in enumerate((image_part, text_part))
    ]
    reduce_plane(wires, streams)
    local_sums[...] = jnp.zeros_like(local_sums)
    for i, (tokens, grad, all_grads) in enumerate(
        ((image_x, image_grad, image_grads), (text_x, text_grad, text_grads))
    ):
        total = streams[i]["total"]

        def finish(span, i=i, tokens=tokens, grad=grad, all_grads=all_grads, total=total):
            pulled = total[span]
            norm, spread = normalise(tokens[span].astype(F32))
            grad_tokens = grad[span] + normalise_back(pulled * (1.0 + mod_ref[i, 1]), norm, spread)
            all_grads[tp, span] = grad_tokens.astype(BF16)
            local_sums[2 * i : 2 * i + 1] += jnp.sum(pulled, axis=0, keepdims=True)
            local_sums[2 * i + 1 : 2 * i + 2] += jnp.sum(pulled * norm, axis=0, keepdims=True)

        over_rows(total.shape[0], finish)
    wide = packed.shape[2]
    for t in range(4):
        cols = slice(t * wide, (t + 1) * wide)
        for i in range(2):
            packed[t, 6 * i : 6 * i + 2] = local_sums[2 * i : 2 * i + 2, cols]
            packed[t, 6 * i + 2 : 6 * i + 6] = sums_ref[i, 0:4, cols]
            packed[t, 12 + 5 * i : 12 + 5 * i + 5] = sums_ref[i, 4:9, cols]
        packed[t, 22:24] = jnp.zeros((2, wide), F32)
    packed_in[me] = packed[tp]
    gathers = [wires.copy(packed.at[peer % 4], packed_in.at[me], (dp, peer // 4, peer % 4)) for peer in peers]
    finals = (image_outs, text_outs, image_grads, text_grads)
    along_y = [wires.copy(final.at[tp], final.at[tp], wires.y_next) for final in finals]
    across = [wires.copy(final.at[tp], final.at[tp], wires.k_next) for final in finals]
    for arrived in gathers:
        arrived.wait_recv()
    total = packed_in[0]
    for source in range(1, 8):
        total = total + packed_in[source]
    own_sums[...] = total
    halves.wait_recv()
    for plane in planes:
        across.append(wires.copy(own_sums, packed_out.at[dp], (plane, x, tp)))
        across.append(wires.copy(both_halves, halves_out.at[dp], (plane, x, tp)))
    packed_out[dp] = total
    halves_out[dp] = both_halves[...]
    far = (1 - y) * 2 + k
    for final, arrived in zip(finals, along_y):
        arrived.wait_recv()
        across.append(wires.copy(final.at[far], final.at[far], wires.k_next))
    for arrived in across:
        arrived.wait_recv()
    wires.finish()


def leave_step(n_dp, parts, tokens, grads, outs_own, sums, mod, halves):
    width = tokens[0].shape[1]
    rows = [part.shape[0] for part in tokens]
    wide = width // 4
    outs = [jax.ShapeDtypeStruct((4, r, width), BF16) for r in rows] * 2
    outs += [
        jax.ShapeDtypeStruct((n_dp, PACKED, wide), F32),
        jax.ShapeDtypeStruct((n_dp, 2) + halves.shape, F32),
    ]
    scratch = []
    for r in rows:
        scratch += reduce_scratch(r, width)
    scratch += [
        pltpu.VMEM((4, PACKED, wide), F32),
        pltpu.VMEM((8, PACKED, wide), F32),
        pltpu.VMEM((PACKED, wide), F32),
        pltpu.VMEM((2,) + halves.shape, F32),
        pltpu.VMEM((8, width), F32),
    ]
    return comm_call(
        functools.partial(leave_kernel, n_dp),
        outs,
        scratch,
        1 + 10 + 7 + 8 + 2 * (n_dp - 1) + 4,
        3,
        "leave",
        [VMEM_SPEC] * 11,
        [VMEM_SPEC] * 6,
    )(*parts, *tokens, *grads, *outs_own, sums, mod, halves)


def share_kernel(part_ref, out_ref, send_sems, recv_sems):
    wires = Wires(send_sems, recv_sems)
    dp, x, tp = wires.dp, wires.x, wires.tp
    lanes = [(dp, x, lax.rem(tp + offset, 4)) for offset in range(1, 4)]
    wires.meet(lanes)
    copies = [wires.copy(part_ref, out_ref.at[tp], lane) for lane in lanes]
    out_ref[tp] = part_ref[...]
    for arrived in copies:
        arrived.wait_recv()
    wires.finish()


def share(part):
    return comm_call(
        share_kernel,
        jax.ShapeDtypeStruct((4,) + part.shape, F32),
        [],
        3,
        4,
        "share",
        [VMEM_SPEC],
        VMEM_SPEC,
    )(part)


def gather_rows(shard, ctx):
    pairs = [(0, 1), (1, 0)]
    kept = lax.dynamic_index_in_dim(shard, ctx, 2, keepdims=False)
    given = lax.dynamic_index_in_dim(shard, 1 - ctx, 2, keepdims=False)
    other = lax.ppermute(given, "ctx", pairs)
    first, last = jnp.where(ctx == 0, kept, other), jnp.where(ctx == 0, other, kept)
    return lax.all_gather(jnp.concatenate([first, last], 1), "dp", axis=1, tiled=True)


def scatter_rows(grad, ctx):
    mine = lax.psum_scatter(grad.astype(BF16), "dp", scatter_dimension=1, tiled=True)
    rows = mine.shape[1] // 2
    kept = lax.dynamic_slice_in_dim(mine, ctx * rows, rows, 1)
    given = lax.dynamic_slice_in_dim(mine, (1 - ctx) * rows, rows, 1)
    other = lax.ppermute(given, "ctx", [(0, 1), (1, 0)])
    first, last = jnp.where(ctx == 0, kept, other), jnp.where(ctx == 0, other, kept)
    return first.astype(F32), last.astype(F32)


def on_device(
    image_tokens,
    text_tokens,
    conditioning,
    ada_weight,
    ada_bias,
    qkv_weight,
    qv_bias,
    out_weight,
    out_bias,
    up_weight,
    up_bias,
    down_weight,
    down_bias,
    image_cotangent,
    text_cotangent,
):
    ctx_n, tp_n, dp_n = lax.axis_size("ctx"), lax.axis_size("tp"), lax.axis_size("dp")
    dp, ctx, tp = lax.axis_index("dp"), lax.axis_index("ctx"), lax.axis_index("tp")
    image_length, text_length, width = image_tokens.shape[1], text_tokens.shape[1], image_tokens.shape[2]
    slice_width = qkv_weight.shape[3]
    shard_rows = qkv_weight.shape[1]
    half = slice_width // ctx_n
    up_half = up_weight.shape[2] // ctx_n
    own_rows = (image_length // tp_n, TEXT_SLOTS // tp_n)
    image_all = image_length * ctx_n
    text_all = TEXT_SLOTS * ctx_n
    joint_pad = -(image_all + text_all) % JOINT_STEP
    pad = ((0, TEXT_SLOTS - text_length), (0, 0))

    qkv_full = gather_rows(
        qkv_weight.reshape(2, shard_rows, 3, ctx_n, half)
        .transpose(0, 1, 3, 2, 4)
        .reshape(2, shard_rows, ctx_n, 3 * half),
        ctx,
    )
    out_full = gather_rows(out_weight.reshape(2, shard_rows, ctx_n, half), ctx)
    up_full = gather_rows(up_weight.reshape(2, shard_rows, ctx_n, up_half), ctx)
    down_full = gather_rows(down_weight.reshape(2, shard_rows, ctx_n, up_half), ctx)
    qv_own = lax.dynamic_slice_in_dim(qv_bias, ctx * half, half, 2).astype(F32)
    up_bias_own = lax.dynamic_slice_in_dim(up_bias, ctx * up_half, up_half, 1).astype(F32)

    tokens = (image_tokens[0], jnp.pad(text_tokens[0], pad))
    cotangents = (image_cotangent[0], jnp.pad(text_cotangent[0], pad))
    cond_float = conditioning.astype(F32)
    activated_low = jax.nn.silu(cond_float).astype(BF16)
    partial_mod = jnp.einsum("nd,adkf->nakf", activated_low, ada_weight, preferred_element_type=F32)
    mod_blocks, bias_blocks, image_blocks, text_blocks = enter(
        partial_mod.reshape(dp_n, 12, slice_width),
        ada_bias.astype(F32).reshape(12, slice_width),
        jnp.concatenate([out_bias, down_bias], 0).astype(F32),
        *[part.reshape(tp_n, rows, width) for part, rows in zip(tokens, own_rows)],
    )
    modulation = mod_blocks.transpose(1, 0, 2).reshape(2, 6, width)
    biases = bias_blocks.transpose(1, 0, 2).reshape(4, width)
    mod_rows = modulation[:, :, None]
    out_bias_rows, down_bias_rows = biases[:2, None], biases[2:, None]
    tokens_all = (image_blocks.reshape(image_all, width), text_blocks.reshape(text_all, width))
    cotangents_all = []
    for part in cotangents:
        other = lax.ppermute(part, "ctx", [(0, 1), (1, 0)])
        first, last = jnp.where(ctx == 0, part, other), jnp.where(ctx == 0, other, part)
        cotangents_all.append(jnp.concatenate([first, last], 0))

    def own(parts):
        return [lax.dynamic_slice_in_dim(part, tp * rows, rows, 0) for part, rows in zip(parts, own_rows)]

    tokens_own, cotangents_own = own(tokens), own(cotangents)
    slots = tp * own_rows[1] + lax.broadcasted_iota(jnp.int32, (own_rows[1], 1), 0)
    valid = jnp.broadcast_to((slots < text_length).astype(F32), (own_rows[1], width))

    def blocks(part):
        return part.reshape(2, 2, 2, part.shape[0] // 8, width)

    normed_low, qkv_parts = [], []
    for stream in range(2):
        norm, _ = normalise(tokens_all[stream].astype(F32))
        normed = (norm * (1.0 + modulation[stream, 1]) + modulation[stream, 0]).astype(BF16)
        normed_low.append(normed)
        bias = jnp.concatenate([qv_own[stream, 0], jnp.zeros((half,), F32), qv_own[stream, 1]])
        qkv_parts.append((dot(normed, qkv_full[stream]) + bias).astype(BF16))
    joint = jnp.concatenate(qkv_parts + [jnp.zeros((joint_pad, 3 * half), BF16)], 0)
    queries, keys, values = joint[:, :half], joint[:, half : 2 * half], joint[:, 2 * half :]
    blended, lse = attend_forward(queries, keys, values, image_all, text_length)
    blended_parts = (blended[:image_all], blended[image_all : image_all + text_all])
    out_parts = [
        blocks(dot(blended_parts[s], out_full[s], ((1,), (1,))).astype(BF16)) for s in range(2)
    ]
    *attentions_middles, image_second, text_second = middle_step(
        *out_parts, *tokens_own, mod_rows, out_bias_rows
    )
    attentions, middles = attentions_middles[:2], attentions_middles[2:]
    second_low = (image_second.reshape(image_all, width), text_second.reshape(text_all, width))

    feed_parts, second_parts = [], []
    down_weight_grads, up_weight_grads, up_bias_grads = [], [], []
    for stream in range(2):
        hidden = dot(second_low[stream], up_full[stream]) + up_bias_own[stream]
        gelu_out, slope = gelu_parts(hidden)
        gelu_low = gelu_out.astype(BF16)
        feed_parts.append(blocks(dot(gelu_low, down_full[stream], ((1,), (1,))).astype(BF16)))
        grad_feed = (cotangents_all[stream].astype(F32) * modulation[stream, 5]).astype(BF16)
        down_weight_grads.append(dot(grad_feed, gelu_low, ((0,), (0,))))
        grad_hidden = (dot(grad_feed, down_full[stream]) * slope).astype(BF16)
        up_bias_grads.append(jnp.sum(grad_hidden.astype(F32), axis=0))
        up_weight_grads.append(dot(second_low[stream], grad_hidden, ((0,), (0,))))
        second_parts.append(blocks(dot(grad_hidden, up_full[stream], ((1,), (1,))).astype(BF16)))
    down_weight_grad = jnp.concatenate(scatter_rows(jnp.stack(down_weight_grads), ctx), 2)
    up_weight_grad = jnp.concatenate(scatter_rows(jnp.stack(up_weight_grads), ctx), 2)
    image_out, text_out, image_middle_grad, text_middle_grad, sums, image_attn, text_attn = turn_step(
        valid, feed_parts, second_parts, attentions, middles, cotangents_own, mod_rows, down_bias_rows
    )
    attention_grad_all = (image_attn.reshape(image_all, width), text_attn.reshape(text_all, width))

    out_weight_grads, blended_grads = [], []
    for stream in range(2):
        out_weight_grads.append(dot(attention_grad_all[stream], blended_parts[stream], ((0,), (0,))))
        blended_grads.append(dot(attention_grad_all[stream], out_full[stream]).astype(BF16))
    grad_queries, grad_keys, grad_values = attend_backward(
        queries,
        keys,
        values,
        jnp.concatenate(blended_grads + [jnp.zeros((joint_pad, half), BF16)], 0),
        lse,
        image_all,
        text_length,
    )
    grad_joint = jnp.concatenate([grad_queries, grad_keys, grad_values], 1)
    grad_parts = (grad_joint[:image_all], grad_joint[image_all : image_all + text_all])
    qkv_weight_grads, qv_bias_grads, normed_parts = [], [], []
    for stream in range(2):
        sums_joint = jnp.sum(grad_parts[stream].astype(F32), axis=0)
        qv_bias_grads.append(jnp.concatenate([sums_joint[:half], sums_joint[2 * half :]]))
        qkv_weight_grads.append(dot(normed_low[stream], grad_parts[stream], ((0,), (0,))))
        normed_parts.append(blocks(dot(grad_parts[stream], qkv_full[stream], ((1,), (1,))).astype(BF16)))
    out_weight_grad = jnp.concatenate(scatter_rows(jnp.stack(out_weight_grads), ctx), 2)
    qkv_weight_grad = jnp.concatenate(
        [part.reshape(2, shard_rows, 3, half) for part in scatter_rows(jnp.stack(qkv_weight_grads), ctx)], 3
    )

    halves = jnp.concatenate(
        [part.reshape(-1, slice_width) for part in (*qv_bias_grads, *up_bias_grads)]
        + [jnp.zeros((2, slice_width), F32)],
        0,
    )
    image_outs, text_outs, image_grads, text_grads, packed, halves_all = leave_step(
        dp_n,
        normed_parts,
        tokens_own,
        (image_middle_grad, text_middle_grad),
        (image_out, text_out),
        sums,
        mod_rows,
        halves,
    )
    grad_mod_low = packed[:, :12].astype(BF16)
    ada_bias_grad = jnp.sum(grad_mod_low.astype(F32), axis=0).reshape(2, 6, slice_width)
    grad_mod_low = grad_mod_low.reshape(dp_n, 2, 6, slice_width)
    ada_weight_grad = jnp.einsum("nd,nakf->adkf", activated_low, grad_mod_low, preferred_element_type=F32)
    cond_partial = jnp.einsum("nakf,adkf->nd", grad_mod_low, ada_weight, preferred_element_type=F32)
    totals = jnp.sum(packed[:, 12:22], axis=0)
    cond_rows = jnp.pad(cond_partial, ((0, -dp_n % 2), (0, slice_width - shard_rows)))
    shared = share(jnp.concatenate([totals, cond_rows], 0))
    cond_total = jnp.sum(shared[:, 10 : 10 + dp_n, :shard_rows], axis=0)
    cond_grad = jax.vjp(jax.nn.silu, cond_float)[1](cond_total)[0]
    full = shared[:, :10].transpose(1, 0, 2).reshape(2, 5, width)
    bias_grads = lax.dynamic_slice_in_dim(full[:, :2], (dp * ctx_n + ctx) * shard_rows, shard_rows, 2)
    squares_total = jnp.sum(full[:, 2:], axis=2).T.reshape(6)
    counts = jnp.array([image_length, text_length] * 3, F32) * (dp_n * ctx_n * width)
    root_means = jnp.sqrt(squares_total / counts)
    half_sums = jnp.sum(halves_all, axis=0)
    qv_rows = half * 2 // slice_width
    up_rows = up_half // slice_width
    qv_bias_grad = (
        half_sums[:, : 2 * qv_rows].reshape(ctx_n, 2, 2, half).transpose(1, 2, 0, 3).reshape(2, 2, slice_width)
    )
    up_bias_grad = (
        half_sums[:, 2 * qv_rows : 2 * (qv_rows + up_rows)]
        .reshape(ctx_n, 2, up_half)
        .transpose(1, 0, 2)
        .reshape(2, ctx_n * up_half)
    )
    return (
        image_outs.reshape(1, image_length, width),
        text_outs.reshape(1, TEXT_SLOTS, width)[:, :text_length],
        image_grads.reshape(1, image_length, width),
        text_grads.reshape(1, TEXT_SLOTS, width)[:, :text_length],
        cond_grad,
        ada_weight_grad,
        ada_bias_grad,
        qkv_weight_grad,
        qv_bias_grad,
        out_weight_grad,
        bias_grads[:, 1],
        up_weight_grad,
        up_bias_grad,
        down_weight_grad,
        bias_grads[:, 0],
        root_means,
    )


def solution(mesh):
    rows = P(None, ("dp", "ctx"))
    tokens = P("dp", "ctx", None)
    stacked = P(None, ("dp", "ctx"), None, "tp")
    matrix = P(None, ("dp", "ctx"), "tp")
    return jax.shard_map(
        on_device,
        mesh=mesh,
        in_specs=(
            tokens,
            tokens,
            rows,
            stacked,
            P(None, None, "tp"),
            stacked,
            P(None, None, "tp"),
            matrix,
            rows,
            matrix,
            P(None, "tp"),
            matrix,
            rows,
            tokens,
            tokens,
        ),
        out_specs=(
            tokens,
            tokens,
            tokens,
            tokens,
            rows,
            stacked,
            P(None, None, "tp"),
            stacked,
            P(None, None, "tp"),
            matrix,
            rows,
            matrix,
            P(None, "tp"),
            matrix,
            rows,
            P(),
        ),
        check_vma=False,
    )
```

```python
import functools

import jax
import jax.numpy as jnp
from jax import lax
from jax.experimental import pallas as pl
from jax.experimental.pallas import tpu as pltpu
from jax.sharding import PartitionSpec as P

HEAD_DIM = 64
F32 = jnp.float32
BF16 = jnp.bfloat16
VMEM_LIMIT = 60 * 1024 * 1024
PLANE = ("ctx", "tp")
TEXT_SLOTS = 96
MOST_GROUPS = 4
QUERY_BLOCK = 256


def dot(left, right, dims=((1,), (0,))):
    return lax.dot_general(left, right, (dims, ((), ())), preferred_element_type=F32)


def local_call(kernel, steps, in_specs, outs, scratch, flops, name):
    return pl.pallas_call(
        kernel,
        grid=(steps,),
        in_specs=in_specs,
        out_specs=[spec for spec, _ in outs],
        out_shape=[shape for _, shape in outs],
        scratch_shapes=scratch,
        compiler_params=pltpu.CompilerParams(vmem_limit_bytes=VMEM_LIMIT),
        cost_estimate=pl.CostEstimate(flops=flops, bytes_accessed=flops // 256, transcendentals=0),
        name=name,
    )


def fixed(shape):
    return pl.BlockSpec(shape, lambda i: (0,) * len(shape), pipeline_mode=pl.Buffered(1))


def stepped(shape):
    return pl.BlockSpec(shape, lambda i: (i,) + (0,) * (len(shape) - 1))


def image_block(shape, last):
    return pl.BlockSpec(shape, lambda i: (jnp.minimum(i, last),) + (0,) * (len(shape) - 1))


def stream_block(shape, steps):
    return pl.BlockSpec(shape, lambda i: (i // steps,) + (0,) * (len(shape) - 1))


def padded(text):
    return jnp.concatenate([text, jnp.zeros((QUERY_BLOCK - text.shape[0], text.shape[1]), text.dtype)], 0)


def by_stream(steps, image_ref, text_ref, body):
    step = pl.program_id(0)

    @pl.when(step < steps)
    def _():
        body(image_ref[...], 0)

    @pl.when(step >= steps)
    def _():
        body(padded(text_ref[...]), 1)


def project_kernel(steps, image_ref, text_ref, mod_ref, weight_ref, bias_ref, normed_ref, q_ref, k_ref, v_ref, out_ref):
    half = q_ref.shape[1]

    def body(tokens, stream):
        norm, _ = normalise(tokens.astype(F32))
        normed = (norm * (1.0 + mod_ref[0, 1]) + mod_ref[0, 0]).astype(BF16)
        normed_ref[...] = normed
        joint = dot(normed, weight_ref[0, :, : 3 * half]) + bias_ref[0]
        q_ref[...] = joint[:, :half].astype(BF16)
        k_ref[...] = joint[:, half : 2 * half].astype(BF16)
        v_ref[...] = joint[:, 2 * half :].astype(BF16)

    by_stream(steps, image_ref, text_ref, body)

    @pl.when(lax.rem(pl.program_id(0), steps) == 0)
    def _():
        out_ref[0] = weight_ref[0, :, 3 * half :]


def project(image, text, mod, weight, bias):
    (rows, width), wide = image.shape, weight.shape[2]
    steps, half = rows // QUERY_BLOCK, wide // 4
    joint = rows + QUERY_BLOCK
    heads = [(stepped((QUERY_BLOCK, half)), jax.ShapeDtypeStruct((joint, half), BF16))] * 3
    return local_call(
        functools.partial(project_kernel, steps),
        steps + 1,
        [
            image_block((QUERY_BLOCK, width), steps - 1),
            fixed(text.shape),
            stream_block((1,) + mod.shape[1:], steps),
            stream_block((1,) + weight.shape[1:], steps),
            stream_block((1,) + bias.shape[1:], steps),
        ],
        [(stepped((QUERY_BLOCK, width)), jax.ShapeDtypeStruct((joint, width), BF16))]
        + heads
        + [(stream_block((1, width, half), steps), jax.ShapeDtypeStruct((2, width, half), BF16))],
        [],
        6 * joint * width * half,
        "project",
    )(image, text, mod, weight, bias)


def key_bias(rows, image_rows, text_rows):
    slot = lax.broadcasted_iota(jnp.int32, (rows, 1), 0)
    text_slot = slot - image_rows
    unused = jnp.logical_or(lax.rem(text_slot, TEXT_SLOTS) >= text_rows, text_slot >= 2 * TEXT_SLOTS)
    masked = jnp.logical_and(text_slot >= 0, unused)
    return jnp.where(masked, -1e30, 0.0).astype(F32)


def attend_forward_kernel(
    steps, heads, text_rows, q_ref, k_ref, v_ref, weight_ref, o_ref, lse_ref, image_ref, text_ref, vt_ref
):
    step = pl.program_id(0)

    @pl.when(step == 0)
    def _():
        vt_ref[...] = v_ref[...].T

    rows = k_ref.shape[0]
    bias = key_bias(rows, steps * QUERY_BLOCK, text_rows)
    queries_t = (q_ref[...] * HEAD_DIM ** (-0.5)).T
    outs = []
    for head in range(heads):
        span = slice(head * HEAD_DIM, (head + 1) * HEAD_DIM)
        scores = dot(k_ref[:, span], queries_t[span]) + bias
        top = jnp.max(scores, axis=0, keepdims=True)
        grown = jnp.exp(scores - top)
        total = jnp.sum(grown, axis=0, keepdims=True)
        lse_ref[head : head + 1] = top + jnp.log(total)
        outs.append(dot(vt_ref[span], grown.astype(BF16)) * (1.0 / total))
    blended = jnp.concatenate(outs, 0).T.astype(BF16)
    o_ref[...] = blended
    branch = dot(blended, weight_ref[0], ((1,), (1,))).astype(BF16)

    @pl.when(step < steps)
    def _():
        image_ref[...] = branch

    @pl.when(step >= steps)
    def _():
        text_ref[...] = branch[: text_ref.shape[0]]


def attend_forward(q, k, v, weight, text_all, text_rows):
    rows, wide = q.shape
    width = weight.shape[1]
    heads = wide // HEAD_DIM
    steps = rows // QUERY_BLOCK - 1
    return local_call(
        functools.partial(attend_forward_kernel, steps, heads, text_rows),
        steps + 1,
        [
            stepped((QUERY_BLOCK, wide)),
            fixed((rows, wide)),
            fixed((rows, wide)),
            stream_block((1, width, wide), steps),
        ],
        [
            (stepped((QUERY_BLOCK, wide)), jax.ShapeDtypeStruct((rows, wide), BF16)),
            (pl.BlockSpec((heads, QUERY_BLOCK), lambda i: (0, i)), jax.ShapeDtypeStruct((heads, rows), F32)),
            (image_block((QUERY_BLOCK, width), steps - 1), jax.ShapeDtypeStruct((steps * QUERY_BLOCK, width), BF16)),
            (pl.BlockSpec((text_all, width), lambda i: (0, 0)), jax.ShapeDtypeStruct((text_all, width), BF16)),
        ],
        [pltpu.VMEM((wide, rows), BF16)],
        4 * rows * rows * wide,
        "attend_forward",
    )(q, k, v, weight)


def attend_backward_kernel(
    steps,
    heads,
    text_rows,
    q_ref,
    k_ref,
    v_ref,
    o_ref,
    lse_ref,
    image_ref,
    text_ref,
    weight_ref,
    dq_ref,
    dk_ref,
    dv_ref,
    dw_ref,
    kt_ref,
    g_ref,
    dk_sum,
    dv_sum,
    dw_sum,
):
    step = pl.program_id(0)
    wide = q_ref.shape[1]

    @pl.when(step == 0)
    def _():
        kt_ref[...] = k_ref[...].T
        dk_sum[...] = jnp.zeros_like(dk_sum)
        dv_sum[...] = jnp.zeros_like(dv_sum)
        dw_sum[...] = jnp.zeros_like(dw_sum)

    def bring(arriving, stream):
        g_ref[...] = dot(arriving, weight_ref[0]).astype(BF16)
        dw_sum[stream] += dot(arriving, o_ref[...], ((0,), (0,)))

    by_stream(steps, image_ref, text_ref, bring)
    rows = k_ref.shape[0]
    bias = key_bias(rows, steps * QUERY_BLOCK, text_rows)
    queries = q_ref[...] * HEAD_DIM ** (-0.5)
    queries_t = queries.T
    grads = g_ref[...]
    grads_t = grads.T
    outs = []
    for head in range(heads):
        span = slice(head * HEAD_DIM, (head + 1) * HEAD_DIM)
        scores = dot(k_ref[:, span], queries_t[span]) + bias
        prob = jnp.exp(scores - lse_ref[head : head + 1])
        grad_prob = dot(v_ref[:, span], grads_t[span])
        weighted = prob * grad_prob
        inner = jnp.sum(weighted, axis=0, keepdims=True)
        grad_score = (weighted - prob * inner).astype(BF16)
        dv_sum[head] += dot(prob.astype(BF16), grads[:, span])
        dk_sum[head] += dot(grad_score, queries[:, span])
        outs.append(dot(kt_ref[span], grad_score) * HEAD_DIM ** (-0.5))
    dq_ref[...] = jnp.concatenate(outs, 0).T.astype(BF16)

    @pl.when(step == steps)
    def _():
        dk_ref[...] = jnp.concatenate([dk_sum[head] for head in range(heads)], 1).astype(BF16)
        dv_ref[...] = jnp.concatenate([dv_sum[head] for head in range(heads)], 1).astype(BF16)
        for stream in range(2):
            dw_ref[:, stream * wide : (stream + 1) * wide] = dw_sum[stream].astype(BF16)


def attend_backward(q, k, v, blended, lse, image, text, weight, text_rows):
    rows, wide = q.shape
    width = weight.shape[1]
    heads = wide // HEAD_DIM
    steps = rows // QUERY_BLOCK - 1
    block = stepped((QUERY_BLOCK, wide))
    whole = pl.BlockSpec((rows, wide), lambda i: (0, 0))
    return local_call(
        functools.partial(attend_backward_kernel, steps, heads, text_rows),
        steps + 1,
        [
            block,
            fixed((rows, wide)),
            fixed((rows, wide)),
            block,
            pl.BlockSpec((heads, QUERY_BLOCK), lambda i: (0, i)),
            image_block((QUERY_BLOCK, width), steps - 1),
            fixed(text.shape),
            stream_block((1, width, wide), steps),
        ],
        [
            (block, jax.ShapeDtypeStruct((rows, wide), BF16)),
            (whole, jax.ShapeDtypeStruct((rows, wide), BF16)),
            (whole, jax.ShapeDtypeStruct((rows, wide), BF16)),
            (pl.BlockSpec((width, 2 * wide), lambda i: (0, 0)), jax.ShapeDtypeStruct((width, 2 * wide), BF16)),
        ],
        [
            pltpu.VMEM((wide, rows), BF16),
            pltpu.VMEM((QUERY_BLOCK, wide), BF16),
            pltpu.VMEM((heads, rows, HEAD_DIM), F32),
            pltpu.VMEM((heads, rows, HEAD_DIM), F32),
            pltpu.VMEM((2, width, wide), F32),
        ],
        10 * rows * rows * wide,
        "attend_backward",
    )(q, k, v, blended, lse, image, text, weight)


def unproject_kernel(
    steps, dq_ref, dk_ref, dv_ref, normed_ref, weight_ref, image_ref, text_ref, dw_ref, sums_ref, dw_sum
):
    step = pl.program_id(0)
    half = dq_ref.shape[1]
    stream = step // steps

    @pl.when(step == 0)
    def _():
        dw_sum[...] = jnp.zeros_like(dw_sum)
        sums_ref[...] = jnp.zeros_like(sums_ref)

    grads = jnp.concatenate([dq_ref[...], dk_ref[...], dv_ref[...]], 1)
    part = dot(grads, weight_ref[0, :, : 3 * half], ((1,), (1,))).astype(BF16)
    dw_sum[stream] += dot(normed_ref[...], grads, ((0,), (0,)))
    sums_ref[stream] += jnp.sum(grads.astype(F32), axis=0, keepdims=True)

    @pl.when(step < steps)
    def _():
        image_ref[...] = part

    @pl.when(step == steps)
    def _():
        text_ref[...] = part[: text_ref.shape[0]]
        for s in range(2):
            dw_ref[:, s * 3 * half : (s + 1) * 3 * half] = dw_sum[s].astype(BF16)


def unproject(dq, dk, dv, normed, weight, text_all):
    rows, half = dq.shape
    width = normed.shape[1]
    steps = rows // QUERY_BLOCK - 1
    block = stepped((QUERY_BLOCK, half))
    return local_call(
        functools.partial(unproject_kernel, steps),
        steps + 1,
        [block, block, block, stepped((QUERY_BLOCK, width)), stream_block((1,) + weight.shape[1:], steps)],
        [
            (image_block((QUERY_BLOCK, width), steps - 1), jax.ShapeDtypeStruct((steps * QUERY_BLOCK, width), BF16)),
            (pl.BlockSpec((text_all, width), lambda i: (0, 0)), jax.ShapeDtypeStruct((text_all, width), BF16)),
            (pl.BlockSpec((width, 6 * half), lambda i: (0, 0)), jax.ShapeDtypeStruct((width, 6 * half), BF16)),
            (pl.BlockSpec((2, 1, 3 * half), lambda i: (0, 0, 0)), jax.ShapeDtypeStruct((2, 1, 3 * half), F32)),
        ],
        [pltpu.VMEM((2, width, 3 * half), F32)],
        12 * rows * width * half,
        "unproject",
    )(dq, dk, dv, normed, weight)


def feed_kernel(second_ref, cot_ref, up_ref, down_ref, bias_ref, feed_ref, pull_ref, dw_ref, sums_ref, up_sum, down_sum):
    step = pl.program_id(0)
    wide = up_ref.shape[1]

    @pl.when(step == 0)
    def _():
        up_sum[...] = jnp.zeros_like(up_sum)
        down_sum[...] = jnp.zeros_like(down_sum)
        sums_ref[...] = jnp.zeros_like(sums_ref)

    second, arriving = second_ref[...], cot_ref[...]
    hidden = dot(second, up_ref[...]) + bias_ref[...]
    gelu_out, slope = gelu_parts(hidden)
    gelu_low = gelu_out.astype(BF16)
    feed_ref[...] = dot(gelu_low, down_ref[...], ((1,), (1,))).astype(BF16)
    down_sum[...] += dot(arriving, gelu_low, ((0,), (0,)))
    pulled = (dot(arriving, down_ref[...]) * slope).astype(BF16)
    sums_ref[...] += jnp.sum(pulled.astype(F32), axis=0, keepdims=True)
    up_sum[...] += dot(second, pulled, ((0,), (0,)))
    pull_ref[...] = dot(pulled, up_ref[...], ((1,), (1,))).astype(BF16)

    @pl.when(step == pl.num_programs(0) - 1)
    def _():
        dw_ref[:, :wide] = up_sum[...].astype(BF16)
        dw_ref[:, wide:] = down_sum[...].astype(BF16)


def feed_forward(second, arriving, up, down, bias):
    (rows, width), wide = second.shape, up.shape[1]
    block_rows = QUERY_BLOCK if rows % QUERY_BLOCK == 0 else rows
    block = stepped((block_rows, width))
    return local_call(
        feed_kernel,
        rows // block_rows,
        [block, block, fixed(up.shape), fixed(down.shape), fixed((1, wide))],
        [
            (block, jax.ShapeDtypeStruct((rows, width), BF16)),
            (block, jax.ShapeDtypeStruct((rows, width), BF16)),
            (pl.BlockSpec((width, 2 * wide), lambda i: (0, 0)), jax.ShapeDtypeStruct((width, 2 * wide), BF16)),
            (pl.BlockSpec((1, wide), lambda i: (0, 0)), jax.ShapeDtypeStruct((1, wide), F32)),
        ],
        [pltpu.VMEM((width, wide), F32)] * 2,
        12 * rows * width * wide,
        "feed_forward",
    )(second, arriving, up, down, bias.reshape(1, wide))


def normalise(inputs):
    centred = inputs - jnp.mean(inputs, axis=-1, keepdims=True)
    spread = lax.rsqrt(jnp.mean(centred * centred, axis=-1, keepdims=True) + 1e-06)
    return centred * spread, spread


def normalise_back(grad_norm, norm, spread):
    return spread * (
        grad_norm
        - jnp.mean(grad_norm, axis=-1, keepdims=True)
        - norm * jnp.mean(grad_norm * norm, axis=-1, keepdims=True)
    )


def gelu_parts(hidden):
    root = 0.7978845608028654
    square = hidden * hidden
    bent = jnp.tanh(hidden * (root + root * 0.044715 * square))
    half = 0.5 * (1.0 + bent)
    slope = half + 0.5 * hidden * (1.0 - bent * bent) * (root + 3.0 * root * 0.044715 * square)
    return hidden * half, slope


MESH = pl.DeviceIdType.MESH
VMEM_SPEC = pl.BlockSpec(memory_space=pltpu.VMEM)
ANY_SPEC = pl.BlockSpec(memory_space=pl.ANY)


class Wires:
    def __init__(self, send_sems, recv_sems):
        self.dp, self.x, self.tp = lax.axis_index("dp"), lax.axis_index("ctx"), lax.axis_index("tp")
        self.y, self.k = self.tp // 2, self.tp % 2
        self.x_next = (self.dp, 1 - self.x, self.tp)
        self.y_next = (self.dp, self.x, (1 - self.y) * 2 + self.k)
        self.k_next = (self.dp, self.x, self.y * 2 + 1 - self.k)
        self.send_sems, self.recv_sems, self.used = send_sems, recv_sems, 0
        self.started = []

    def copy(self, source, target, device):
        wire = pltpu.make_async_remote_copy(
            src_ref=source,
            dst_ref=target,
            send_sem=self.send_sems.at[self.used],
            recv_sem=self.recv_sems.at[self.used],
            device_id=device,
            device_id_type=MESH,
        )
        self.used += 1
        wire.start()
        self.started.append(wire)
        return wire

    def meet(self, devices):
        barrier = pltpu.get_barrier_semaphore()
        for device in devices:
            pl.semaphore_signal(barrier, inc=1, device_id=device, device_id_type=MESH)
        pl.semaphore_wait(barrier, len(devices))

    def finish(self):
        for wire in self.started:
            wire.wait_send()


def row_step(rows):
    return 32 if rows % 32 == 0 else rows


def over_rows(rows, body):
    step = row_step(rows)
    if step == rows:
        body(slice(0, rows))
        return

    def one(index, carry):
        body(pl.ds(pl.multiple_of(index * step, step), step))
        return carry

    lax.fori_loop(0, rows // step, one, 0)


def reduce_plane(wires, streams):
    x, y, k = wires.x, wires.y, wires.k
    first = [wires.copy(s["part"].at[:, :, 1 - k], s["core"], wires.k_next) for s in streams]
    second = []
    for s, arrived in zip(streams, first):
        part, core, held = s["part"], s["core"], s["held"]
        rows, width = part.shape[3], part.shape[4]
        cut = width // 2
        arrived.wait_recv()
        for i in range(2):
            for j in range(2):

                def add(span, i=i, j=j):
                    held[i, j, span] = (part[i, j, k, span].astype(F32) + core[i, j, span].astype(F32)).astype(BF16)

                over_rows(rows, add)
        second.append(
            (
                wires.copy(held.at[:, 1 - y, :, pl.ds(0, cut)], s["along_y"], wires.y_next),
                wires.copy(held.at[1 - x, :, :, pl.ds(cut, cut)], s["along_x"], wires.x_next),
            )
        )
    third = []
    for s, (from_y, from_x) in zip(streams, second):
        held, along_y, along_x, out_x, out_y = s["held"], s["along_y"], s["along_x"], s["out_x"], s["out_y"]
        rows, width = held.shape[2], held.shape[3]
        cut = width // 2
        from_y.wait_recv()
        from_x.wait_recv()

        def add(span):
            out_x[span] = (
                held[1 - x, y, span, :cut].astype(F32) + along_y[1 - x, span].astype(F32)
            ).astype(BF16)
            out_y[span] = (
                held[x, 1 - y, span, cut:].astype(F32) + along_x[1 - y, span].astype(F32)
            ).astype(BF16)

        over_rows(rows, add)
        third.append(
            (
                wires.copy(out_x, s["last_x"], wires.x_next),
                wires.copy(out_y, s["last_y"], wires.y_next),
            )
        )
    for s, (from_x, from_y) in zip(streams, third):
        held, along_y, along_x, last_x, last_y, total = (
            s["held"],
            s["along_y"],
            s["along_x"],
            s["last_x"],
            s["last_y"],
            s["total"],
        )
        rows, width = held.shape[2], held.shape[3]
        cut = width // 2
        from_x.wait_recv()
        from_y.wait_recv()

        def add(span):
            total[span, :cut] = (
                held[x, y, span, :cut].astype(F32) + along_y[x, span].astype(F32) + last_x[span].astype(F32)
            )
            total[span, cut:] = (
                held[x, y, span, cut:].astype(F32) + along_x[y, span].astype(F32) + last_y[span].astype(F32)
            )

        over_rows(rows, add)


REDUCE_KEYS = ("core", "held", "along_y", "along_x", "out_x", "out_y", "last_x", "last_y", "total")


def reduce_scratch(rows, width):
    half = width // 2
    return [
        pltpu.VMEM((2, 2, rows, width), BF16),
        pltpu.VMEM((2, 2, rows, width), BF16),
        pltpu.VMEM((2, rows, half), BF16),
        pltpu.VMEM((2, rows, half), BF16),
        pltpu.VMEM((rows, half), BF16),
        pltpu.VMEM((rows, half), BF16),
        pltpu.VMEM((rows, half), BF16),
        pltpu.VMEM((rows, half), BF16),
        pltpu.VMEM((rows, width), F32),
    ]


def block_halves(block):
    cut = block.shape[-1] // 2
    inner = (slice(None),) * (len(block.shape) - 4)
    return inner + (pl.ds(0, cut),), inner + (pl.ds(cut, cut),)


def spread_first(wires, block):
    x, y, k = wires.x, wires.y, wires.k
    low, high = block_halves(block)
    mine = block.at[(x, y, k) + low], block.at[(x, y, k) + high]
    return wires.copy(mine[0], mine[0], wires.x_next), wires.copy(mine[1], mine[1], wires.y_next)


def spread_second(wires, block, first):
    x, y, k = wires.x, wires.y, wires.k
    low, high = block_halves(block)
    for arrived in first:
        arrived.wait_recv()
    lows, highs = block.at[(slice(None), y, k) + low], block.at[(x, slice(None), k) + high]
    return wires.copy(lows, lows, wires.y_next), wires.copy(highs, highs, wires.x_next)


def spread_third(wires, block, second):
    for arrived in second:
        arrived.wait_recv()
    gathered = block.at[:, :, wires.k]
    return wires.copy(gathered, gathered, wires.k_next)


def spread_plane(wires, blocks, started=()):
    first = list(started) + [spread_first(wires, block) for block in blocks[len(started) :]]
    second = [spread_second(wires, block, arrived) for block, arrived in zip(blocks, first)]
    third = [spread_third(wires, block, arrived) for block, arrived in zip(blocks, second)]
    for arrived in third:
        arrived.wait_recv()


def comm_call(kernel, outs, scratch, wires, collective_id, name, in_specs, out_specs):
    return pl.pallas_call(
        kernel,
        out_shape=outs,
        in_specs=in_specs,
        out_specs=out_specs,
        scratch_shapes=scratch + [pltpu.SemaphoreType.DMA((wires,)), pltpu.SemaphoreType.DMA((wires,))],
        compiler_params=pltpu.CompilerParams(
            collective_id=collective_id, has_side_effects=True, vmem_limit_bytes=VMEM_LIMIT
        ),
        name=name,
    )


def enter_kernel(
    n_dp,
    groups,
    part_ref,
    bias_ref,
    rows_ref,
    image_ref,
    text_ref,
    attn_ref,
    up_ref,
    down_ref,
    mod_ref,
    rows_out,
    image_out,
    text_out,
    gates_out,
    attn_out,
    ffn_out,
    mod_in,
    send_sems,
    recv_sems,
):
    wires = Wires(send_sems, recv_sems)
    dp, x, y, k, tp = wires.dp, wires.x, wires.y, wires.k, wires.tp
    count = n_dp * 2
    me = dp * 2 + x
    peers = [lax.rem(me + offset, count) for offset in range(1, count)]
    others = [(peer // 2, peer % 2, tp) for peer in peers]
    lanes = [lax.rem(tp + offset, 4) for offset in range(1, 4)]
    z_next = (lax.rem(dp + 1, n_dp), x, tp)
    wires.meet(others + [(dp, x, lane) for lane in lanes])

    sums = [wires.copy(part_ref.at[peer // 2], mod_in.at[me], other) for peer, other in zip(peers, others)]
    rows = [wires.copy(rows_ref, rows_out.at[me], other) for other in others]
    swaps = [wires.copy(attn_ref.at[1 - x, s], attn_out.at[s, dp, x], wires.x_next) for s in range(2)]
    mod_in[me] = part_ref[dp]
    rows_out[me] = rows_ref[...]
    for arrived in sums:
        arrived.wait_recv()
    total = bias_ref[...]
    for source in range(count):
        total = total + mod_in[source]
    mod_ref[tp] = total
    mods = [wires.copy(mod_ref.at[tp], mod_ref.at[tp], (dp, x, lane)) for lane in lanes]
    for arrived in mods:
        arrived.wait_recv()
    gates = []
    if groups > 1:
        gates = [
            wires.copy(mod_ref.at[:, 11], gates_out.at[dp], (lax.rem(dp + offset, groups), x, tp))
            for offset in range(1, groups)
        ]
        for lane in range(4):
            gates_out[dp, lane] = mod_ref[lane, 11]

    ring = {(s, 0): wires.copy(attn_ref.at[x, s], attn_out.at[s, dp, x], z_next) for s in range(2)}

    def pass_on(turn, side):
        for s in range(2):
            ring[s, side].wait_recv()
            if turn < n_dp - 1:
                origin = lax.rem(dp + n_dp - turn, n_dp)
                block = attn_out.at[s, origin, x if side == 0 else 1 - x]
                ring[s, side] = wires.copy(block, block, z_next)

    streams = ((image_ref, image_out), (text_ref, text_out))
    cols = ffn_out.shape[3]
    wide = ffn_out.shape[0] // 2
    held = []
    for i, weight in enumerate((up_ref, down_ref)):
        for s in range(wide):
            given = weight.at[s, :, pl.ds(pl.multiple_of((1 - x) * cols, cols), cols)]
            held.append((given, ffn_out.at[i * wide + s, x]))
    for s, arrived in enumerate(swaps):
        arrived.wait_recv()
        block = attn_out.at[s, dp, 1 - x]
        ring[s, 1] = wires.copy(block, block, z_next)
    along_x = [wires.copy(ref.at[tp], out.at[x, tp], wires.x_next) for ref, out in streams]
    pass_on(1, 0)
    along_y = []
    for (_, out), arrived in zip(streams, along_x):
        arrived.wait_recv()
        block = out.at[1 - x, tp]
        along_y.append(wires.copy(block, block, wires.y_next))
    across = []
    for _, out in streams:
        block = out.at[1 - x, tp]
        across.append(wires.copy(block, block, wires.k_next))
    later = [wires.copy(given, place, wires.x_next) for given, place in held]

    def keep_tokens(span):
        for block in range(4):
            image_out[x, block, span] = image_ref[block, span]

    def keep_weights(span):
        for s in range(2):
            attn_out[s, dp, x, span] = attn_ref[x, s, span]
        for i, weight in enumerate((up_ref, down_ref)):
            for s in range(wide):
                first, last = weight[s, span, :cols], weight[s, span, cols:]
                ffn_out[i * wide + s, x, span] = jnp.where(x == 0, first, last)

    over_rows(image_ref.shape[1], keep_tokens)
    over_rows(attn_ref.shape[2], keep_weights)
    for block in range(4):
        text_out[x, block] = text_ref[block]
    pass_on(1, 1)
    far = (1 - y) * 2 + k
    for (_, out), arrived in zip(streams, along_y):
        arrived.wait_recv()
        block = out.at[1 - x, far]
        across.append(wires.copy(block, block, wires.k_next))
    for turn in range(2, n_dp - 1):
        pass_on(turn, 0)
        pass_on(turn, 1)
    if n_dp > 2:
        pass_on(n_dp - 1, 0)
        pass_on(n_dp - 1, 1)
    for arrived in rows + across + later + gates:
        arrived.wait_recv()
    wires.finish()


def enter(groups, partial_mod, ada_bias, bias_rows, image, text, attn, up, down, wide):
    n_dp, kinds, slice_width = partial_mod.shape
    count = 2 * n_dp
    rows, cols = up.shape[1], up.shape[2] // 2
    width = image.shape[2]
    return comm_call(
        functools.partial(enter_kernel, n_dp, groups),
        [
            jax.ShapeDtypeStruct((4, kinds, slice_width), F32),
            jax.ShapeDtypeStruct((count,) + bias_rows.shape, F32),
            jax.ShapeDtypeStruct((2,) + image.shape, BF16),
            jax.ShapeDtypeStruct((2,) + text.shape, BF16),
            jax.ShapeDtypeStruct((groups, 4, slice_width), F32),
            jax.ShapeDtypeStruct((2, n_dp, 2) + attn.shape[2:], BF16),
            jax.ShapeDtypeStruct((2 * wide, 2, rows, cols), BF16),
        ],
        [pltpu.VMEM((count, kinds, slice_width), F32)],
        2 * (count - 1) + 2 + 4 * n_dp + 16 + groups + 5,
        0,
        "enter",
        [VMEM_SPEC] * 8,
        [VMEM_SPEC] * 7,
    )(partial_mod, ada_bias, bias_rows, image, text, attn, up, down)


def meet_groups(wires, groups, more=()):
    dp, x, tp = wires.dp, wires.x, wires.tp
    count = groups * 2
    if groups == 1:
        others = [wires.x_next]
    else:
        peers = [lax.rem(dp * 2 + x + offset, count) for offset in range(1, count)]
        others = [(peer // 2, peer % 2, tp) for peer in peers]
    wires.meet(others + [wires.y_next, wires.k_next, *more])


def start_moves(wires, groups, moved_ref, moved_out, local_sem):
    if groups == 1:
        return []
    dp, x, tp = wires.dp, wires.x, wires.tp
    count = groups * 2
    me = dp * 2 + x
    peers = [lax.rem(me + offset, count) for offset in range(1, count)]
    local = pltpu.make_async_copy(moved_ref.at[me], moved_out.at[me], local_sem)
    local.start()
    return [local] + [
        wires.copy(moved_ref.at[peer], moved_out.at[me], (peer // 2, peer % 2, tp)) for peer in peers
    ]


def end_moves(moves):
    if moves:
        moves[0].wait()
    for arrived in moves[1:]:
        arrived.wait_recv()


def middle_kernel(
    n_dp,
    groups,
    image_part,
    text_part,
    image_x,
    text_x,
    mod_ref,
    bias_ref,
    moved_ref,
    *rest,
):
    ffn_refs = rest[: n_dp - 1]
    (
        cot_ref,
        image_attention,
        text_attention,
        image_middle,
        text_middle,
        image_all,
        text_all,
        cots_all,
        moved_out,
        ffn_out,
    ) = rest[n_dp - 1 : n_dp + 9]
    scratch = rest[n_dp + 9 :]
    local_sem, send_sems, recv_sems = scratch[-3:]
    wires = Wires(send_sems, recv_sems)
    dp, x, y, k, tp = wires.dp, wires.x, wires.y, wires.k, wires.tp
    z_next = (lax.rem(dp + 1, n_dp), x, tp)
    meet_groups(wires, groups, [z_next] if groups == 1 else [])
    cots = []
    if groups > 1:
        cots_all[x, y, k, dp] = cot_ref[...]
        for offset in range(1, groups):
            block = cots_all.at[x, y, k, dp]
            cots.append(wires.copy(block, block, (lax.rem(dp + offset, groups), x, tp)))
    last = wires.copy(ffn_refs[n_dp - 2], ffn_out.at[:, lax.rem(dp + 2, n_dp)], z_next)
    size = len(REDUCE_KEYS)
    streams = [
        dict(zip(("part",) + REDUCE_KEYS, (part,) + scratch[i * size : (i + 1) * size]))
        for i, part in enumerate((image_part, text_part))
    ]

    def keep(span):
        for turn, block in enumerate(ffn_refs):
            for i in range(block.shape[0]):
                ffn_out[i, lax.rem(dp + n_dp - turn, n_dp), span] = block[i, span]

    reduce_plane(wires, streams)
    for arrived in cots:
        arrived.wait_recv()
    gathers, started = [image_all, text_all], []
    if groups > 1:
        gathers, started = [cots_all] + gathers, [spread_first(wires, cots_all)]
    zs = []
    for i, tokens, attention, middle, gathered in (
        (1, text_x, text_attention, text_middle, text_all.at[:, :, :, dp if groups > 1 else 0]),
        (0, image_x, image_attention, image_middle, image_all),
    ):
        total = streams[i]["total"]

        def finish(span, i=i, tokens=tokens, attention=attention, middle=middle, gathered=gathered, total=total):
            branch = total[span] + bias_ref[i]
            attention[span] = branch
            value = tokens[span].astype(F32) + mod_ref[i, 2] * branch
            middle[span] = value
            norm, _ = normalise(value)
            gathered[x, y, k, span] = (norm * (1.0 + mod_ref[i, 4]) + mod_ref[i, 3]).astype(BF16)

        over_rows(total.shape[0], finish)
        if i == 1:
            for offset in range(1, groups):
                block = text_all.at[x, y, k, dp]
                zs.append(wires.copy(block, block, (lax.rem(dp + offset, groups), x, tp)))
    for arrived in zs:
        arrived.wait_recv()
    moves = start_moves(wires, groups, moved_ref, moved_out, local_sem)
    over_rows(ffn_out.shape[2], keep)
    spread_plane(wires, gathers, started)
    end_moves(moves)
    last.wait_recv()
    wires.finish()


def middle_step(groups, image_part, text_part, image_x, text_x, mod, bias, moved, ffn, cot):
    (image_rows, width), text_rows = image_x.shape, text_x.shape[0]
    outs = []
    for _ in range(2):
        outs += [jax.ShapeDtypeStruct((rows, width), F32) for rows in (image_rows, text_rows)]
    outs += [jax.ShapeDtypeStruct(image_part.shape, BF16)]
    outs += [jax.ShapeDtypeStruct((2, 2, 2, groups, text_rows, width), BF16)] * 2
    outs += [jax.ShapeDtypeStruct(moved.shape, BF16)]
    n_dp = len(ffn) + 1
    outs += [jax.ShapeDtypeStruct((ffn[0].shape[0], n_dp) + ffn[0].shape[1:], BF16)]
    return comm_call(
        functools.partial(middle_kernel, n_dp, groups),
        outs,
        reduce_scratch(image_rows, width) + reduce_scratch(text_rows, width) + [pltpu.SemaphoreType.DMA(())],
        30 + 4 * groups,
        1,
        "middle",
        [VMEM_SPEC] * 6 + [ANY_SPEC] + [VMEM_SPEC] * n_dp,
        [VMEM_SPEC] * 7 + [ANY_SPEC, VMEM_SPEC],
    )(image_part, text_part, image_x, text_x, mod, bias, moved, *ffn, cot)


def turn_kernel(
    groups,
    valid_ref,
    image_feed,
    text_feed,
    image_second,
    text_second,
    image_attention,
    text_attention,
    image_middle,
    text_middle,
    image_cot,
    text_cot,
    mod_ref,
    bias_ref,
    moved_ref,
    image_out,
    text_out,
    image_grad,
    text_grad,
    sums_ref,
    image_all,
    text_all,
    moved_out,
    *scratch,
):
    z_out, z_in, local_sem, send_sems, recv_sems = scratch[-5:]
    wires = Wires(send_sems, recv_sems)
    dp, x, y, k, tp = wires.dp, wires.x, wires.y, wires.k, wires.tp
    meet_groups(wires, groups)
    size = len(REDUCE_KEYS)
    streams = [
        dict(zip(("part",) + REDUCE_KEYS, (part,) + scratch[i * size : (i + 1) * size]))
        for i, part in enumerate((text_second, text_feed, image_second, image_feed))
    ]
    reduce_plane(wires, streams)
    streams = [streams[2], streams[0], streams[3], streams[1]]
    zs = []
    rows = text_middle.shape[0]
    if groups > 1:
        for i in range(2):
            total = streams[1 + 2 * i]["total"]
            for group in range(groups):
                z_out[i, group] = total[group * rows : (group + 1) * rows].astype(BF16)
            z_in[i, dp] = z_out[i, dp]
            for offset in range(1, groups):
                plane = lax.rem(dp + offset, groups)
                zs.append(wires.copy(z_out.at[i, plane], z_in.at[i, dp], (plane, x, tp)))
    sums_ref[...] = jnp.zeros_like(sums_ref)
    sides = (
        (image_attention, image_middle, image_cot, image_out, image_grad, image_all),
        (text_attention, text_middle, text_cot, text_out, text_grad, text_all),
    )
    for i, (attention, middle, cot, out, grad, gathered) in enumerate(sides):
        second, feed = streams[i]["total"], streams[2 + i]["total"]
        if i == 1 and groups > 1:
            for arrived in zs:
                arrived.wait_recv()
            for j, total in enumerate((second, feed)):
                summed = z_in[j, 0].astype(F32)
                for group in range(1, groups):
                    summed = summed + z_in[j, group].astype(F32)
                total[0:rows] = summed

        def finish(span, i=i, attention=attention, middle=middle, cot=cot, out=out, grad=grad, gathered=gathered, second=second, feed=feed):
            branch, value, arriving, pulled = attention[span], middle[span], cot[span].astype(F32), second[span]
            fed = feed[span] + bias_ref[i]
            gated_branch = mod_ref[i, 2] * branch
            gated_feed = mod_ref[i, 5] * fed
            result = value + gated_feed
            out[span] = result.astype(BF16)
            norm, spread = normalise(value)
            grad_middle = arriving + normalise_back(pulled * (1.0 + mod_ref[i, 4]), norm, spread)
            grad[span] = grad_middle
            low = (grad_middle * mod_ref[i, 2]).astype(BF16)
            gathered[x, y, k, span] = low
            if i == 1:
                kept = valid_ref[span]
                result, gated_branch, gated_feed = result * kept, gated_branch * kept, gated_feed * kept
            own_feed = (arriving * mod_ref[i, 5]).astype(BF16).astype(F32)
            terms = (
                grad_middle * branch,
                pulled,
                pulled * norm,
                arriving * fed,
                own_feed,
                low.astype(F32),
                result * result,
                gated_branch * gated_branch,
                gated_feed * gated_feed,
            )
            for t, term in enumerate(terms):
                sums_ref[i, t : t + 1] += jnp.sum(term, axis=0, keepdims=True)

        over_rows(middle.shape[0], finish)
    moves = start_moves(wires, groups, moved_ref, moved_out, local_sem)
    spread_plane(wires, [image_all, text_all])
    end_moves(moves)
    wires.finish()


def turn_step(groups, valid, feeds, seconds, attentions, middles, cots, mod, bias, moved):
    width = middles[0].shape[1]
    rows = [part.shape[0] for part in middles]
    outs = [jax.ShapeDtypeStruct((r, width), BF16) for r in rows]
    outs += [jax.ShapeDtypeStruct((r, width), F32) for r in rows]
    outs += [jax.ShapeDtypeStruct((2, 16, width), F32)]
    outs += [jax.ShapeDtypeStruct((2, 2, 2, r, width), BF16) for r in rows]
    outs += [jax.ShapeDtypeStruct(moved.shape, BF16)]
    scratch = []
    for r in (rows[1] * groups, rows[0]):
        scratch += reduce_scratch(r, width) + reduce_scratch(r, width)
    scratch += [pltpu.VMEM((2, groups, rows[1], width), BF16)] * 2 + [pltpu.SemaphoreType.DMA(())]
    return comm_call(
        functools.partial(turn_kernel, groups),
        outs,
        scratch,
        30 + 4 * groups,
        2,
        "turn",
        [VMEM_SPEC] * 13 + [ANY_SPEC],
        [VMEM_SPEC] * 7 + [ANY_SPEC],
    )(valid, *feeds, *seconds, *attentions, *middles, *cots, mod, bias, moved)


PACKED = 24


def leave_kernel(
    n_dp,
    image_part,
    text_part,
    image_x,
    text_x,
    image_grad,
    text_grad,
    image_out,
    text_out,
    sums_ref,
    mod_ref,
    halves_ref,
    image_outs,
    text_outs,
    image_grads,
    text_grads,
    packed_out,
    halves_out,
    *scratch,
):
    send_sems, recv_sems = scratch[-2:]
    packed, packed_in, own_sums, both_halves, local_sums = scratch[-7:-2]
    wires = Wires(send_sems, recv_sems)
    dp, x, y, k, tp = wires.dp, wires.x, wires.y, wires.k, wires.tp
    me = x * 4 + tp
    peers = [lax.rem(me + offset, 8) for offset in range(1, 8)]
    planes = [lax.rem(dp + offset, n_dp) for offset in range(1, n_dp)]
    wires.meet([(dp, peer // 4, peer % 4) for peer in peers] + [(plane, x, tp) for plane in planes])

    image_outs[tp] = image_out[...]
    text_outs[tp] = text_out[...]
    both_halves[x] = halves_ref[...]
    halves = wires.copy(both_halves.at[x], both_halves.at[x], wires.x_next)
    size = len(REDUCE_KEYS)
    streams = [
        dict(zip(("part",) + REDUCE_KEYS, (part,) + scratch[i * size : (i + 1) * size]))
        for i, part in enumerate((image_part, text_part))
    ]
    reduce_plane(wires, streams)
    local_sums[...] = jnp.zeros_like(local_sums)
    for i, (tokens, grad, all_grads) in enumerate(
        ((image_x, image_grad, image_grads), (text_x, text_grad, text_grads))
    ):
        total = streams[i]["total"]

        def finish(span, i=i, tokens=tokens, grad=grad, all_grads=all_grads, total=total):
            pulled = total[span]
            norm, spread = normalise(tokens[span].astype(F32))
            grad_tokens = grad[span] + normalise_back(pulled * (1.0 + mod_ref[i, 1]), norm, spread)
            all_grads[tp, span] = grad_tokens.astype(BF16)
            local_sums[2 * i : 2 * i + 1] += jnp.sum(pulled, axis=0, keepdims=True)
            local_sums[2 * i + 1 : 2 * i + 2] += jnp.sum(pulled * norm, axis=0, keepdims=True)

        over_rows(total.shape[0], finish)
    wide = packed.shape[2]
    for t in range(4):
        cols = slice(t * wide, (t + 1) * wide)
        for i in range(2):
            packed[t, 6 * i : 6 * i + 2] = local_sums[2 * i : 2 * i + 2, cols]
            packed[t, 6 * i + 2 : 6 * i + 6] = sums_ref[i, 0:4, cols]
            packed[t, 12 + 5 * i : 12 + 5 * i + 5] = sums_ref[i, 4:9, cols]
        packed[t, 22:24] = jnp.zeros((2, wide), F32)
    packed_in[me] = packed[tp]
    gathers = [wires.copy(packed.at[peer % 4], packed_in.at[me], (dp, peer // 4, peer % 4)) for peer in peers]
    finals = (image_outs, text_outs, image_grads, text_grads)
    along_y = [wires.copy(final.at[tp], final.at[tp], wires.y_next) for final in finals]
    across = [wires.copy(final.at[tp], final.at[tp], wires.k_next) for final in finals]
    for arrived in gathers:
        arrived.wait_recv()
    total = packed_in[0]
    for source in range(1, 8):
        total = total + packed_in[source]
    own_sums[...] = total
    halves.wait_recv()
    for plane in planes:
        across.append(wires.copy(own_sums, packed_out.at[dp], (plane, x, tp)))
        across.append(wires.copy(both_halves, halves_out.at[dp], (plane, x, tp)))
    packed_out[dp] = total
    halves_out[dp] = both_halves[...]
    far = (1 - y) * 2 + k
    for final, arrived in zip(finals, along_y):
        arrived.wait_recv()
        across.append(wires.copy(final.at[far], final.at[far], wires.k_next))
    for arrived in across:
        arrived.wait_recv()
    wires.finish()


def leave_step(n_dp, parts, tokens, grads, outs_own, sums, mod, halves):
    width = tokens[0].shape[1]
    rows = [part.shape[0] for part in tokens]
    wide = width // 4
    outs = [jax.ShapeDtypeStruct((4, r, width), BF16) for r in rows] * 2
    outs += [
        jax.ShapeDtypeStruct((n_dp, PACKED, wide), F32),
        jax.ShapeDtypeStruct((n_dp, 2) + halves.shape, F32),
    ]
    scratch = []
    for r in rows:
        scratch += reduce_scratch(r, width)
    scratch += [
        pltpu.VMEM((4, PACKED, wide), F32),
        pltpu.VMEM((8, PACKED, wide), F32),
        pltpu.VMEM((PACKED, wide), F32),
        pltpu.VMEM((2,) + halves.shape, F32),
        pltpu.VMEM((8, width), F32),
    ]
    return comm_call(
        functools.partial(leave_kernel, n_dp),
        outs,
        scratch,
        1 + 10 + 7 + 8 + 2 * (n_dp - 1) + 4,
        3,
        "leave",
        [VMEM_SPEC] * 11,
        [VMEM_SPEC] * 6,
    )(*parts, *tokens, *grads, *outs_own, sums, mod, halves)


def share_kernel(part_ref, out_ref, send_sems, recv_sems):
    wires = Wires(send_sems, recv_sems)
    dp, x, tp = wires.dp, wires.x, wires.tp
    lanes = [(dp, x, lax.rem(tp + offset, 4)) for offset in range(1, 4)]
    wires.meet(lanes)
    copies = [wires.copy(part_ref, out_ref.at[tp], lane) for lane in lanes]
    out_ref[tp] = part_ref[...]
    for arrived in copies:
        arrived.wait_recv()
    wires.finish()


def share(part):
    return comm_call(
        share_kernel,
        jax.ShapeDtypeStruct((4,) + part.shape, F32),
        [],
        3,
        4,
        "share",
        [VMEM_SPEC],
        VMEM_SPEC,
    )(part)


def scatter_rows(grad):
    return lax.psum_scatter(grad, "dp", scatter_dimension=0, tiled=True)


def swap_halves(mine, ctx):
    rows = mine.shape[0] // 2
    kept = lax.dynamic_slice_in_dim(mine, ctx * rows, rows, 0)
    given = lax.dynamic_slice_in_dim(mine, (1 - ctx) * rows, rows, 0)
    other = lax.ppermute(given, "ctx", [(0, 1), (1, 0)])
    first, last = jnp.where(ctx == 0, kept, other), jnp.where(ctx == 0, other, kept)
    return first.astype(F32), last.astype(F32)


def swap_streams(mine, ctx):
    rows, cols = mine.shape[0] // 2, mine.shape[1] // 2
    return [part.reshape(rows, 2, cols).transpose(1, 0, 2) for part in swap_halves(mine, ctx)]


def on_device(
    image_tokens,
    text_tokens,
    conditioning,
    ada_weight,
    ada_bias,
    qkv_weight,
    qv_bias,
    out_weight,
    out_bias,
    up_weight,
    up_bias,
    down_weight,
    down_bias,
    image_cotangent,
    text_cotangent,
):
    ctx_n, tp_n, dp_n = lax.axis_size("ctx"), lax.axis_size("tp"), lax.axis_size("dp")
    dp, ctx, tp = lax.axis_index("dp"), lax.axis_index("ctx"), lax.axis_index("tp")
    image_length, text_length, width = image_tokens.shape[1], text_tokens.shape[1], image_tokens.shape[2]
    slice_width = qkv_weight.shape[3]
    shard_rows = qkv_weight.shape[1]
    half = slice_width // ctx_n
    up_half = up_weight.shape[2] // ctx_n
    own_rows = (image_length // tp_n, TEXT_SLOTS // tp_n)
    image_all = image_length * ctx_n
    text_all = TEXT_SLOTS * ctx_n
    pad = ((0, TEXT_SLOTS - text_length), (0, 0))

    groups = dp_n if dp_n <= MOST_GROUPS else 1
    wide = 1 if groups > 1 else 2
    text_cols = up_half // groups
    text_start = ctx * up_half + (dp * text_cols if groups > 1 else 0)

    tokens = (image_tokens[0], jnp.pad(text_tokens[0], pad))
    cotangents = (image_cotangent[0], jnp.pad(text_cotangent[0], pad))

    def own(parts):
        return [lax.dynamic_slice_in_dim(part, tp * rows, rows, 0) for part, rows in zip(parts, own_rows)]

    tokens_own, cotangents_own = own(tokens), own(cotangents)
    cond_float = conditioning.astype(F32)
    activated_low = jax.nn.silu(cond_float).astype(BF16)
    partial_mod = jnp.einsum("nd,adkf->nakf", activated_low, ada_weight, preferred_element_type=F32)
    (
        mod_blocks,
        bias_blocks,
        image_blocks,
        text_blocks,
        text_gates,
        attn_full,
        ffn_mixed,
    ) = enter(
        groups,
        partial_mod.reshape(dp_n, 12, slice_width),
        ada_bias.astype(F32).reshape(12, slice_width),
        jnp.concatenate([out_bias, down_bias], 0).astype(F32),
        *[part.reshape(tp_n, rows, width) for part, rows in zip(tokens, own_rows)],
        jnp.stack(
            [
                jnp.concatenate(
                    [qkv_weight[:, :, j, c * half : (c + 1) * half] for j in range(3)]
                    + [out_weight[:, :, c * half : (c + 1) * half]],
                    2,
                )
                for c in range(ctx_n)
            ]
        ),
        up_weight,
        down_weight,
        wide,
    )
    cotangents = (lax.optimization_barrier((cotangents[0], mod_blocks))[0], cotangents[1])
    attn_full = attn_full.reshape(2, width, 4 * half)
    ffn_blocks = [ffn_mixed.reshape(2 * wide, 2 * shard_rows, up_half)]
    around = [(i, (i + 1) % dp_n) for i in range(dp_n)]
    ffn_blocks.append(lax.ppermute(ffn_blocks[0], "dp", around))
    modulation = mod_blocks.transpose(1, 0, 2).reshape(2, 6, width)
    biases = bias_blocks.transpose(1, 0, 2).reshape(4, width)
    mod_rows = modulation[:, :, None]
    out_bias_rows, down_bias_rows = biases[:2, None], biases[2:, None]
    tokens_all = (image_blocks.reshape(image_all, width), text_blocks.reshape(text_all, width))
    qv_own = lax.dynamic_slice_in_dim(qv_bias, ctx * half, half, 2).astype(F32)
    up_bias_own = (
        lax.dynamic_slice_in_dim(up_bias[0], ctx * up_half, up_half, 0).astype(F32),
        lax.dynamic_slice_in_dim(up_bias[1], text_start, text_cols, 0).astype(F32),
    )
    slots = tp * own_rows[1] + lax.broadcasted_iota(jnp.int32, (own_rows[1], 1), 0)
    valid = jnp.broadcast_to((slots < text_length).astype(F32), (own_rows[1], width))

    def to_devices(weight):
        parts = weight.reshape(shard_rows, ctx_n, dp_n, text_cols)
        return parts.transpose(2, 1, 0, 3).reshape(dp_n * ctx_n, shard_rows, text_cols)

    if groups > 1:
        moved = jnp.concatenate([to_devices(up_weight[1]), to_devices(down_weight[1])], 2)
    else:
        moved = jnp.zeros((1, 8, 128), BF16)

    def both_halves(part):
        other = lax.ppermute(part, "ctx", [(0, 1), (1, 0)])
        first, last = jnp.where(ctx == 0, part, other), jnp.where(ctx == 0, other, part)
        return jnp.concatenate([first, last], 0)

    def feed_grad(stream):
        return (both_halves(cotangents[stream]).astype(F32) * modulation[stream, 5]).astype(BF16)

    def blocks(part):
        return part.reshape(2, 2, 2, part.shape[0] // 8, width)

    qv_bias_rows = jnp.concatenate([qv_own[:, 0], jnp.zeros((2, half), F32), qv_own[:, 1]], 1)[:, None]
    normed_low, queries, keys, values, out_full = project(
        *tokens_all, mod_rows[:, :2], attn_full, qv_bias_rows
    )
    queries, ffn_blocks[1] = lax.optimization_barrier((queries, ffn_blocks[1]))
    for _ in range(dp_n - 3):
        ffn_blocks.append(lax.ppermute(ffn_blocks[-1], "dp", around))
    blended, lse, *out_parts = attend_forward(queries, keys, values, out_full, text_all, text_length)
    out_parts = [blocks(part) for part in out_parts]
    *attentions_middles, image_second, text_second, text_cots, moved_in, ffn_full = middle_step(
        groups, *out_parts, *tokens_own, mod_rows, out_bias_rows, moved, ffn_blocks, cotangents_own[1]
    )
    ffn_full = ffn_full.reshape(2 * wide, width, up_half)
    attentions, middles = attentions_middles[:2], attentions_middles[2:]
    second_low = (image_second.reshape(-1, width), text_second.reshape(-1, width))

    up_full, down_full = [ffn_full[0]], [ffn_full[wide]]
    if groups > 1:
        moved_in = moved_in.reshape(width, 2 * text_cols)
        up_full.append(moved_in[:, :text_cols])
        down_full.append(moved_in[:, text_cols:])
        gates = text_gates.reshape(groups, 1, width)
        feed_grads = (
            feed_grad(0),
            (text_cots.reshape(8, groups, own_rows[1], width).astype(F32) * gates).astype(BF16).reshape(-1, width),
        )
    else:
        up_full.append(ffn_full[1])
        down_full.append(ffn_full[3])
        feed_grads = (feed_grad(0), feed_grad(1))
    feed_parts, second_parts, ffn_grads, up_bias_grads = [], [], [], []
    for stream in range(2):
        feed, pulled, grads, sums = feed_forward(
            second_low[stream], feed_grads[stream], up_full[stream], down_full[stream], up_bias_own[stream]
        )
        feed_parts.append(blocks(feed))
        second_parts.append(blocks(pulled))
        ffn_grads.append(grads)
        up_bias_grads.append(sums[0])
    if groups > 1:
        ffn_mine = scatter_rows(ffn_grads[0])
        moved = ffn_grads[1].reshape(dp_n * ctx_n, shard_rows, 2 * text_cols)
    else:
        ffn_mine = scatter_rows(jnp.concatenate(ffn_grads, 1))
    image_out, text_out, image_middle_grad, text_middle_grad, sums, image_attn, text_attn, moved_in = turn_step(
        groups, valid, feed_parts, second_parts, attentions, middles, cotangents_own, mod_rows, down_bias_rows, moved
    )
    attention_grad_all = (image_attn.reshape(-1, width), text_attn.reshape(-1, width))
    if groups > 1:
        back = (
            moved_in.reshape(dp_n, ctx_n, shard_rows, 2, text_cols)
            .transpose(3, 2, 1, 0, 4)
            .reshape(2, shard_rows, ctx_n * up_half)
            .astype(F32)
        )

    grad_queries, grad_keys, grad_values, out_weight_grads = attend_backward(
        queries, keys, values, blended, lse, *attention_grad_all, out_full, text_length
    )
    out_weight_grads, ffn_mine = lax.optimization_barrier((out_weight_grads, ffn_mine))
    out_mine = scatter_rows(out_weight_grads)
    *normed_parts, qkv_weight_grads, joint_sums = unproject(
        grad_queries, grad_keys, grad_values, normed_low, attn_full, text_all
    )
    normed_parts = [blocks(part) for part in normed_parts]
    qkv_weight_grads, out_mine = lax.optimization_barrier((qkv_weight_grads, out_mine))
    qkv_mine = scatter_rows(qkv_weight_grads)
    qv_bias_grads = [
        jnp.concatenate([joint_sums[stream, 0, :half], joint_sums[stream, 0, 2 * half :]]) for stream in range(2)
    ]
    qkv_weight_grad = jnp.concatenate(
        [part.reshape(2, shard_rows, 3, half) for part in swap_streams(qkv_mine, ctx)], 3
    )
    out_weight_grad = jnp.concatenate(swap_streams(out_mine, ctx), 2)
    ffn_halves = swap_halves(ffn_mine, ctx)
    if groups > 1:
        up_weight_grad, down_weight_grad = [
            jnp.stack([jnp.concatenate([part[:, i * up_half : (i + 1) * up_half] for part in ffn_halves], 1), back[i]])
            for i in range(2)
        ]
    else:
        up_weight_grad, down_weight_grad = [
            jnp.stack(
                [
                    jnp.concatenate([part[:, c * up_half : (c + 1) * up_half] for part in ffn_halves], 1)
                    for c in (i, 2 + i)
                ]
            )
            for i in range(2)
        ]

    if groups > 1:
        up_bias_grads[1] = lax.dynamic_update_slice_in_dim(
            jnp.zeros((up_half,), F32), up_bias_grads[1], dp * text_cols, 0
        )
    halves = jnp.concatenate(
        [part.reshape(-1, slice_width) for part in (*qv_bias_grads, *up_bias_grads)], 0
    )
    image_outs, text_outs, image_grads, text_grads, packed, halves_all = leave_step(
        dp_n,
        normed_parts,
        tokens_own,
        (image_middle_grad, text_middle_grad),
        (image_out, text_out),
        sums,
        mod_rows,
        halves,
    )
    grad_mod_low = packed[:, :12].astype(BF16)
    ada_bias_grad = jnp.sum(grad_mod_low.astype(F32), axis=0).reshape(2, 6, slice_width)
    grad_mod_low = grad_mod_low.reshape(dp_n, 2, 6, slice_width)
    ada_weight_grad = jnp.einsum("nd,nakf->adkf", activated_low, grad_mod_low, preferred_element_type=F32)
    cond_partial = jnp.einsum("nakf,adkf->nd", grad_mod_low, ada_weight, preferred_element_type=F32)
    totals = jnp.sum(packed[:, 12:22], axis=0)
    cond_rows = jnp.pad(cond_partial, ((0, -dp_n % 2), (0, slice_width - shard_rows)))
    shared = share(jnp.concatenate([totals, cond_rows], 0))
    cond_total = jnp.sum(shared[:, 10 : 10 + dp_n, :shard_rows], axis=0)
    cond_grad = jax.vjp(jax.nn.silu, cond_float)[1](cond_total)[0]
    full = shared[:, :10].transpose(1, 0, 2).reshape(2, 5, width)
    bias_grads = lax.dynamic_slice_in_dim(full[:, :2], (dp * ctx_n + ctx) * shard_rows, shard_rows, 2)
    squares_total = jnp.sum(full[:, 2:], axis=2).T.reshape(6)
    counts = jnp.array([image_length, text_length] * 3, F32) * (dp_n * ctx_n * width)
    root_means = jnp.sqrt(squares_total / counts)
    half_sums = jnp.sum(halves_all, axis=0)
    qv_rows = half * 2 // slice_width
    up_rows = up_half // slice_width
    qv_bias_grad = (
        half_sums[:, : 2 * qv_rows].reshape(ctx_n, 2, 2, half).transpose(1, 2, 0, 3).reshape(2, 2, slice_width)
    )
    up_bias_grad = (
        half_sums[:, 2 * qv_rows : 2 * (qv_rows + up_rows)]
        .reshape(ctx_n, 2, up_half)
        .transpose(1, 0, 2)
        .reshape(2, ctx_n * up_half)
    )
    return (
        image_outs.reshape(1, image_length, width),
        text_outs.reshape(1, TEXT_SLOTS, width)[:, :text_length],
        image_grads.reshape(1, image_length, width),
        text_grads.reshape(1, TEXT_SLOTS, width)[:, :text_length],
        cond_grad,
        ada_weight_grad,
        ada_bias_grad,
        qkv_weight_grad,
        qv_bias_grad,
        out_weight_grad,
        bias_grads[:, 1],
        up_weight_grad,
        up_bias_grad,
        down_weight_grad,
        bias_grads[:, 0],
        root_means,
    )


def solution(mesh):
    rows = P(None, ("dp", "ctx"))
    tokens = P("dp", "ctx", None)
    stacked = P(None, ("dp", "ctx"), None, "tp")
    matrix = P(None, ("dp", "ctx"), "tp")
    return jax.shard_map(
        on_device,
        mesh=mesh,
        in_specs=(
            tokens,
            tokens,
            rows,
            stacked,
            P(None, None, "tp"),
            stacked,
            P(None, None, "tp"),
            matrix,
            rows,
            matrix,
            P(None, "tp"),
            matrix,
            rows,
            tokens,
            tokens,
        ),
        out_specs=(
            tokens,
            tokens,
            tokens,
            tokens,
            rows,
            stacked,
            P(None, None, "tp"),
            stacked,
            P(None, None, "tp"),
            matrix,
            rows,
            matrix,
            P(None, "tp"),
            matrix,
            rows,
            P(),
        ),
        check_vma=False,
    )
```

```python
import functools

import jax
import jax.numpy as jnp
from jax import lax
from jax.experimental import pallas as pl
from jax.experimental.pallas import tpu as pltpu
from jax.sharding import PartitionSpec as P

HEAD_DIM = 64
F32 = jnp.float32
BF16 = jnp.bfloat16
VMEM_LIMIT = 60 * 1024 * 1024
PLANE = ("ctx", "tp")
TEXT_SLOTS = 96
MOST_GROUPS = 4
QUERY_BLOCK = 256


def dot(left, right, dims=((1,), (0,))):
    return lax.dot_general(left, right, (dims, ((), ())), preferred_element_type=F32)


def local_call(kernel, steps, in_specs, outs, scratch, flops, name):
    return pl.pallas_call(
        kernel,
        grid=(steps,),
        in_specs=in_specs,
        out_specs=[spec for spec, _ in outs],
        out_shape=[shape for _, shape in outs],
        scratch_shapes=scratch,
        compiler_params=pltpu.CompilerParams(vmem_limit_bytes=VMEM_LIMIT),
        cost_estimate=pl.CostEstimate(flops=flops, bytes_accessed=flops // 256, transcendentals=0),
        name=name,
    )


def fixed(shape):
    return pl.BlockSpec(shape, lambda i: (0,) * len(shape), pipeline_mode=pl.Buffered(1))


def stepped(shape):
    return pl.BlockSpec(shape, lambda i: (i,) + (0,) * (len(shape) - 1))


def image_block(shape, last):
    return pl.BlockSpec(shape, lambda i: (jnp.minimum(i, last),) + (0,) * (len(shape) - 1))


def stream_block(shape, steps):
    return pl.BlockSpec(shape, lambda i: (i // steps,) + (0,) * (len(shape) - 1))


def padded(text):
    return jnp.concatenate([text, jnp.zeros((QUERY_BLOCK - text.shape[0], text.shape[1]), text.dtype)], 0)


def by_stream(steps, image_ref, text_ref, body):
    step = pl.program_id(0)

    @pl.when(step < steps)
    def _():
        body(image_ref[...], 0)

    @pl.when(step >= steps)
    def _():
        body(padded(text_ref[...]), 1)


def project_kernel(steps, image_ref, text_ref, mod_ref, weight_ref, bias_ref, normed_ref, q_ref, k_ref, v_ref, out_ref):
    half = q_ref.shape[1]

    def body(tokens, stream):
        norm, _ = normalise(tokens.astype(F32))
        normed = (norm * (1.0 + mod_ref[0, 1]) + mod_ref[0, 0]).astype(BF16)
        normed_ref[...] = normed
        joint = dot(normed, weight_ref[0, :, : 3 * half]) + bias_ref[0]
        q_ref[...] = joint[:, :half].astype(BF16)
        k_ref[...] = joint[:, half : 2 * half].astype(BF16)
        v_ref[...] = joint[:, 2 * half :].astype(BF16)

    by_stream(steps, image_ref, text_ref, body)

    @pl.when(lax.rem(pl.program_id(0), steps) == 0)
    def _():
        out_ref[0] = weight_ref[0, :, 3 * half :]


def project(image, text, mod, weight, bias):
    (rows, width), wide = image.shape, weight.shape[2]
    steps, half = rows // QUERY_BLOCK, wide // 4
    joint = rows + QUERY_BLOCK
    heads = [(stepped((QUERY_BLOCK, half)), jax.ShapeDtypeStruct((joint, half), BF16))] * 3
    return local_call(
        functools.partial(project_kernel, steps),
        steps + 1,
        [
            image_block((QUERY_BLOCK, width), steps - 1),
            fixed(text.shape),
            stream_block((1,) + mod.shape[1:], steps),
            stream_block((1,) + weight.shape[1:], steps),
            stream_block((1,) + bias.shape[1:], steps),
        ],
        [(stepped((QUERY_BLOCK, width)), jax.ShapeDtypeStruct((joint, width), BF16))]
        + heads
        + [(stream_block((1, width, half), steps), jax.ShapeDtypeStruct((2, width, half), BF16))],
        [],
        6 * joint * width * half,
        "project",
    )(image, text, mod, weight, bias)


def key_bias(rows, image_rows, text_rows):
    slot = lax.broadcasted_iota(jnp.int32, (rows, 1), 0)
    text_slot = slot - image_rows
    unused = jnp.logical_or(lax.rem(text_slot, TEXT_SLOTS) >= text_rows, text_slot >= 2 * TEXT_SLOTS)
    masked = jnp.logical_and(text_slot >= 0, unused)
    return jnp.where(masked, -1e30, 0.0).astype(F32)


def attend_forward_kernel(
    steps, heads, text_rows, q_ref, k_ref, v_ref, weight_ref, o_ref, lse_ref, image_ref, text_ref, vt_ref
):
    step = pl.program_id(0)

    @pl.when(step == 0)
    def _():
        vt_ref[...] = v_ref[...].T

    rows = k_ref.shape[0]
    bias = key_bias(rows, steps * QUERY_BLOCK, text_rows)
    queries_t = (q_ref[...] * HEAD_DIM ** (-0.5)).T
    outs = []
    for head in range(heads):
        span = slice(head * HEAD_DIM, (head + 1) * HEAD_DIM)
        scores = dot(k_ref[:, span], queries_t[span]) + bias
        top = jnp.max(scores, axis=0, keepdims=True)
        grown = jnp.exp(scores - top)
        total = jnp.sum(grown, axis=0, keepdims=True)
        lse_ref[head : head + 1] = top + jnp.log(total)
        outs.append(dot(vt_ref[span], grown.astype(BF16)) * (1.0 / total))
    blended = jnp.concatenate(outs, 0).T.astype(BF16)
    o_ref[...] = blended
    branch = dot(blended, weight_ref[0], ((1,), (1,))).astype(BF16)

    @pl.when(step < steps)
    def _():
        image_ref[...] = branch

    @pl.when(step >= steps)
    def _():
        text_ref[...] = branch[: text_ref.shape[0]]


def attend_forward(q, k, v, weight, text_all, text_rows):
    rows, wide = q.shape
    width = weight.shape[1]
    heads = wide // HEAD_DIM
    steps = rows // QUERY_BLOCK - 1
    return local_call(
        functools.partial(attend_forward_kernel, steps, heads, text_rows),
        steps + 1,
        [
            stepped((QUERY_BLOCK, wide)),
            fixed((rows, wide)),
            fixed((rows, wide)),
            stream_block((1, width, wide), steps),
        ],
        [
            (stepped((QUERY_BLOCK, wide)), jax.ShapeDtypeStruct((rows, wide), BF16)),
            (pl.BlockSpec((heads, QUERY_BLOCK), lambda i: (0, i)), jax.ShapeDtypeStruct((heads, rows), F32)),
            (image_block((QUERY_BLOCK, width), steps - 1), jax.ShapeDtypeStruct((steps * QUERY_BLOCK, width), BF16)),
            (pl.BlockSpec((text_all, width), lambda i: (0, 0)), jax.ShapeDtypeStruct((text_all, width), BF16)),
        ],
        [pltpu.VMEM((wide, rows), BF16)],
        4 * rows * rows * wide,
        "attend_forward",
    )(q, k, v, weight)


def out_gradient_kernel(steps, image_ref, text_ref, o_ref, dw_ref, dw_sum):
    step = pl.program_id(0)
    wide = o_ref.shape[1]

    @pl.when(step == 0)
    def _():
        dw_sum[...] = jnp.zeros_like(dw_sum)

    def add(arriving, stream):
        dw_sum[stream] += dot(arriving, o_ref[...], ((0,), (0,)))

    by_stream(steps, image_ref, text_ref, add)

    @pl.when(step == steps)
    def _():
        for stream in range(2):
            dw_ref[:, stream * wide : (stream + 1) * wide] = dw_sum[stream].astype(BF16)


def out_gradient(image, text, blended):
    rows, wide = blended.shape
    width = image.shape[1]
    steps = rows // QUERY_BLOCK - 1
    return local_call(
        functools.partial(out_gradient_kernel, steps),
        steps + 1,
        [image_block((QUERY_BLOCK, width), steps - 1), fixed(text.shape), stepped((QUERY_BLOCK, wide))],
        [(pl.BlockSpec((width, 2 * wide), lambda i: (0, 0)), jax.ShapeDtypeStruct((width, 2 * wide), BF16))],
        [pltpu.VMEM((2, width, wide), F32)],
        2 * rows * width * wide,
        "out_gradient",
    )(image, text, blended)[0]


def attend_backward_kernel(
    steps,
    heads,
    text_rows,
    q_ref,
    k_ref,
    v_ref,
    lse_ref,
    image_ref,
    text_ref,
    weight_ref,
    dq_ref,
    dk_ref,
    dv_ref,
    kt_ref,
    g_ref,
    dk_sum,
    dv_sum,
):
    step = pl.program_id(0)

    @pl.when(step == 0)
    def _():
        kt_ref[...] = k_ref[...].T
        dk_sum[...] = jnp.zeros_like(dk_sum)
        dv_sum[...] = jnp.zeros_like(dv_sum)

    def bring(arriving, stream):
        g_ref[...] = dot(arriving, weight_ref[0]).astype(BF16)

    by_stream(steps, image_ref, text_ref, bring)
    rows = k_ref.shape[0]
    bias = key_bias(rows, steps * QUERY_BLOCK, text_rows)
    queries = q_ref[...] * HEAD_DIM ** (-0.5)
    queries_t = queries.T
    grads = g_ref[...]
    grads_t = grads.T
    outs = []
    for head in range(heads):
        span = slice(head * HEAD_DIM, (head + 1) * HEAD_DIM)
        scores = dot(k_ref[:, span], queries_t[span]) + bias
        prob = jnp.exp(scores - lse_ref[head : head + 1])
        grad_prob = dot(v_ref[:, span], grads_t[span])
        weighted = prob * grad_prob
        inner = jnp.sum(weighted, axis=0, keepdims=True)
        grad_score = (weighted - prob * inner).astype(BF16)
        dv_sum[head] += dot(prob.astype(BF16), grads[:, span])
        dk_sum[head] += dot(grad_score, queries[:, span])
        outs.append(dot(kt_ref[span], grad_score) * HEAD_DIM ** (-0.5))
    dq_ref[...] = jnp.concatenate(outs, 0).T.astype(BF16)

    @pl.when(step == steps)
    def _():
        dk_ref[...] = jnp.concatenate([dk_sum[head] for head in range(heads)], 1).astype(BF16)
        dv_ref[...] = jnp.concatenate([dv_sum[head] for head in range(heads)], 1).astype(BF16)


def attend_backward(q, k, v, lse, image, text, weight, text_rows):
    rows, wide = q.shape
    width = weight.shape[1]
    heads = wide // HEAD_DIM
    steps = rows // QUERY_BLOCK - 1
    block = stepped((QUERY_BLOCK, wide))
    whole = pl.BlockSpec((rows, wide), lambda i: (0, 0))
    return local_call(
        functools.partial(attend_backward_kernel, steps, heads, text_rows),
        steps + 1,
        [
            block,
            fixed((rows, wide)),
            fixed((rows, wide)),
            pl.BlockSpec((heads, QUERY_BLOCK), lambda i: (0, i)),
            image_block((QUERY_BLOCK, width), steps - 1),
            fixed(text.shape),
            stream_block((1, width, wide), steps),
        ],
        [
            (block, jax.ShapeDtypeStruct((rows, wide), BF16)),
            (whole, jax.ShapeDtypeStruct((rows, wide), BF16)),
            (whole, jax.ShapeDtypeStruct((rows, wide), BF16)),
        ],
        [
            pltpu.VMEM((wide, rows), BF16),
            pltpu.VMEM((QUERY_BLOCK, wide), BF16),
            pltpu.VMEM((heads, rows, HEAD_DIM), F32),
            pltpu.VMEM((heads, rows, HEAD_DIM), F32),
        ],
        10 * rows * rows * wide,
        "attend_backward",
    )(q, k, v, lse, image, text, weight)


def unproject_kernel(
    steps, dq_ref, dk_ref, dv_ref, normed_ref, weight_ref, image_ref, text_ref, dw_ref, sums_ref, dw_sum
):
    step = pl.program_id(0)
    half = dq_ref.shape[1]
    stream = step // steps

    @pl.when(step == 0)
    def _():
        dw_sum[...] = jnp.zeros_like(dw_sum)
        sums_ref[...] = jnp.zeros_like(sums_ref)

    grads = jnp.concatenate([dq_ref[...], dk_ref[...], dv_ref[...]], 1)
    part = dot(grads, weight_ref[0, :, : 3 * half], ((1,), (1,))).astype(BF16)
    dw_sum[stream] += dot(normed_ref[...], grads, ((0,), (0,)))
    sums_ref[stream] += jnp.sum(grads.astype(F32), axis=0, keepdims=True)

    @pl.when(step < steps)
    def _():
        image_ref[...] = part

    @pl.when(step == steps)
    def _():
        text_ref[...] = part[: text_ref.shape[0]]
        for s in range(2):
            dw_ref[:, s * 3 * half : (s + 1) * 3 * half] = dw_sum[s].astype(BF16)


def unproject(dq, dk, dv, normed, weight, text_all):
    rows, half = dq.shape
    width = normed.shape[1]
    steps = rows // QUERY_BLOCK - 1
    block = stepped((QUERY_BLOCK, half))
    return local_call(
        functools.partial(unproject_kernel, steps),
        steps + 1,
        [
            block,
            block,
            block,
            stepped((QUERY_BLOCK, width)),
            stream_block((1,) + weight.shape[1:], steps),
        ],
        [
            (image_block((QUERY_BLOCK, width), steps - 1), jax.ShapeDtypeStruct((steps * QUERY_BLOCK, width), BF16)),
            (pl.BlockSpec((text_all, width), lambda i: (0, 0)), jax.ShapeDtypeStruct((text_all, width), BF16)),
            (pl.BlockSpec((width, 6 * half), lambda i: (0, 0)), jax.ShapeDtypeStruct((width, 6 * half), BF16)),
            (pl.BlockSpec((2, 1, 3 * half), lambda i: (0, 0, 0)), jax.ShapeDtypeStruct((2, 1, 3 * half), F32)),
        ],
        [pltpu.VMEM((2, width, 3 * half), F32)],
        12 * rows * width * half,
        "unproject",
    )(dq, dk, dv, normed, weight)


def feed_kernel(
    halves,
    ctx_ref,
    second_ref,
    cot_ref,
    other_ref,
    gate_ref,
    up_ref,
    down_ref,
    bias_ref,
    feed_ref,
    pull_ref,
    dw_ref,
    sums_ref,
    up_sum,
    down_sum,
    gate_rows,
):
    step = pl.program_id(0)
    wide = up_ref.shape[1]

    @pl.when(step == 0)
    def _():
        up_sum[...] = jnp.zeros_like(up_sum)
        down_sum[...] = jnp.zeros_like(down_sum)
        sums_ref[...] = jnp.zeros_like(sums_ref)
        groups = gate_ref.shape[0]
        if halves:
            gate_rows[...] = gate_ref[...]
        else:
            rows = gate_rows.shape[0] // (2 * groups)
            for block in range(2 * groups):
                gate = gate_ref[block % groups : block % groups + 1]
                gate_rows[block * rows : (block + 1) * rows] = jnp.broadcast_to(gate, (rows, gate.shape[1]))

    arriving = cot_ref[...]
    if halves:
        arriving = jnp.where(step // halves == ctx_ref[0], arriving, other_ref[...])
    arriving = (arriving.astype(F32) * gate_rows[...]).astype(BF16)
    second = second_ref[...]
    hidden = dot(second, up_ref[...]) + bias_ref[...]
    gelu_out, slope = gelu_parts(hidden)
    gelu_low = gelu_out.astype(BF16)
    feed_ref[...] = dot(gelu_low, down_ref[...], ((1,), (1,))).astype(BF16)
    down_sum[...] += dot(arriving, gelu_low, ((0,), (0,)))
    pulled = (dot(arriving, down_ref[...]) * slope).astype(BF16)
    sums_ref[...] += jnp.sum(pulled.astype(F32), axis=0, keepdims=True)
    up_sum[...] += dot(second, pulled, ((0,), (0,)))
    pull_ref[...] = dot(pulled, up_ref[...], ((1,), (1,))).astype(BF16)

    @pl.when(step == pl.num_programs(0) - 1)
    def _():
        dw_ref[:, :wide] = up_sum[...].astype(BF16)
        dw_ref[:, wide:] = down_sum[...].astype(BF16)


def feed_forward(ctx, second, cot, other, gate, up, down, bias):
    (up, up_at), (down, down_at) = up, down
    (rows, width), wide, groups = second.shape, up.shape[2], gate.shape[0]
    if other is None:
        block_rows, halves, gate_rows = 2 * TEXT_SLOTS // 4 * groups, 0, 2 * TEXT_SLOTS // 4 * groups
        other, last = cot[:8], 0
        cot_spec = pl.BlockSpec((block_rows, width), lambda i, c: (i, 0))
        other_spec = pl.BlockSpec((8, width), lambda i, c: (0, 0))
    else:
        block_rows = min(QUERY_BLOCK, cot.shape[0])
        halves, gate_rows = cot.shape[0] // block_rows, 1
        last = halves - 1
        cot_spec = pl.BlockSpec((block_rows, width), lambda i, c: (jnp.clip(i - c[0] * halves, 0, last), 0))
        other_spec = pl.BlockSpec((block_rows, width), lambda i, c: (jnp.clip(i - (1 - c[0]) * halves, 0, last), 0))
    block = pl.BlockSpec((block_rows, width), lambda i, c: (i, 0))

    def once(shape):
        return pl.BlockSpec(shape, lambda i, c: (0, 0), pipeline_mode=pl.Buffered(1))

    flops = 12 * rows * width * wide
    return pl.pallas_call(
        functools.partial(feed_kernel, halves),
        grid_spec=pltpu.PrefetchScalarGridSpec(
            num_scalar_prefetch=1,
            grid=(rows // block_rows,),
            in_specs=[
                block,
                cot_spec,
                other_spec,
                once(gate.shape),
                pl.BlockSpec(
                    (None,) + up.shape[1:], lambda i, c: (up_at, 0, 0), pipeline_mode=pl.Buffered(1)
                ),
                pl.BlockSpec(
                    (None,) + down.shape[1:], lambda i, c: (down_at, 0, 0), pipeline_mode=pl.Buffered(1)
                ),
                once((1, wide)),
            ],
            out_specs=[
                block,
                block,
                pl.BlockSpec((width, 2 * wide), lambda i, c: (0, 0)),
                pl.BlockSpec((1, wide), lambda i, c: (0, 0)),
            ],
            scratch_shapes=[pltpu.VMEM((width, wide), F32)] * 2 + [pltpu.VMEM((gate_rows, width), F32)],
        ),
        out_shape=[
            jax.ShapeDtypeStruct((rows, width), BF16),
            jax.ShapeDtypeStruct((rows, width), BF16),
            jax.ShapeDtypeStruct((width, 2 * wide), BF16),
            jax.ShapeDtypeStruct((1, wide), F32),
        ],
        compiler_params=pltpu.CompilerParams(vmem_limit_bytes=VMEM_LIMIT),
        cost_estimate=pl.CostEstimate(flops=flops, bytes_accessed=flops // 256, transcendentals=0),
        name="feed_forward",
    )(ctx, second, cot, other, gate, up, down, bias.reshape(1, wide))


def place_feed_kernel(ctx_ref, mine_ref, other_ref, moved_ref, up_ref, down_ref):
    ctx = ctx_ref[0]
    cols = mine_ref.shape[2] // 2
    text_cols = moved_ref.shape[2] // 2
    groups = moved_ref.shape[0] // 2

    def place(span):
        kept, other = mine_ref[ctx, span], other_ref[span]
        for c in range(2):
            part = jnp.where(ctx == c, kept, other).astype(F32)
            up_ref[0, span, c * cols : (c + 1) * cols] = part[:, :cols]
            down_ref[0, span, c * cols : (c + 1) * cols] = part[:, cols:]
            for group in range(groups):
                start = c * cols + group * text_cols
                text = moved_ref[group * 2 + c, span].astype(F32)
                up_ref[1, span, start : start + text_cols] = text[:, :text_cols]
                down_ref[1, span, start : start + text_cols] = text[:, text_cols:]

    over_rows(other_ref.shape[0], place)


def place_feed(ctx, mine, other, moved):
    rows, cols = other.shape
    shape = jax.ShapeDtypeStruct((2, rows, cols), F32)
    return pl.pallas_call(
        place_feed_kernel,
        in_specs=[pl.BlockSpec(memory_space=pltpu.SMEM)] + [pl.BlockSpec(memory_space=pltpu.VMEM)] * 3,
        out_specs=[pl.BlockSpec(memory_space=pltpu.VMEM)] * 2,
        out_shape=[shape, shape],
        compiler_params=pltpu.CompilerParams(vmem_limit_bytes=VMEM_LIMIT),
        name="place_feed",
    )(ctx, mine.reshape(2, rows, cols), other, moved)


def place_heads_kernel(kinds, ctx_ref, mine_ref, other_ref, out_ref):
    ctx = ctx_ref[0]
    half = out_ref.shape[3] // 2

    def place(span):
        kept, other = mine_ref[ctx, span], other_ref[span]
        for c in range(2):
            part = jnp.where(ctx == c, kept, other).astype(F32)
            for s in range(2):
                for j in range(kinds):
                    start = (kinds * s + j) * half
                    out_ref[s, j, span, c * half : (c + 1) * half] = part[:, start : start + half]

    over_rows(other_ref.shape[0], place)


def place_heads(kinds, ctx, mine, other):
    rows, cols = other.shape
    return pl.pallas_call(
        functools.partial(place_heads_kernel, kinds),
        in_specs=[pl.BlockSpec(memory_space=pltpu.SMEM)] + [pl.BlockSpec(memory_space=pltpu.VMEM)] * 2,
        out_specs=pl.BlockSpec(memory_space=pltpu.VMEM),
        out_shape=jax.ShapeDtypeStruct((2, kinds, rows, cols // kinds), F32),
        compiler_params=pltpu.CompilerParams(vmem_limit_bytes=VMEM_LIMIT),
        name="place_heads",
    )(ctx, mine.reshape(2, rows, cols), other)


def place_qkv(ctx, mine, other):
    return place_heads(3, ctx, mine, other).transpose(0, 2, 1, 3)


def place_out(ctx, mine, other):
    return place_heads(1, ctx, mine, other)[:, 0]


def normalise(inputs):
    centred = inputs - jnp.mean(inputs, axis=-1, keepdims=True)
    spread = lax.rsqrt(jnp.mean(centred * centred, axis=-1, keepdims=True) + 1e-06)
    return centred * spread, spread


def normalise_back(grad_norm, norm, spread):
    return spread * (
        grad_norm
        - jnp.mean(grad_norm, axis=-1, keepdims=True)
        - norm * jnp.mean(grad_norm * norm, axis=-1, keepdims=True)
    )


def gelu_parts(hidden):
    root = 0.7978845608028654
    square = hidden * hidden
    bent = jnp.tanh(hidden * (root + root * 0.044715 * square))
    half = 0.5 * (1.0 + bent)
    slope = half + 0.5 * hidden * (1.0 - bent * bent) * (root + 3.0 * root * 0.044715 * square)
    return hidden * half, slope


MESH = pl.DeviceIdType.MESH
VMEM_SPEC = pl.BlockSpec(memory_space=pltpu.VMEM)
ANY_SPEC = pl.BlockSpec(memory_space=pl.ANY)


class Wires:
    def __init__(self, send_sems, recv_sems):
        self.dp, self.x, self.tp = lax.axis_index("dp"), lax.axis_index("ctx"), lax.axis_index("tp")
        self.y, self.k = self.tp // 2, self.tp % 2
        self.x_next = (self.dp, 1 - self.x, self.tp)
        self.y_next = (self.dp, self.x, (1 - self.y) * 2 + self.k)
        self.k_next = (self.dp, self.x, self.y * 2 + 1 - self.k)
        self.send_sems, self.recv_sems, self.used = send_sems, recv_sems, 0
        self.started = []

    def copy(self, source, target, device):
        wire = pltpu.make_async_remote_copy(
            src_ref=source,
            dst_ref=target,
            send_sem=self.send_sems.at[self.used],
            recv_sem=self.recv_sems.at[self.used],
            device_id=device,
            device_id_type=MESH,
        )
        self.used += 1
        wire.start()
        self.started.append(wire)
        return wire

    def meet(self, devices):
        barrier = pltpu.get_barrier_semaphore()
        for device in devices:
            pl.semaphore_signal(barrier, inc=1, device_id=device, device_id_type=MESH)
        pl.semaphore_wait(barrier, len(devices))

    def finish(self):
        for wire in self.started:
            wire.wait_send()


def row_step(rows):
    return 32 if rows % 32 == 0 else rows


def over_rows(rows, body):
    step = row_step(rows)
    if step == rows:
        body(slice(0, rows))
        return

    def one(index, carry):
        body(pl.ds(pl.multiple_of(index * step, step), step))
        return carry

    lax.fori_loop(0, rows // step, one, 0)


def reduce_first(wires, s):
    return wires.copy(s["part"].at[:, :, 1 - wires.k], s["core"], wires.k_next)


def reduce_add(wires, s, arrived):
    k = wires.k
    part, core, held = s["part"], s["core"], s["held"]
    arrived.wait_recv()
    for i in range(2):
        for j in range(2):

            def add(span, i=i, j=j):
                held[i, j, span] = (part[i, j, k, span].astype(F32) + core[i, j, span].astype(F32)).astype(BF16)

            over_rows(part.shape[3], add)


def reduce_second(wires, s):
    held = s["held"]
    cut = held.shape[3] // 2
    return (
        wires.copy(held.at[:, 1 - wires.y, :, pl.ds(0, cut)], s["along_y"], wires.y_next),
        wires.copy(held.at[1 - wires.x, :, :, pl.ds(cut, cut)], s["along_x"], wires.x_next),
    )


def reduce_third(wires, s, second):
    x, y = wires.x, wires.y
    held, along_y, along_x, out_x, out_y = s["held"], s["along_y"], s["along_x"], s["out_x"], s["out_y"]
    cut = held.shape[3] // 2
    for arrived in second:
        arrived.wait_recv()

    def add(span):
        out_x[span] = (held[1 - x, y, span, :cut].astype(F32) + along_y[1 - x, span].astype(F32)).astype(BF16)
        out_y[span] = (held[x, 1 - y, span, cut:].astype(F32) + along_x[1 - y, span].astype(F32)).astype(BF16)

    over_rows(held.shape[2], add)
    return (
        wires.copy(out_x, s["last_x"], wires.x_next),
        wires.copy(out_y, s["last_y"], wires.y_next),
    )


def reduce_last(wires, s, third):
    x, y = wires.x, wires.y
    held, along_y, along_x, last_x, last_y, total = (
        s["held"],
        s["along_y"],
        s["along_x"],
        s["last_x"],
        s["last_y"],
        s["total"],
    )
    cut = held.shape[3] // 2
    for arrived in third:
        arrived.wait_recv()

    def add(span):
        total[span, :cut] = (
            held[x, y, span, :cut].astype(F32) + along_y[x, span].astype(F32) + last_x[span].astype(F32)
        )
        total[span, cut:] = (
            held[x, y, span, cut:].astype(F32) + along_x[y, span].astype(F32) + last_y[span].astype(F32)
        )

    over_rows(held.shape[2], add)


def reduce_plane(wires, streams):
    first = [reduce_first(wires, s) for s in streams]
    second = []
    for s, arrived in zip(streams, first):
        reduce_add(wires, s, arrived)
        second.append(reduce_second(wires, s))
    third = [reduce_third(wires, s, arrived) for s, arrived in zip(streams, second)]
    for s, arrived in zip(streams, third):
        reduce_last(wires, s, arrived)


REDUCE_KEYS = ("core", "held", "along_y", "along_x", "out_x", "out_y", "last_x", "last_y", "total")


def reduce_scratch(rows, width):
    half = width // 2
    return [
        pltpu.VMEM((2, 2, rows, width), BF16),
        pltpu.VMEM((2, 2, rows, width), BF16),
        pltpu.VMEM((2, rows, half), BF16),
        pltpu.VMEM((2, rows, half), BF16),
        pltpu.VMEM((rows, half), BF16),
        pltpu.VMEM((rows, half), BF16),
        pltpu.VMEM((rows, half), BF16),
        pltpu.VMEM((rows, half), BF16),
        pltpu.VMEM((rows, width), F32),
    ]


def block_halves(block):
    cut = block.shape[-1] // 2
    inner = (slice(None),) * (len(block.shape) - 4)
    return inner + (pl.ds(0, cut),), inner + (pl.ds(cut, cut),)


def spread_first(wires, block):
    x, y, k = wires.x, wires.y, wires.k
    low, high = block_halves(block)
    mine = block.at[(x, y, k) + low], block.at[(x, y, k) + high]
    return wires.copy(mine[0], mine[0], wires.x_next), wires.copy(mine[1], mine[1], wires.y_next)


def spread_second(wires, block, first):
    x, y, k = wires.x, wires.y, wires.k
    low, high = block_halves(block)
    for arrived in first:
        arrived.wait_recv()
    lows, highs = block.at[(slice(None), y, k) + low], block.at[(x, slice(None), k) + high]
    return wires.copy(lows, lows, wires.y_next), wires.copy(highs, highs, wires.x_next)


def spread_third(wires, block, second):
    for arrived in second:
        arrived.wait_recv()
    gathered = block.at[:, :, wires.k]
    return wires.copy(gathered, gathered, wires.k_next)


def spread_plane(wires, blocks, started=()):
    first = list(started) + [spread_first(wires, block) for block in blocks[len(started) :]]
    second = [spread_second(wires, block, arrived) for block, arrived in zip(blocks, first)]
    third = [spread_third(wires, block, arrived) for block, arrived in zip(blocks, second)]
    for arrived in third:
        arrived.wait_recv()


def comm_call(kernel, outs, scratch, wires, collective_id, name, in_specs, out_specs):
    return pl.pallas_call(
        kernel,
        out_shape=outs,
        in_specs=in_specs,
        out_specs=out_specs,
        scratch_shapes=scratch + [pltpu.SemaphoreType.DMA((wires,)), pltpu.SemaphoreType.DMA((wires,))],
        compiler_params=pltpu.CompilerParams(
            collective_id=collective_id, has_side_effects=True, vmem_limit_bytes=VMEM_LIMIT
        ),
        name=name,
    )


def enter_kernel(
    n_dp,
    groups,
    part_ref,
    bias_ref,
    rows_ref,
    image_ref,
    text_ref,
    attn_ref,
    up_ref,
    down_ref,
    mod_ref,
    rows_out,
    image_out,
    text_out,
    gates_out,
    attn_out,
    ffn_out,
    moved_out,
    mod_in,
    send_sems,
    recv_sems,
):
    wires = Wires(send_sems, recv_sems)
    dp, x, y, k, tp = wires.dp, wires.x, wires.y, wires.k, wires.tp
    count = n_dp * 2
    me = dp * 2 + x
    peers = [lax.rem(me + offset, count) for offset in range(1, count)]
    others = [(peer // 2, peer % 2, tp) for peer in peers]
    lanes = [lax.rem(tp + offset, 4) for offset in range(1, 4)]
    z_next = (lax.rem(dp + 1, n_dp), x, tp)
    wires.meet(others + [(dp, x, lane) for lane in lanes])

    sums = [wires.copy(part_ref.at[peer // 2], mod_in.at[me], other) for peer, other in zip(peers, others)]
    rows = [wires.copy(rows_ref, rows_out.at[me], other) for other in others]
    swaps = [wires.copy(attn_ref.at[1 - x, s], attn_out.at[s, dp, x], wires.x_next) for s in range(2)]
    mod_in[me] = part_ref[dp]
    rows_out[me] = rows_ref[...]
    for arrived in sums:
        arrived.wait_recv()
    ring = {(s, 0): wires.copy(attn_ref.at[x, s], attn_out.at[s, dp, x], z_next) for s in range(2)}
    total = bias_ref[...]
    for source in range(count):
        total = total + mod_in[source]
    mod_ref[tp] = total
    mods = [wires.copy(mod_ref.at[tp], mod_ref.at[tp], (dp, x, lane)) for lane in lanes]
    for arrived in mods:
        arrived.wait_recv()
    gates = []
    if groups > 1:
        gates = [
            wires.copy(mod_ref.at[:, 11], gates_out.at[dp], (lax.rem(dp + offset, groups), x, tp))
            for offset in range(1, groups)
        ]
        for lane in range(4):
            gates_out[dp, lane] = mod_ref[lane, 11]

    def pass_on(turn, side):
        for s in range(2):
            ring[s, side].wait_recv()
            if turn < n_dp - 1:
                origin = lax.rem(dp + n_dp - turn, n_dp)
                block = attn_out.at[s, origin, x if side == 0 else 1 - x]
                ring[s, side] = wires.copy(block, block, z_next)

    streams = ((image_ref, image_out), (text_ref, text_out))
    cols = ffn_out.shape[3]
    wide = ffn_out.shape[0] // 2
    held = []
    for i, weight in enumerate((up_ref, down_ref)):
        for s in range(wide):
            given = weight.at[s, :, pl.ds(pl.multiple_of((1 - x) * cols, cols), cols)]
            held.append((given, ffn_out.at[i * wide + s, x]))
    for s, arrived in enumerate(swaps):
        arrived.wait_recv()
        block = attn_out.at[s, dp, 1 - x]
        ring[s, 1] = wires.copy(block, block, z_next)
    along_x = [wires.copy(ref.at[tp], out.at[x, tp], wires.x_next) for ref, out in streams]
    pass_on(1, 0)
    along_y = []
    for (_, out), arrived in zip(streams, along_x):
        arrived.wait_recv()
        block = out.at[1 - x, tp]
        along_y.append(wires.copy(block, block, wires.y_next))
    across = []
    for _, out in streams:
        block = out.at[1 - x, tp]
        across.append(wires.copy(block, block, wires.k_next))
    later = [wires.copy(given, place, wires.x_next) for given, place in held]

    def keep_tokens(span):
        for block in range(4):
            image_out[x, block, span] = image_ref[block, span]

    def keep_weights(span):
        for s in range(2):
            attn_out[s, dp, x, span] = attn_ref[x, s, span]
        for i, weight in enumerate((up_ref, down_ref)):
            for s in range(wide):
                first, last = weight[s, span, :cols], weight[s, span, cols:]
                ffn_out[i * wide + s, x, span] = jnp.where(x == 0, first, last)
            if groups > 1:
                text_cols = cols // groups
                for peer in range(count):
                    start = (peer % 2) * cols + (peer // 2) * text_cols
                    text = weight[1, span, start : start + text_cols]
                    moved_out[peer, span, i * text_cols : (i + 1) * text_cols] = text

    over_rows(image_ref.shape[1], keep_tokens)
    over_rows(attn_ref.shape[2], keep_weights)
    for block in range(4):
        text_out[x, block] = text_ref[block]
    pass_on(1, 1)
    far = (1 - y) * 2 + k
    for (_, out), arrived in zip(streams, along_y):
        arrived.wait_recv()
        block = out.at[1 - x, far]
        across.append(wires.copy(block, block, wires.k_next))
    for turn in range(2, n_dp - 1):
        pass_on(turn, 0)
        pass_on(turn, 1)
    if n_dp > 2:
        pass_on(n_dp - 1, 0)
        pass_on(n_dp - 1, 1)
    for arrived in rows + across + later + gates:
        arrived.wait_recv()
    wires.finish()


def enter(groups, partial_mod, ada_bias, bias_rows, image, text, attn, up, down, wide):
    n_dp, kinds, slice_width = partial_mod.shape
    count = 2 * n_dp
    rows, cols = up.shape[1], up.shape[2] // 2
    width = image.shape[2]
    return comm_call(
        functools.partial(enter_kernel, n_dp, groups),
        [
            jax.ShapeDtypeStruct((4, kinds, slice_width), F32),
            jax.ShapeDtypeStruct((count,) + bias_rows.shape, F32),
            jax.ShapeDtypeStruct((2,) + image.shape, BF16),
            jax.ShapeDtypeStruct((2,) + text.shape, BF16),
            jax.ShapeDtypeStruct((groups, 4, slice_width), F32),
            jax.ShapeDtypeStruct((2, n_dp, 2) + attn.shape[2:], BF16),
            jax.ShapeDtypeStruct((2 * wide, 2, rows, cols), BF16),
            jax.ShapeDtypeStruct((2 * groups, rows, 2 * cols // groups) if groups > 1 else (1, 8, 128), BF16),
        ],
        [pltpu.VMEM((count, kinds, slice_width), F32)],
        2 * (count - 1) + 2 + 4 * n_dp + 16 + groups + 5,
        0,
        "enter",
        [VMEM_SPEC] * 8,
        [VMEM_SPEC] * 8,
    )(partial_mod, ada_bias, bias_rows, image, text, attn, up, down)


def meet_groups(wires, groups, more=()):
    dp, x, tp = wires.dp, wires.x, wires.tp
    count = groups * 2
    if groups == 1:
        others = [wires.x_next]
    else:
        peers = [lax.rem(dp * 2 + x + offset, count) for offset in range(1, count)]
        others = [(peer // 2, peer % 2, tp) for peer in peers]
    wires.meet(others + [wires.y_next, wires.k_next, *more])


def start_moves(wires, groups, moved_ref, moved_out, local_sem):
    if groups == 1:
        return []
    dp, x, tp = wires.dp, wires.x, wires.tp
    count = groups * 2
    me = dp * 2 + x
    peers = [lax.rem(me + offset, count) for offset in range(1, count)]
    local = pltpu.make_async_copy(moved_ref.at[me], moved_out.at[me], local_sem)
    local.start()
    return [local] + [
        wires.copy(moved_ref.at[peer], moved_out.at[me], (peer // 2, peer % 2, tp)) for peer in peers
    ]


def end_moves(moves):
    if moves:
        moves[0].wait()
    for arrived in moves[1:]:
        arrived.wait_recv()


def middle_kernel(
    n_dp,
    groups,
    image_part,
    text_part,
    image_x,
    text_x,
    mod_ref,
    bias_ref,
    moved_ref,
    *rest,
):
    ffn_refs = rest[: n_dp - 1]
    (
        cot_ref,
        image_attention,
        text_attention,
        image_middle,
        text_middle,
        image_all,
        text_all,
        cots_all,
        moved_out,
        ffn_out,
    ) = rest[n_dp - 1 : n_dp + 9]
    scratch = rest[n_dp + 9 :]
    local_sem, send_sems, recv_sems = scratch[-3:]
    wires = Wires(send_sems, recv_sems)
    dp, x, y, k, tp = wires.dp, wires.x, wires.y, wires.k, wires.tp
    z_next = (lax.rem(dp + 1, n_dp), x, tp)
    meet_groups(wires, groups, [z_next] if groups == 1 else [])
    cots = []
    if groups > 1:
        cots_all[x, y, k, dp] = cot_ref[...]
        for offset in range(1, groups):
            block = cots_all.at[x, y, k, dp]
            cots.append(wires.copy(block, block, (lax.rem(dp + offset, groups), x, tp)))
    last = wires.copy(ffn_refs[n_dp - 2], ffn_out.at[:, lax.rem(dp + 2, n_dp)], z_next)
    size = len(REDUCE_KEYS)
    streams = [
        dict(zip(("part",) + REDUCE_KEYS, (part,) + scratch[i * size : (i + 1) * size]))
        for i, part in enumerate((image_part, text_part))
    ]

    def keep(span):
        for turn, block in enumerate(ffn_refs):
            for i in range(block.shape[0]):
                ffn_out[i, lax.rem(dp + n_dp - turn, n_dp), span] = block[i, span]

    image, text = streams
    first = reduce_first(wires, text), reduce_first(wires, image)
    reduce_add(wires, text, first[0])
    text_second = reduce_second(wires, text)
    reduce_add(wires, image, first[1])
    image_second = reduce_second(wires, image)
    for arrived in cots:
        arrived.wait_recv()
    if groups > 1:
        cots_first = spread_first(wires, cots_all)
    text_third = reduce_third(wires, text, text_second)
    image_third = reduce_third(wires, image, image_second)

    def second_rows(i, tokens, attention, middle, gathered):
        total = streams[i]["total"]

        def finish(span):
            branch = total[span] + bias_ref[i]
            attention[span] = branch
            value = tokens[span].astype(F32) + mod_ref[i, 2] * branch
            middle[span] = value
            norm, _ = normalise(value)
            gathered[x, y, k, span] = (norm * (1.0 + mod_ref[i, 4]) + mod_ref[i, 3]).astype(BF16)

        over_rows(total.shape[0], finish)

    reduce_last(wires, text, text_third)
    second_rows(1, text_x, text_attention, text_middle, text_all.at[:, :, :, dp if groups > 1 else 0])
    zs = []
    for offset in range(1, groups):
        block = text_all.at[x, y, k, dp]
        zs.append(wires.copy(block, block, (lax.rem(dp + offset, groups), x, tp)))
    if groups > 1:
        cots_second = spread_second(wires, cots_all, cots_first)
    reduce_last(wires, image, image_third)
    second_rows(0, image_x, image_attention, image_middle, image_all)
    image_first = spread_first(wires, image_all)
    for arrived in zs:
        arrived.wait_recv()
    text_first = spread_first(wires, text_all)
    moves = start_moves(wires, groups, moved_ref, moved_out, local_sem)
    thirds = [spread_third(wires, cots_all, cots_second)] if groups > 1 else []
    over_rows(ffn_out.shape[2], keep)
    image_next = spread_second(wires, image_all, image_first)
    text_next = spread_second(wires, text_all, text_first)
    thirds += [spread_third(wires, image_all, image_next), spread_third(wires, text_all, text_next)]
    for arrived in thirds:
        arrived.wait_recv()
    end_moves(moves)
    last.wait_recv()
    wires.finish()


def middle_step(groups, image_part, text_part, image_x, text_x, mod, bias, moved, ffn, cot):
    (image_rows, width), text_rows = image_x.shape, text_x.shape[0]
    outs = []
    for _ in range(2):
        outs += [jax.ShapeDtypeStruct((rows, width), F32) for rows in (image_rows, text_rows)]
    outs += [jax.ShapeDtypeStruct(image_part.shape, BF16)]
    outs += [jax.ShapeDtypeStruct((2, 2, 2, groups, text_rows, width), BF16)] * 2
    outs += [jax.ShapeDtypeStruct(moved.shape, BF16)]
    n_dp = len(ffn) + 1
    outs += [jax.ShapeDtypeStruct((ffn[0].shape[0], n_dp) + ffn[0].shape[1:], BF16)]
    return comm_call(
        functools.partial(middle_kernel, n_dp, groups),
        outs,
        reduce_scratch(image_rows, width) + reduce_scratch(text_rows, width) + [pltpu.SemaphoreType.DMA(())],
        30 + 4 * groups,
        1,
        "middle",
        [VMEM_SPEC] * 6 + [ANY_SPEC] + [VMEM_SPEC] * n_dp,
        [VMEM_SPEC] * 7 + [ANY_SPEC, VMEM_SPEC],
    )(image_part, text_part, image_x, text_x, mod, bias, moved, *ffn, cot)


def turn_kernel(
    groups,
    valid_ref,
    image_feed,
    text_feed,
    image_second,
    text_second,
    image_attention,
    text_attention,
    image_middle,
    text_middle,
    image_cot,
    text_cot,
    mod_ref,
    bias_ref,
    moved_ref,
    image_out,
    text_out,
    image_grad,
    text_grad,
    sums_ref,
    image_all,
    text_all,
    moved_out,
    *scratch,
):
    z_out, z_in, local_sem, send_sems, recv_sems = scratch[-5:]
    wires = Wires(send_sems, recv_sems)
    dp, x, y, k, tp = wires.dp, wires.x, wires.y, wires.k, wires.tp
    meet_groups(wires, groups)
    size = len(REDUCE_KEYS)
    streams = [
        dict(zip(("part",) + REDUCE_KEYS, (part,) + scratch[i * size : (i + 1) * size]))
        for i, part in enumerate((text_second, text_feed, image_second, image_feed))
    ]
    pulls, feeds = (streams[2], streams[0]), (streams[3], streams[1])
    order = [pulls[1], pulls[0], feeds[1], feeds[0]]
    rows = text_middle.shape[0]

    def to_planes(i, total):
        copies = []
        if groups > 1:
            for group in range(groups):
                z_out[i, group] = total[group * rows : (group + 1) * rows].astype(BF16)
            z_in[i, dp] = z_out[i, dp]
            for offset in range(1, groups):
                plane = lax.rem(dp + offset, groups)
                copies.append(wires.copy(z_out.at[i, plane], z_in.at[i, dp], (plane, x, tp)))
        return copies

    def from_planes(i, total, copies):
        for arrived in copies:
            arrived.wait_recv()
        if groups > 1:
            summed = z_in[i, 0].astype(F32)
            for group in range(1, groups):
                summed = summed + z_in[i, group].astype(F32)
            total[0:rows] = summed

    sums_ref[...] = jnp.zeros_like(sums_ref)
    sides = (
        (image_attention, image_middle, image_cot, image_out, image_grad, image_all),
        (text_attention, text_middle, text_cot, text_out, text_grad, text_all),
    )

    def add_sums(i, start, terms):
        for t, term in enumerate(terms):
            sums_ref[i, start + t : start + t + 1] += jnp.sum(term, axis=0, keepdims=True)

    def pull_side(i):
        attention, middle, cot, _, grad, gathered = sides[i]
        total = pulls[i]["total"]

        def finish(span):
            branch, value, arriving, pulled = attention[span], middle[span], cot[span].astype(F32), total[span]
            norm, spread = normalise(value)
            grad_middle = arriving + normalise_back(pulled * (1.0 + mod_ref[i, 4]), norm, spread)
            grad[span] = grad_middle
            low = (grad_middle * mod_ref[i, 2]).astype(BF16)
            gathered[x, y, k, span] = low
            add_sums(i, 0, (grad_middle * branch, pulled, pulled * norm))
            add_sums(i, 5, (low.astype(F32),))

        over_rows(middle.shape[0], finish)

    def feed_side(i):
        attention, middle, cot, out, _, _ = sides[i]
        total = feeds[i]["total"]

        def finish(span):
            branch, value, arriving = attention[span], middle[span], cot[span].astype(F32)
            fed = total[span] + bias_ref[i]
            gated_branch = mod_ref[i, 2] * branch
            gated_feed = mod_ref[i, 5] * fed
            result = value + gated_feed
            out[span] = result.astype(BF16)
            if i == 1:
                kept = valid_ref[span]
                result, gated_branch, gated_feed = result * kept, gated_branch * kept, gated_feed * kept
            own_feed = (arriving * mod_ref[i, 5]).astype(BF16).astype(F32)
            add_sums(i, 3, (arriving * fed, own_feed))
            add_sums(i, 6, (result * result, gated_branch * gated_branch, gated_feed * gated_feed))

        over_rows(middle.shape[0], finish)

    first = [reduce_first(wires, s) for s in order]
    pull_second = []
    for s, arrived in zip(order[:2], first[:2]):
        reduce_add(wires, s, arrived)
        pull_second.append(reduce_second(wires, s))
    for s, arrived in zip(order[2:], first[2:]):
        reduce_add(wires, s, arrived)
    pull_third = [reduce_third(wires, s, arrived) for s, arrived in zip(order[:2], pull_second)]
    feed_second = [reduce_second(wires, s) for s in order[2:]]
    reduce_last(wires, pulls[1], pull_third[0])
    planes = to_planes(0, pulls[1]["total"])
    reduce_last(wires, pulls[0], pull_third[1])
    pull_side(0)
    spread_one = [spread_first(wires, image_all)]
    from_planes(0, pulls[1]["total"], planes)
    pull_side(1)
    spread_one.append(spread_first(wires, text_all))
    feed_third = [reduce_third(wires, s, arrived) for s, arrived in zip(order[2:], feed_second)]
    spread_two = [spread_second(wires, block, arrived) for block, arrived in zip((image_all, text_all), spread_one)]
    reduce_last(wires, feeds[1], feed_third[0])
    planes = to_planes(1, feeds[1]["total"])
    moves = start_moves(wires, groups, moved_ref, moved_out, local_sem)
    reduce_last(wires, feeds[0], feed_third[1])
    spread_three = [spread_third(wires, block, arrived) for block, arrived in zip((image_all, text_all), spread_two)]
    feed_side(0)
    from_planes(1, feeds[1]["total"], planes)
    feed_side(1)
    for arrived in spread_three:
        arrived.wait_recv()
    end_moves(moves)
    wires.finish()


def turn_step(groups, valid, feeds, seconds, attentions, middles, cots, mod, bias, moved):
    width = middles[0].shape[1]
    rows = [part.shape[0] for part in middles]
    outs = [jax.ShapeDtypeStruct((r, width), BF16) for r in rows]
    outs += [jax.ShapeDtypeStruct((r, width), F32) for r in rows]
    outs += [jax.ShapeDtypeStruct((2, 16, width), F32)]
    outs += [jax.ShapeDtypeStruct((2, 2, 2, r, width), BF16) for r in rows]
    outs += [jax.ShapeDtypeStruct(moved.shape, BF16)]
    scratch = []
    for r in (rows[1] * groups, rows[0]):
        scratch += reduce_scratch(r, width) + reduce_scratch(r, width)
    scratch += [pltpu.VMEM((2, groups, rows[1], width), BF16)] * 2 + [pltpu.SemaphoreType.DMA(())]
    return comm_call(
        functools.partial(turn_kernel, groups),
        outs,
        scratch,
        30 + 4 * groups,
        2,
        "turn",
        [VMEM_SPEC] * 13 + [ANY_SPEC],
        [VMEM_SPEC] * 7 + [ANY_SPEC],
    )(valid, *feeds, *seconds, *attentions, *middles, *cots, mod, bias, moved)


PACKED = 24


def leave_kernel(
    n_dp,
    image_part,
    text_part,
    image_x,
    text_x,
    image_grad,
    text_grad,
    image_out,
    text_out,
    sums_ref,
    mod_ref,
    halves_ref,
    ffn_mine,
    out_mine,
    image_outs,
    text_outs,
    image_grads,
    text_grads,
    packed_out,
    halves_out,
    ffn_other,
    out_other,
    *scratch,
):
    send_sems, recv_sems = scratch[-2:]
    packed, packed_in, own_sums, both_halves, local_sums = scratch[-7:-2]
    wires = Wires(send_sems, recv_sems)
    dp, x, y, k, tp = wires.dp, wires.x, wires.y, wires.k, wires.tp
    me = x * 4 + tp
    peers = [lax.rem(me + offset, 8) for offset in range(1, 8)]
    planes = [lax.rem(dp + offset, n_dp) for offset in range(1, n_dp)]
    wires.meet([(dp, peer // 4, peer % 4) for peer in peers] + [(plane, x, tp) for plane in planes])

    image_outs[tp] = image_out[...]
    text_outs[tp] = text_out[...]
    both_halves[x] = halves_ref[...]
    halves = wires.copy(both_halves.at[x], both_halves.at[x], wires.x_next)
    size = len(REDUCE_KEYS)
    streams = [
        dict(zip(("part",) + REDUCE_KEYS, (part,) + scratch[i * size : (i + 1) * size]))
        for i, part in enumerate((image_part, text_part))
    ]
    reduce_plane(wires, streams)
    given = ffn_other.shape[0]
    given = pl.ds(pl.multiple_of((1 - x) * given, given), given)
    swaps = [
        wires.copy(mine.at[given], other, wires.x_next)
        for mine, other in ((ffn_mine, ffn_other), (out_mine, out_other))
    ]
    local_sums[...] = jnp.zeros_like(local_sums)
    for i, (tokens, grad, all_grads) in enumerate(
        ((image_x, image_grad, image_grads), (text_x, text_grad, text_grads))
    ):
        total = streams[i]["total"]

        def finish(span, i=i, tokens=tokens, grad=grad, all_grads=all_grads, total=total):
            pulled = total[span]
            norm, spread = normalise(tokens[span].astype(F32))
            grad_tokens = grad[span] + normalise_back(pulled * (1.0 + mod_ref[i, 1]), norm, spread)
            all_grads[tp, span] = grad_tokens.astype(BF16)
            local_sums[2 * i : 2 * i + 1] += jnp.sum(pulled, axis=0, keepdims=True)
            local_sums[2 * i + 1 : 2 * i + 2] += jnp.sum(pulled * norm, axis=0, keepdims=True)

        over_rows(total.shape[0], finish)
    wide = packed.shape[2]
    for t in range(4):
        cols = slice(t * wide, (t + 1) * wide)
        for i in range(2):
            packed[t, 6 * i : 6 * i + 2] = local_sums[2 * i : 2 * i + 2, cols]
            packed[t, 6 * i + 2 : 6 * i + 6] = sums_ref[i, 0:4, cols]
            packed[t, 12 + 5 * i : 12 + 5 * i + 5] = sums_ref[i, 4:9, cols]
        packed[t, 22:24] = jnp.zeros((2, wide), F32)
    packed_in[me] = packed[tp]
    gathers = [wires.copy(packed.at[peer % 4], packed_in.at[me], (dp, peer // 4, peer % 4)) for peer in peers]
    finals = (image_outs, text_outs, image_grads, text_grads)
    along_y = [wires.copy(final.at[tp], final.at[tp], wires.y_next) for final in finals]
    across = [wires.copy(final.at[tp], final.at[tp], wires.k_next) for final in finals]
    for arrived in gathers:
        arrived.wait_recv()
    total = packed_in[0]
    for source in range(1, 8):
        total = total + packed_in[source]
    own_sums[...] = total
    halves.wait_recv()
    for plane in planes:
        across.append(wires.copy(own_sums, packed_out.at[dp], (plane, x, tp)))
        across.append(wires.copy(both_halves, halves_out.at[dp], (plane, x, tp)))
    packed_out[dp] = total
    halves_out[dp] = both_halves[...]
    far = (1 - y) * 2 + k
    for final, arrived in zip(finals, along_y):
        arrived.wait_recv()
        across.append(wires.copy(final.at[far], final.at[far], wires.k_next))
    for arrived in across + swaps:
        arrived.wait_recv()
    wires.finish()


def leave_step(n_dp, parts, tokens, grads, outs_own, sums, mod, halves, ffn_mine, out_mine):
    width = tokens[0].shape[1]
    rows = [part.shape[0] for part in tokens]
    wide = width // 4
    outs = [jax.ShapeDtypeStruct((4, r, width), BF16) for r in rows] * 2
    outs += [
        jax.ShapeDtypeStruct((n_dp, PACKED, wide), F32),
        jax.ShapeDtypeStruct((n_dp, 2) + halves.shape, F32),
    ]
    outs += [jax.ShapeDtypeStruct((mine.shape[0] // 2, mine.shape[1]), BF16) for mine in (ffn_mine, out_mine)]
    scratch = []
    for r in rows:
        scratch += reduce_scratch(r, width)
    scratch += [
        pltpu.VMEM((4, PACKED, wide), F32),
        pltpu.VMEM((8, PACKED, wide), F32),
        pltpu.VMEM((PACKED, wide), F32),
        pltpu.VMEM((2,) + halves.shape, F32),
        pltpu.VMEM((8, width), F32),
    ]
    return comm_call(
        functools.partial(leave_kernel, n_dp),
        outs,
        scratch,
        1 + 10 + 7 + 8 + 2 * (n_dp - 1) + 6,
        3,
        "leave",
        [VMEM_SPEC] * 11 + [ANY_SPEC] * 2,
        [VMEM_SPEC] * 6 + [ANY_SPEC] * 2,
    )(*parts, *tokens, *grads, *outs_own, sums, mod, halves, ffn_mine, out_mine)


def share_kernel(part_ref, out_ref, send_sems, recv_sems):
    wires = Wires(send_sems, recv_sems)
    dp, x, tp = wires.dp, wires.x, wires.tp
    lanes = [(dp, x, lax.rem(tp + offset, 4)) for offset in range(1, 4)]
    wires.meet(lanes)
    copies = [wires.copy(part_ref, out_ref.at[tp], lane) for lane in lanes]
    out_ref[tp] = part_ref[...]
    for arrived in copies:
        arrived.wait_recv()
    wires.finish()


def share(part):
    return comm_call(
        share_kernel,
        jax.ShapeDtypeStruct((4,) + part.shape, F32),
        [],
        3,
        4,
        "share",
        [VMEM_SPEC],
        VMEM_SPEC,
    )(part)


def scatter_rows(grad):
    return lax.psum_scatter(grad, "dp", scatter_dimension=0, tiled=True)


def on_device(
    image_tokens,
    text_tokens,
    conditioning,
    ada_weight,
    ada_bias,
    qkv_weight,
    qv_bias,
    out_weight,
    out_bias,
    up_weight,
    up_bias,
    down_weight,
    down_bias,
    image_cotangent,
    text_cotangent,
):
    ctx_n, tp_n, dp_n = lax.axis_size("ctx"), lax.axis_size("tp"), lax.axis_size("dp")
    dp, ctx, tp = lax.axis_index("dp"), lax.axis_index("ctx"), lax.axis_index("tp")
    image_length, text_length, width = image_tokens.shape[1], text_tokens.shape[1], image_tokens.shape[2]
    slice_width = qkv_weight.shape[3]
    shard_rows = qkv_weight.shape[1]
    half = slice_width // ctx_n
    up_half = up_weight.shape[2] // ctx_n
    own_rows = (image_length // tp_n, TEXT_SLOTS // tp_n)
    image_all = image_length * ctx_n
    text_all = TEXT_SLOTS * ctx_n
    pad = ((0, TEXT_SLOTS - text_length), (0, 0))

    groups = dp_n if dp_n <= MOST_GROUPS else 1
    wide = 1 if groups > 1 else 2
    text_cols = up_half // groups
    text_start = ctx * up_half + (dp * text_cols if groups > 1 else 0)

    tokens = (image_tokens[0], jnp.pad(text_tokens[0], pad))
    cotangents = (image_cotangent[0], jnp.pad(text_cotangent[0], pad))

    def own(parts):
        return [lax.dynamic_slice_in_dim(part, tp * rows, rows, 0) for part, rows in zip(parts, own_rows)]

    tokens_own, cotangents_own = own(tokens), own(cotangents)
    cond_float = conditioning.astype(F32)
    activated_low = jax.nn.silu(cond_float).astype(BF16)
    partial_mod = jnp.einsum("nd,adkf->nakf", activated_low, ada_weight, preferred_element_type=F32)
    (
        mod_blocks,
        bias_blocks,
        image_blocks,
        text_blocks,
        text_gates,
        attn_full,
        ffn_mixed,
        moved,
    ) = enter(
        groups,
        partial_mod.reshape(dp_n, 12, slice_width),
        ada_bias.astype(F32).reshape(12, slice_width),
        jnp.concatenate([out_bias, down_bias], 0).astype(F32),
        *[part.reshape(tp_n, rows, width) for part, rows in zip(tokens, own_rows)],
        jnp.stack(
            [
                jnp.concatenate(
                    [qkv_weight[:, :, j, c * half : (c + 1) * half] for j in range(3)]
                    + [out_weight[:, :, c * half : (c + 1) * half]],
                    2,
                )
                for c in range(ctx_n)
            ]
        ),
        up_weight,
        down_weight,
        wide,
    )
    cotangents = (lax.optimization_barrier((cotangents[0], mod_blocks))[0], cotangents[1])
    image_other = lax.ppermute(cotangents[0], "ctx", [(0, 1), (1, 0)])
    attn_full = attn_full.reshape(2, width, 4 * half)
    ffn_blocks = [ffn_mixed.reshape(2 * wide, 2 * shard_rows, up_half)]
    around = [(i, (i + 1) % dp_n) for i in range(dp_n)]
    ffn_blocks.append(lax.ppermute(ffn_blocks[0], "dp", around))
    modulation = mod_blocks.transpose(1, 0, 2).reshape(2, 6, width)
    biases = bias_blocks.transpose(1, 0, 2).reshape(4, width)
    mod_rows = modulation[:, :, None]
    out_bias_rows, down_bias_rows = biases[:2, None], biases[2:, None]
    tokens_all = (image_blocks.reshape(image_all, width), text_blocks.reshape(text_all, width))
    qv_own = lax.dynamic_slice_in_dim(qv_bias, ctx * half, half, 2).astype(F32)
    up_bias_own = (
        lax.dynamic_slice_in_dim(up_bias[0], ctx * up_half, up_half, 0).astype(F32),
        lax.dynamic_slice_in_dim(up_bias[1], text_start, text_cols, 0).astype(F32),
    )
    slots = tp * own_rows[1] + lax.broadcasted_iota(jnp.int32, (own_rows[1], 1), 0)
    valid = jnp.broadcast_to((slots < text_length).astype(F32), (own_rows[1], width))

    own_ctx = jnp.full((1,), ctx, jnp.int32)

    def other_half(part):
        return lax.ppermute(part, "ctx", [(0, 1), (1, 0)])

    def blocks(part):
        return part.reshape(2, 2, 2, part.shape[0] // 8, width)

    qv_bias_rows = jnp.concatenate([qv_own[:, 0], jnp.zeros((2, half), F32), qv_own[:, 1]], 1)[:, None]
    normed_low, queries, keys, values, out_full = project(
        *tokens_all, mod_rows[:, :2], attn_full, qv_bias_rows
    )
    queries, ffn_blocks[1] = lax.optimization_barrier((queries, ffn_blocks[1]))
    for _ in range(dp_n - 3):
        ffn_blocks.append(lax.ppermute(ffn_blocks[-1], "dp", around))
    blended, lse, *out_parts = attend_forward(queries, keys, values, out_full, text_all, text_length)
    out_parts = [blocks(part) for part in out_parts]
    *attentions_middles, image_second, text_second, text_cots, moved_in, ffn_full = middle_step(
        groups, *out_parts, *tokens_own, mod_rows, out_bias_rows, moved, ffn_blocks, cotangents_own[1]
    )
    ffn_full = ffn_full.reshape(2 * wide, width, up_half)
    attentions, middles = attentions_middles[:2], attentions_middles[2:]
    second_low = (image_second.reshape(-1, width), text_second.reshape(-1, width))

    up_full, down_full = [(ffn_full, 0)], [(ffn_full, wide)]
    if groups > 1:
        moved_in = moved_in.reshape(width, 2 * text_cols)
        up_full.append((moved_in[None, :, :text_cols], 0))
        down_full.append((moved_in[None, :, text_cols:], 0))
        text_feed = (text_cots.reshape(-1, width), None, text_gates.reshape(groups, width))
    else:
        up_full.append((ffn_full, 1))
        down_full.append((ffn_full, 3))
        text_feed = (cotangents[1], other_half(cotangents[1]), mod_rows[1, 5])
    arrivals = ((cotangents[0], image_other, mod_rows[0, 5]), text_feed)
    feed_parts, second_parts, ffn_grads, up_bias_grads = [], [], [], []
    for stream in range(2):
        feed, pulled, grads, sums = feed_forward(
            own_ctx, second_low[stream], *arrivals[stream], up_full[stream], down_full[stream], up_bias_own[stream]
        )
        feed_parts.append(blocks(feed))
        second_parts.append(blocks(pulled))
        ffn_grads.append(grads)
        up_bias_grads.append(sums[0])
    if groups > 1:
        ffn_mine = scatter_rows(ffn_grads[0])
        moved = ffn_grads[1].reshape(dp_n * ctx_n, shard_rows, 2 * text_cols)
    else:
        ffn_mine = scatter_rows(jnp.concatenate(ffn_grads, 1))
    image_out, text_out, image_middle_grad, text_middle_grad, sums, image_attn, text_attn, moved_in = turn_step(
        groups, valid, feed_parts, second_parts, attentions, middles, cotangents_own, mod_rows, down_bias_rows, moved
    )
    attention_grad_all = (image_attn.reshape(-1, width), text_attn.reshape(-1, width))
    out_weight_grads = out_gradient(*attention_grad_all, blended)
    out_weight_grads, ffn_mine = lax.optimization_barrier((out_weight_grads, ffn_mine))
    out_mine = scatter_rows(out_weight_grads)
    grad_queries, grad_keys, grad_values = attend_backward(
        queries, keys, values, lse, *attention_grad_all, out_full, text_length
    )
    *normed_parts, qkv_weight_grads, joint_sums = unproject(
        grad_queries, grad_keys, grad_values, normed_low, attn_full, text_all
    )
    normed_parts = [blocks(part) for part in normed_parts]
    qkv_weight_grads, out_mine = lax.optimization_barrier((qkv_weight_grads, out_mine))
    qkv_mine = scatter_rows(qkv_weight_grads)

    def given(mine):
        return lax.dynamic_slice_in_dim(mine, (1 - ctx) * shard_rows, shard_rows, 0)

    qv_bias_grads = [
        jnp.concatenate([joint_sums[stream, 0, :half], joint_sums[stream, 0, 2 * half :]]) for stream in range(2)
    ]
    qkv_weight_grad = place_qkv(own_ctx, qkv_mine, other_half(given(qkv_mine)))
    if groups > 1:
        up_bias_grads[1] = lax.dynamic_update_slice_in_dim(
            jnp.zeros((up_half,), F32), up_bias_grads[1], dp * text_cols, 0
        )
    halves = jnp.concatenate(
        [part.reshape(-1, slice_width) for part in (*qv_bias_grads, *up_bias_grads)], 0
    )
    image_outs, text_outs, image_grads, text_grads, packed, halves_all, ffn_other, out_other = leave_step(
        dp_n,
        normed_parts,
        tokens_own,
        (image_middle_grad, text_middle_grad),
        (image_out, text_out),
        sums,
        mod_rows,
        halves,
        ffn_mine,
        out_mine,
    )
    out_weight_grad = place_out(own_ctx, out_mine, out_other)
    if groups > 1:
        up_weight_grad, down_weight_grad = place_feed(own_ctx, ffn_mine, ffn_other, moved_in)
    else:
        kept, other = lax.dynamic_slice_in_dim(ffn_mine, ctx * shard_rows, shard_rows, 0), ffn_other
        ffn_halves = [jnp.where(ctx == c, kept, other).astype(F32) for c in range(2)]
        up_weight_grad, down_weight_grad = [
            jnp.stack(
                [
                    jnp.concatenate([part[:, c * up_half : (c + 1) * up_half] for part in ffn_halves], 1)
                    for c in (i, 2 + i)
                ]
            )
            for i in range(2)
        ]
    grad_mod_low = packed[:, :12].astype(BF16)
    ada_bias_grad = jnp.sum(grad_mod_low.astype(F32), axis=0).reshape(2, 6, slice_width)
    grad_mod_low = grad_mod_low.reshape(dp_n, 2, 6, slice_width)
    ada_weight_grad = jnp.einsum("nd,nakf->adkf", activated_low, grad_mod_low, preferred_element_type=F32)
    cond_partial = jnp.einsum("nakf,adkf->nd", grad_mod_low, ada_weight, preferred_element_type=F32)
    totals = jnp.sum(packed[:, 12:22], axis=0)
    cond_rows = jnp.pad(cond_partial, ((0, -dp_n % 2), (0, slice_width - shard_rows)))
    shared = share(jnp.concatenate([totals, cond_rows], 0))
    cond_total = jnp.sum(shared[:, 10 : 10 + dp_n, :shard_rows], axis=0)
    cond_grad = jax.vjp(jax.nn.silu, cond_float)[1](cond_total)[0]
    full = shared[:, :10].transpose(1, 0, 2).reshape(2, 5, width)
    bias_grads = lax.dynamic_slice_in_dim(full[:, :2], (dp * ctx_n + ctx) * shard_rows, shard_rows, 2)
    squares_total = jnp.sum(full[:, 2:], axis=2).T.reshape(6)
    counts = jnp.array([image_length, text_length] * 3, F32) * (dp_n * ctx_n * width)
    root_means = jnp.sqrt(squares_total / counts)
    half_sums = jnp.sum(halves_all, axis=0)
    qv_rows = half * 2 // slice_width
    up_rows = up_half // slice_width
    qv_bias_grad = (
        half_sums[:, : 2 * qv_rows].reshape(ctx_n, 2, 2, half).transpose(1, 2, 0, 3).reshape(2, 2, slice_width)
    )
    up_bias_grad = (
        half_sums[:, 2 * qv_rows : 2 * (qv_rows + up_rows)]
        .reshape(ctx_n, 2, up_half)
        .transpose(1, 0, 2)
        .reshape(2, ctx_n * up_half)
    )
    return (
        image_outs.reshape(1, image_length, width),
        text_outs.reshape(1, TEXT_SLOTS, width)[:, :text_length],
        image_grads.reshape(1, image_length, width),
        text_grads.reshape(1, TEXT_SLOTS, width)[:, :text_length],
        cond_grad,
        ada_weight_grad,
        ada_bias_grad,
        qkv_weight_grad,
        qv_bias_grad,
        out_weight_grad,
        bias_grads[:, 1],
        up_weight_grad,
        up_bias_grad,
        down_weight_grad,
        bias_grads[:, 0],
        root_means,
    )


def solution(mesh):
    rows = P(None, ("dp", "ctx"))
    tokens = P("dp", "ctx", None)
    stacked = P(None, ("dp", "ctx"), None, "tp")
    matrix = P(None, ("dp", "ctx"), "tp")
    return jax.shard_map(
        on_device,
        mesh=mesh,
        in_specs=(
            tokens,
            tokens,
            rows,
            stacked,
            P(None, None, "tp"),
            stacked,
            P(None, None, "tp"),
            matrix,
            rows,
            matrix,
            P(None, "tp"),
            matrix,
            rows,
            tokens,
            tokens,
        ),
        out_specs=(
            tokens,
            tokens,
            tokens,
            tokens,
            rows,
            stacked,
            P(None, None, "tp"),
            stacked,
            P(None, None, "tp"),
            matrix,
            rows,
            matrix,
            P(None, "tp"),
            matrix,
            rows,
            P(),
        ),
        check_vma=False,
    )
```

```python
import functools

import jax
import jax.numpy as jnp
from jax import lax
from jax.experimental import pallas as pl
from jax.experimental.pallas import tpu as pltpu
from jax.sharding import PartitionSpec as P

HEAD_DIM = 64
F32 = jnp.float32
BF16 = jnp.bfloat16
VMEM_LIMIT = 60 * 1024 * 1024
PLANE = ("ctx", "tp")
TEXT_SLOTS = 96
MOST_GROUPS = 4
QUERY_BLOCK = 256


def dot(left, right, dims=((1,), (0,))):
    return lax.dot_general(left, right, (dims, ((), ())), preferred_element_type=F32)


def local_call(kernel, steps, in_specs, outs, scratch, flops, name):
    return pl.pallas_call(
        kernel,
        grid=(steps,),
        in_specs=in_specs,
        out_specs=[spec for spec, _ in outs],
        out_shape=[shape for _, shape in outs],
        scratch_shapes=scratch,
        compiler_params=pltpu.CompilerParams(vmem_limit_bytes=VMEM_LIMIT),
        cost_estimate=pl.CostEstimate(flops=flops, bytes_accessed=flops // 256, transcendentals=0),
        name=name,
    )


def fixed(shape):
    return pl.BlockSpec(shape, lambda i: (0,) * len(shape), pipeline_mode=pl.Buffered(1))


def stepped(shape):
    return pl.BlockSpec(shape, lambda i: (i,) + (0,) * (len(shape) - 1))


def image_block(shape, last):
    return pl.BlockSpec(shape, lambda i: (jnp.minimum(i, last),) + (0,) * (len(shape) - 1))


def stream_block(shape, steps):
    return pl.BlockSpec(shape, lambda i: (i // steps,) + (0,) * (len(shape) - 1))


def padded(text):
    return jnp.concatenate([text, jnp.zeros((QUERY_BLOCK - text.shape[0], text.shape[1]), text.dtype)], 0)


def by_stream(steps, image_ref, text_ref, body):
    step = pl.program_id(0)

    @pl.when(step < steps)
    def _():
        body(image_ref[...], 0)

    @pl.when(step >= steps)
    def _():
        body(padded(text_ref[...]), 1)


def project_kernel(steps, image_ref, text_ref, mod_ref, weight_ref, bias_ref, normed_ref, q_ref, k_ref, v_ref, out_ref):
    half = q_ref.shape[1]

    def body(tokens, stream):
        norm, _ = normalise(tokens.astype(F32))
        normed = (norm * (1.0 + mod_ref[0, 1]) + mod_ref[0, 0]).astype(BF16)
        normed_ref[...] = normed
        joint = dot(normed, weight_ref[0, :, : 3 * half]) + bias_ref[0]
        q_ref[...] = joint[:, :half].astype(BF16)
        k_ref[...] = joint[:, half : 2 * half].astype(BF16)
        v_ref[...] = joint[:, 2 * half :].astype(BF16)

    by_stream(steps, image_ref, text_ref, body)

    @pl.when(lax.rem(pl.program_id(0), steps) == 0)
    def _():
        out_ref[0] = weight_ref[0, :, 3 * half :]


def project(image, text, mod, weight, bias):
    (rows, width), wide = image.shape, weight.shape[2]
    steps, half = rows // QUERY_BLOCK, wide // 4
    joint = rows + QUERY_BLOCK
    heads = [(stepped((QUERY_BLOCK, half)), jax.ShapeDtypeStruct((joint, half), BF16))] * 3
    return local_call(
        functools.partial(project_kernel, steps),
        steps + 1,
        [
            image_block((QUERY_BLOCK, width), steps - 1),
            fixed(text.shape),
            stream_block((1,) + mod.shape[1:], steps),
            stream_block((1,) + weight.shape[1:], steps),
            stream_block((1,) + bias.shape[1:], steps),
        ],
        [(stepped((QUERY_BLOCK, width)), jax.ShapeDtypeStruct((joint, width), BF16))]
        + heads
        + [(stream_block((1, width, half), steps), jax.ShapeDtypeStruct((2, width, half), BF16))],
        [],
        6 * joint * width * half,
        "project",
    )(image, text, mod, weight, bias)


def key_bias(rows, image_rows, text_rows):
    slot = lax.broadcasted_iota(jnp.int32, (rows, 1), 0)
    text_slot = slot - image_rows
    unused = jnp.logical_or(lax.rem(text_slot, TEXT_SLOTS) >= text_rows, text_slot >= 2 * TEXT_SLOTS)
    masked = jnp.logical_and(text_slot >= 0, unused)
    return jnp.where(masked, -1e30, 0.0).astype(F32)


def attend_forward_kernel(
    steps, heads, text_rows, q_ref, k_ref, v_ref, weight_ref, o_ref, lse_ref, image_ref, text_ref, vt_ref
):
    step = pl.program_id(0)

    @pl.when(step == 0)
    def _():
        vt_ref[...] = v_ref[...].T

    rows = k_ref.shape[0]
    bias = key_bias(rows, steps * QUERY_BLOCK, text_rows)
    queries_t = (q_ref[...] * HEAD_DIM ** (-0.5)).T
    outs = []
    for head in range(heads):
        span = slice(head * HEAD_DIM, (head + 1) * HEAD_DIM)
        scores = dot(k_ref[:, span], queries_t[span]) + bias
        top = jnp.max(scores, axis=0, keepdims=True)
        grown = jnp.exp(scores - top)
        total = jnp.sum(grown, axis=0, keepdims=True)
        lse_ref[head : head + 1] = top + jnp.log(total)
        outs.append(dot(vt_ref[span], grown.astype(BF16)) * (1.0 / total))
    blended = jnp.concatenate(outs, 0).T.astype(BF16)
    o_ref[...] = blended
    branch = dot(blended, weight_ref[0], ((1,), (1,))).astype(BF16)

    @pl.when(step < steps)
    def _():
        image_ref[...] = branch

    @pl.when(step >= steps)
    def _():
        text_ref[...] = branch[: text_ref.shape[0]]


def attend_forward(q, k, v, weight, text_all, text_rows):
    rows, wide = q.shape
    width = weight.shape[1]
    heads = wide // HEAD_DIM
    steps = rows // QUERY_BLOCK - 1
    return local_call(
        functools.partial(attend_forward_kernel, steps, heads, text_rows),
        steps + 1,
        [
            stepped((QUERY_BLOCK, wide)),
            fixed((rows, wide)),
            fixed((rows, wide)),
            stream_block((1, width, wide), steps),
        ],
        [
            (stepped((QUERY_BLOCK, wide)), jax.ShapeDtypeStruct((rows, wide), BF16)),
            (pl.BlockSpec((heads, QUERY_BLOCK), lambda i: (0, i)), jax.ShapeDtypeStruct((heads, rows), F32)),
            (image_block((QUERY_BLOCK, width), steps - 1), jax.ShapeDtypeStruct((steps * QUERY_BLOCK, width), BF16)),
            (pl.BlockSpec((text_all, width), lambda i: (0, 0)), jax.ShapeDtypeStruct((text_all, width), BF16)),
        ],
        [pltpu.VMEM((wide, rows), BF16)],
        4 * rows * rows * wide,
        "attend_forward",
    )(q, k, v, weight)


def out_gradient_kernel(steps, image_ref, text_ref, o_ref, dw_ref, dw_sum):
    step = pl.program_id(0)
    wide = o_ref.shape[1]

    @pl.when(step == 0)
    def _():
        dw_sum[...] = jnp.zeros_like(dw_sum)

    def add(arriving, stream):
        dw_sum[stream] += dot(arriving, o_ref[...], ((0,), (0,)))

    by_stream(steps, image_ref, text_ref, add)

    @pl.when(step == steps)
    def _():
        for stream in range(2):
            dw_ref[:, stream * wide : (stream + 1) * wide] = dw_sum[stream].astype(BF16)


def out_gradient(image, text, blended):
    rows, wide = blended.shape
    width = image.shape[1]
    steps = rows // QUERY_BLOCK - 1
    return local_call(
        functools.partial(out_gradient_kernel, steps),
        steps + 1,
        [image_block((QUERY_BLOCK, width), steps - 1), fixed(text.shape), stepped((QUERY_BLOCK, wide))],
        [(pl.BlockSpec((width, 2 * wide), lambda i: (0, 0)), jax.ShapeDtypeStruct((width, 2 * wide), BF16))],
        [pltpu.VMEM((2, width, wide), F32)],
        2 * rows * width * wide,
        "out_gradient",
    )(image, text, blended)[0]


def attend_backward_kernel(
    steps,
    heads,
    text_rows,
    q_ref,
    k_ref,
    v_ref,
    lse_ref,
    image_ref,
    text_ref,
    weight_ref,
    dq_ref,
    dk_ref,
    dv_ref,
    kt_ref,
    g_ref,
    dk_sum,
    dv_sum,
):
    step = pl.program_id(0)

    @pl.when(step == 0)
    def _():
        kt_ref[...] = k_ref[...].T
        dk_sum[...] = jnp.zeros_like(dk_sum)
        dv_sum[...] = jnp.zeros_like(dv_sum)

    def bring(arriving, stream):
        g_ref[...] = dot(arriving, weight_ref[0]).astype(BF16)

    by_stream(steps, image_ref, text_ref, bring)
    rows = k_ref.shape[0]
    bias = key_bias(rows, steps * QUERY_BLOCK, text_rows)
    queries = q_ref[...] * HEAD_DIM ** (-0.5)
    queries_t = queries.T
    grads = g_ref[...]
    grads_t = grads.T
    outs = []
    for head in range(heads):
        span = slice(head * HEAD_DIM, (head + 1) * HEAD_DIM)
        scores = dot(k_ref[:, span], queries_t[span]) + bias
        prob = jnp.exp(scores - lse_ref[head : head + 1])
        grad_prob = dot(v_ref[:, span], grads_t[span])
        weighted = prob * grad_prob
        inner = jnp.sum(weighted, axis=0, keepdims=True)
        grad_score = (weighted - prob * inner).astype(BF16)
        dv_sum[head] += dot(prob.astype(BF16), grads[:, span])
        dk_sum[head] += dot(grad_score, queries[:, span])
        outs.append(dot(kt_ref[span], grad_score) * HEAD_DIM ** (-0.5))
    dq_ref[...] = jnp.concatenate(outs, 0).T.astype(BF16)

    @pl.when(step == steps)
    def _():
        dk_ref[...] = jnp.concatenate([dk_sum[head] for head in range(heads)], 1).astype(BF16)
        dv_ref[...] = jnp.concatenate([dv_sum[head] for head in range(heads)], 1).astype(BF16)


def attend_backward(q, k, v, lse, image, text, weight, text_rows):
    rows, wide = q.shape
    width = weight.shape[1]
    heads = wide // HEAD_DIM
    steps = rows // QUERY_BLOCK - 1
    block = stepped((QUERY_BLOCK, wide))
    whole = pl.BlockSpec((rows, wide), lambda i: (0, 0))
    return local_call(
        functools.partial(attend_backward_kernel, steps, heads, text_rows),
        steps + 1,
        [
            block,
            fixed((rows, wide)),
            fixed((rows, wide)),
            pl.BlockSpec((heads, QUERY_BLOCK), lambda i: (0, i)),
            image_block((QUERY_BLOCK, width), steps - 1),
            fixed(text.shape),
            stream_block((1, width, wide), steps),
        ],
        [
            (block, jax.ShapeDtypeStruct((rows, wide), BF16)),
            (whole, jax.ShapeDtypeStruct((rows, wide), BF16)),
            (whole, jax.ShapeDtypeStruct((rows, wide), BF16)),
        ],
        [
            pltpu.VMEM((wide, rows), BF16),
            pltpu.VMEM((QUERY_BLOCK, wide), BF16),
            pltpu.VMEM((heads, rows, HEAD_DIM), F32),
            pltpu.VMEM((heads, rows, HEAD_DIM), F32),
        ],
        10 * rows * rows * wide,
        "attend_backward",
    )(q, k, v, lse, image, text, weight)


def unproject_kernel(
    steps, dq_ref, dk_ref, dv_ref, normed_ref, weight_ref, image_ref, text_ref, dw_ref, sums_ref, dw_sum
):
    step = pl.program_id(0)
    half = dq_ref.shape[1]
    stream = step // steps

    @pl.when(step == 0)
    def _():
        dw_sum[...] = jnp.zeros_like(dw_sum)
        sums_ref[...] = jnp.zeros_like(sums_ref)

    grads = jnp.concatenate([dq_ref[...], dk_ref[...], dv_ref[...]], 1)
    part = dot(grads, weight_ref[0, :, : 3 * half], ((1,), (1,))).astype(BF16)
    dw_sum[stream] += dot(normed_ref[...], grads, ((0,), (0,)))
    sums_ref[stream] += jnp.sum(grads.astype(F32), axis=0, keepdims=True)

    @pl.when(step < steps)
    def _():
        image_ref[...] = part

    @pl.when(step == steps)
    def _():
        text_ref[...] = part[: text_ref.shape[0]]
        for s in range(2):
            dw_ref[:, s * 3 * half : (s + 1) * 3 * half] = dw_sum[s].astype(BF16)


def unproject(dq, dk, dv, normed, weight, text_all):
    rows, half = dq.shape
    width = normed.shape[1]
    steps = rows // QUERY_BLOCK - 1
    block = stepped((QUERY_BLOCK, half))
    return local_call(
        functools.partial(unproject_kernel, steps),
        steps + 1,
        [
            block,
            block,
            block,
            stepped((QUERY_BLOCK, width)),
            stream_block((1,) + weight.shape[1:], steps),
        ],
        [
            (image_block((QUERY_BLOCK, width), steps - 1), jax.ShapeDtypeStruct((steps * QUERY_BLOCK, width), BF16)),
            (pl.BlockSpec((text_all, width), lambda i: (0, 0)), jax.ShapeDtypeStruct((text_all, width), BF16)),
            (pl.BlockSpec((width, 6 * half), lambda i: (0, 0)), jax.ShapeDtypeStruct((width, 6 * half), BF16)),
            (pl.BlockSpec((2, 1, 3 * half), lambda i: (0, 0, 0)), jax.ShapeDtypeStruct((2, 1, 3 * half), F32)),
        ],
        [pltpu.VMEM((2, width, 3 * half), F32)],
        12 * rows * width * half,
        "unproject",
    )(dq, dk, dv, normed, weight)


def feed_kernel(
    halves,
    ctx_ref,
    second_ref,
    cot_ref,
    other_ref,
    gate_ref,
    up_ref,
    down_ref,
    bias_ref,
    feed_ref,
    pull_ref,
    dw_ref,
    sums_ref,
    up_sum,
    down_sum,
    gate_rows,
):
    step = pl.program_id(0)
    wide = up_ref.shape[1]

    @pl.when(step == 0)
    def _():
        up_sum[...] = jnp.zeros_like(up_sum)
        down_sum[...] = jnp.zeros_like(down_sum)
        sums_ref[...] = jnp.zeros_like(sums_ref)
        groups = gate_ref.shape[0]
        if halves:
            gate_rows[...] = gate_ref[...]
        else:
            rows = gate_rows.shape[0] // (2 * groups)
            for block in range(2 * groups):
                gate = gate_ref[block % groups : block % groups + 1]
                gate_rows[block * rows : (block + 1) * rows] = jnp.broadcast_to(gate, (rows, gate.shape[1]))

    arriving = cot_ref[...]
    if halves:
        arriving = jnp.where(step // halves == ctx_ref[0], arriving, other_ref[...])
    arriving = (arriving.astype(F32) * gate_rows[...]).astype(BF16)
    second = second_ref[...]
    hidden = dot(second, up_ref[...]) + bias_ref[...]
    gelu_out, slope = gelu_parts(hidden)
    gelu_low = gelu_out.astype(BF16)
    feed_ref[...] = dot(gelu_low, down_ref[...], ((1,), (1,))).astype(BF16)
    down_sum[...] += dot(arriving, gelu_low, ((0,), (0,)))
    pulled = (dot(arriving, down_ref[...]) * slope).astype(BF16)
    sums_ref[...] += jnp.sum(pulled.astype(F32), axis=0, keepdims=True)
    up_sum[...] += dot(second, pulled, ((0,), (0,)))
    pull_ref[...] = dot(pulled, up_ref[...], ((1,), (1,))).astype(BF16)

    @pl.when(step == pl.num_programs(0) - 1)
    def _():
        dw_ref[:, :wide] = up_sum[...].astype(BF16)
        dw_ref[:, wide:] = down_sum[...].astype(BF16)


def feed_forward(ctx, second, cot, other, gate, up, down, bias):
    (up, up_at), (down, down_at) = up, down
    (rows, width), wide, groups = second.shape, up.shape[2], gate.shape[0]
    if other is None:
        block_rows, halves, gate_rows = 2 * TEXT_SLOTS // 4 * groups, 0, 2 * TEXT_SLOTS // 4 * groups
        other, last = cot[:8], 0
        cot_spec = pl.BlockSpec((block_rows, width), lambda i, c: (i, 0))
        other_spec = pl.BlockSpec((8, width), lambda i, c: (0, 0))
    else:
        block_rows = min(QUERY_BLOCK, cot.shape[0])
        halves, gate_rows = cot.shape[0] // block_rows, 1
        last = halves - 1
        cot_spec = pl.BlockSpec((block_rows, width), lambda i, c: (jnp.clip(i - c[0] * halves, 0, last), 0))
        other_spec = pl.BlockSpec((block_rows, width), lambda i, c: (jnp.clip(i - (1 - c[0]) * halves, 0, last), 0))
    block = pl.BlockSpec((block_rows, width), lambda i, c: (i, 0))

    def once(shape):
        return pl.BlockSpec(shape, lambda i, c: (0, 0), pipeline_mode=pl.Buffered(1))

    flops = 12 * rows * width * wide
    return pl.pallas_call(
        functools.partial(feed_kernel, halves),
        grid_spec=pltpu.PrefetchScalarGridSpec(
            num_scalar_prefetch=1,
            grid=(rows // block_rows,),
            in_specs=[
                block,
                cot_spec,
                other_spec,
                once(gate.shape),
                pl.BlockSpec(
                    (None,) + up.shape[1:], lambda i, c: (up_at, 0, 0), pipeline_mode=pl.Buffered(1)
                ),
                pl.BlockSpec(
                    (None,) + down.shape[1:], lambda i, c: (down_at, 0, 0), pipeline_mode=pl.Buffered(1)
                ),
                once((1, wide)),
            ],
            out_specs=[
                block,
                block,
                pl.BlockSpec((width, 2 * wide), lambda i, c: (0, 0)),
                pl.BlockSpec((1, wide), lambda i, c: (0, 0)),
            ],
            scratch_shapes=[pltpu.VMEM((width, wide), F32)] * 2 + [pltpu.VMEM((gate_rows, width), F32)],
        ),
        out_shape=[
            jax.ShapeDtypeStruct((rows, width), BF16),
            jax.ShapeDtypeStruct((rows, width), BF16),
            jax.ShapeDtypeStruct((width, 2 * wide), BF16),
            jax.ShapeDtypeStruct((1, wide), F32),
        ],
        compiler_params=pltpu.CompilerParams(vmem_limit_bytes=VMEM_LIMIT),
        cost_estimate=pl.CostEstimate(flops=flops, bytes_accessed=flops // 256, transcendentals=0),
        name="feed_forward",
    )(ctx, second, cot, other, gate, up, down, bias.reshape(1, wide))


def feed_moving_kernel(
    groups,
    halves,
    second_ref,
    own_ref,
    other_ref,
    gate_ref,
    up_ref,
    down_ref,
    bias_ref,
    moved_ref,
    feed_ref,
    pull_ref,
    dw_ref,
    sums_ref,
    moved_out,
    up_sum,
    down_sum,
    local_sem,
    send_sems,
    recv_sems,
):
    step = pl.program_id(0)
    dp, x, tp = lax.axis_index("dp"), lax.axis_index("ctx"), lax.axis_index("tp")
    wide = up_ref.shape[1]
    block_rows = second_ref.shape[0]
    count = groups * 2
    me = dp * 2 + x
    peers = [lax.rem(me + offset, count) for offset in range(1, count)]
    devices = [(peer // 2, peer % 2, tp) for peer in peers]
    local = pltpu.make_async_copy(moved_ref.at[me], moved_out.at[me], local_sem)
    moves = [
        pltpu.make_async_remote_copy(
            src_ref=moved_ref.at[peer],
            dst_ref=moved_out.at[me],
            send_sem=send_sems.at[i],
            recv_sem=recv_sems.at[i],
            device_id=device,
            device_id_type=MESH,
        )
        for i, (peer, device) in enumerate(zip(peers, devices))
    ]

    @pl.when(step == 0)
    def _():
        barrier = pltpu.get_barrier_semaphore()
        for device in devices:
            pl.semaphore_signal(barrier, inc=1, device_id=device, device_id_type=MESH)
        pl.semaphore_wait(barrier, len(devices))
        local.start()
        for move in moves:
            move.start()
        up_sum[...] = jnp.zeros_like(up_sum)
        down_sum[...] = jnp.zeros_like(down_sum)
        sums_ref[...] = jnp.zeros_like(sums_ref)

    rows = pl.ds(pl.multiple_of(lax.rem(step, halves) * block_rows, block_rows), block_rows)
    arriving = jnp.where(step // halves == x, own_ref[rows], other_ref[rows])
    arriving = (arriving.astype(F32) * gate_ref[...]).astype(BF16)
    second = second_ref[...]
    hidden = dot(second, up_ref[...]) + bias_ref[...]
    gelu_out, slope = gelu_parts(hidden)
    gelu_low = gelu_out.astype(BF16)
    feed_ref[...] = dot(gelu_low, down_ref[...], ((1,), (1,))).astype(BF16)
    down_sum[...] += dot(arriving, gelu_low, ((0,), (0,)))
    pulled = (dot(arriving, down_ref[...]) * slope).astype(BF16)
    sums_ref[...] += jnp.sum(pulled.astype(F32), axis=0, keepdims=True)
    up_sum[...] += dot(second, pulled, ((0,), (0,)))
    pull_ref[...] = dot(pulled, up_ref[...], ((1,), (1,))).astype(BF16)

    @pl.when(step == pl.num_programs(0) - 1)
    def _():
        dw_ref[:, :wide] = up_sum[...].astype(BF16)
        dw_ref[:, wide:] = down_sum[...].astype(BF16)
        local.wait()
        for move in moves:
            move.wait()


def feed_forward_moving(groups, second, own, other, gate, up, down, bias, moved):
    (up, up_at), (down, down_at) = up, down
    (rows, width), wide = second.shape, up.shape[2]
    block_rows = min(QUERY_BLOCK, own.shape[0])
    block = stepped((block_rows, width))
    peers = 2 * groups - 1

    def weight(shape, place):
        return pl.BlockSpec((None,) + shape[1:], lambda i: (place, 0, 0), pipeline_mode=pl.Buffered(1))

    return pl.pallas_call(
        functools.partial(feed_moving_kernel, groups, own.shape[0] // block_rows),
        grid=(rows // block_rows,),
        in_specs=[
            block,
            fixed(own.shape),
            fixed(other.shape),
            fixed(gate.shape),
            weight(up.shape, up_at),
            weight(down.shape, down_at),
            fixed((1, wide)),
            pl.BlockSpec(memory_space=pl.ANY),
        ],
        out_specs=[
            block,
            block,
            pl.BlockSpec((width, 2 * wide), lambda i: (0, 0)),
            pl.BlockSpec((1, wide), lambda i: (0, 0)),
            pl.BlockSpec(memory_space=pl.ANY),
        ],
        out_shape=[
            jax.ShapeDtypeStruct((rows, width), BF16),
            jax.ShapeDtypeStruct((rows, width), BF16),
            jax.ShapeDtypeStruct((width, 2 * wide), BF16),
            jax.ShapeDtypeStruct((1, wide), F32),
            jax.ShapeDtypeStruct(moved.shape, BF16),
        ],
        scratch_shapes=[pltpu.VMEM((width, wide), F32)] * 2
        + [
            pltpu.SemaphoreType.DMA(()),
            pltpu.SemaphoreType.DMA((peers,)),
            pltpu.SemaphoreType.DMA((peers,)),
        ],
        compiler_params=pltpu.CompilerParams(
            collective_id=5, has_side_effects=True, vmem_limit_bytes=VMEM_LIMIT
        ),
        name="feed_moving",
    )(second, own, other, gate, up, down, bias.reshape(1, wide), moved)


def place_feed_kernel(ctx_ref, mine_ref, other_ref, moved_ref, up_ref, down_ref):
    ctx = ctx_ref[0]
    cols = mine_ref.shape[2] // 2
    text_cols = moved_ref.shape[2] // 2
    groups = moved_ref.shape[0] // 2

    def place(span):
        kept, other = mine_ref[ctx, span], other_ref[span]
        for c in range(2):
            part = jnp.where(ctx == c, kept, other).astype(F32)
            up_ref[0, span, c * cols : (c + 1) * cols] = part[:, :cols]
            down_ref[0, span, c * cols : (c + 1) * cols] = part[:, cols:]
            for group in range(groups):
                start = c * cols + group * text_cols
                text = moved_ref[group * 2 + c, span].astype(F32)
                up_ref[1, span, start : start + text_cols] = text[:, :text_cols]
                down_ref[1, span, start : start + text_cols] = text[:, text_cols:]

    over_rows(other_ref.shape[0], place)


def place_feed(ctx, mine, other, moved):
    rows, cols = other.shape
    shape = jax.ShapeDtypeStruct((2, rows, cols), F32)
    return pl.pallas_call(
        place_feed_kernel,
        in_specs=[pl.BlockSpec(memory_space=pltpu.SMEM)] + [pl.BlockSpec(memory_space=pltpu.VMEM)] * 3,
        out_specs=[pl.BlockSpec(memory_space=pltpu.VMEM)] * 2,
        out_shape=[shape, shape],
        compiler_params=pltpu.CompilerParams(vmem_limit_bytes=VMEM_LIMIT),
        name="place_feed",
    )(ctx, mine.reshape(2, rows, cols), other, moved)


def place_tokens_kernel(image_out, text_out, image_grad, text_grad, *outs):
    for source, place in zip((image_out, image_grad), outs[::2]):
        rows = source.shape[1]
        for block in range(source.shape[0]):
            place[0, block * rows : (block + 1) * rows] = source[block]
    for source, place in zip((text_out, text_grad), outs[1::2]):
        rows, length = source.shape[1], place.shape[1]
        for block in range(source.shape[0]):
            used = min(rows, length - block * rows)
            place[0, block * rows : block * rows + used] = source[block, :used]


def place_tokens(parts, image_length, text_length):
    shapes = [
        jax.ShapeDtypeStruct((1, length, parts[0].shape[2]), BF16) for length in (image_length, text_length) * 2
    ]
    return pl.pallas_call(
        place_tokens_kernel,
        in_specs=[pl.BlockSpec(memory_space=pltpu.VMEM)] * 4,
        out_specs=[pl.BlockSpec(memory_space=pltpu.VMEM)] * 4,
        out_shape=shapes,
        compiler_params=pltpu.CompilerParams(vmem_limit_bytes=VMEM_LIMIT),
        name="place_tokens",
    )(*parts)


def place_heads_kernel(kinds, ctx_ref, mine_ref, other_ref, out_ref):
    ctx = ctx_ref[0]
    half = out_ref.shape[3] // 2

    def place(span):
        kept, other = mine_ref[ctx, span], other_ref[span]
        for c in range(2):
            part = jnp.where(ctx == c, kept, other).astype(F32)
            for s in range(2):
                for j in range(kinds):
                    start = (kinds * s + j) * half
                    out_ref[s, j, span, c * half : (c + 1) * half] = part[:, start : start + half]

    over_rows(other_ref.shape[0], place)


def place_heads(kinds, ctx, mine, other):
    rows, cols = other.shape
    return pl.pallas_call(
        functools.partial(place_heads_kernel, kinds),
        in_specs=[pl.BlockSpec(memory_space=pltpu.SMEM)] + [pl.BlockSpec(memory_space=pltpu.VMEM)] * 2,
        out_specs=pl.BlockSpec(memory_space=pltpu.VMEM),
        out_shape=jax.ShapeDtypeStruct((2, kinds, rows, cols // kinds), F32),
        compiler_params=pltpu.CompilerParams(vmem_limit_bytes=VMEM_LIMIT),
        name="place_heads",
    )(ctx, mine.reshape(2, rows, cols), other)


def place_qkv(ctx, mine, other):
    return place_heads(3, ctx, mine, other).transpose(0, 2, 1, 3)


def place_out(ctx, mine, other):
    return place_heads(1, ctx, mine, other)[:, 0]


def normalise(inputs):
    centred = inputs - jnp.mean(inputs, axis=-1, keepdims=True)
    spread = lax.rsqrt(jnp.mean(centred * centred, axis=-1, keepdims=True) + 1e-06)
    return centred * spread, spread


def normalise_back(grad_norm, norm, spread):
    return spread * (
        grad_norm
        - jnp.mean(grad_norm, axis=-1, keepdims=True)
        - norm * jnp.mean(grad_norm * norm, axis=-1, keepdims=True)
    )


def gelu_parts(hidden):
    root = 0.7978845608028654
    square = hidden * hidden
    bent = jnp.tanh(hidden * (root + root * 0.044715 * square))
    half = 0.5 * (1.0 + bent)
    slope = half + 0.5 * hidden * (1.0 - bent * bent) * (root + 3.0 * root * 0.044715 * square)
    return hidden * half, slope


MESH = pl.DeviceIdType.MESH
VMEM_SPEC = pl.BlockSpec(memory_space=pltpu.VMEM)
ANY_SPEC = pl.BlockSpec(memory_space=pl.ANY)


class Wires:
    def __init__(self, send_sems, recv_sems):
        self.dp, self.x, self.tp = lax.axis_index("dp"), lax.axis_index("ctx"), lax.axis_index("tp")
        self.y, self.k = self.tp // 2, self.tp % 2
        self.x_next = (self.dp, 1 - self.x, self.tp)
        self.y_next = (self.dp, self.x, (1 - self.y) * 2 + self.k)
        self.k_next = (self.dp, self.x, self.y * 2 + 1 - self.k)
        self.send_sems, self.recv_sems, self.used = send_sems, recv_sems, 0
        self.started = []

    def copy(self, source, target, device):
        wire = pltpu.make_async_remote_copy(
            src_ref=source,
            dst_ref=target,
            send_sem=self.send_sems.at[self.used],
            recv_sem=self.recv_sems.at[self.used],
            device_id=device,
            device_id_type=MESH,
        )
        self.used += 1
        wire.start()
        self.started.append(wire)
        return wire

    def meet(self, devices):
        barrier = pltpu.get_barrier_semaphore()
        for device in devices:
            pl.semaphore_signal(barrier, inc=1, device_id=device, device_id_type=MESH)
        pl.semaphore_wait(barrier, len(devices))

    def finish(self):
        for wire in self.started:
            wire.wait_send()


def row_step(rows):
    return 32 if rows % 32 == 0 else rows


def over_rows(rows, body):
    step = row_step(rows)
    if step == rows:
        body(slice(0, rows))
        return

    def one(index, carry):
        body(pl.ds(pl.multiple_of(index * step, step), step))
        return carry

    lax.fori_loop(0, rows // step, one, 0)


def reduce_first(wires, s):
    return wires.copy(s["part"].at[:, :, 1 - wires.k], s["core"], wires.k_next)


def reduce_add(wires, s, arrived):
    k = wires.k
    part, core, held = s["part"], s["core"], s["held"]
    arrived.wait_recv()
    for i in range(2):
        for j in range(2):

            def add(span, i=i, j=j):
                held[i, j, span] = (part[i, j, k, span].astype(F32) + core[i, j, span].astype(F32)).astype(BF16)

            over_rows(part.shape[3], add)


def reduce_second(wires, s):
    held = s["held"]
    cut = held.shape[3] // 2
    return (
        wires.copy(held.at[:, 1 - wires.y, :, pl.ds(0, cut)], s["along_y"], wires.y_next),
        wires.copy(held.at[1 - wires.x, :, :, pl.ds(cut, cut)], s["along_x"], wires.x_next),
    )


def reduce_third(wires, s, second):
    x, y = wires.x, wires.y
    held, along_y, along_x, out_x, out_y = s["held"], s["along_y"], s["along_x"], s["out_x"], s["out_y"]
    cut = held.shape[3] // 2
    for arrived in second:
        arrived.wait_recv()

    def add(span):
        out_x[span] = (held[1 - x, y, span, :cut].astype(F32) + along_y[1 - x, span].astype(F32)).astype(BF16)
        out_y[span] = (held[x, 1 - y, span, cut:].astype(F32) + along_x[1 - y, span].astype(F32)).astype(BF16)

    over_rows(held.shape[2], add)
    return (
        wires.copy(out_x, s["last_x"], wires.x_next),
        wires.copy(out_y, s["last_y"], wires.y_next),
    )


def reduce_last(wires, s, third):
    x, y = wires.x, wires.y
    held, along_y, along_x, last_x, last_y, total = (
        s["held"],
        s["along_y"],
        s["along_x"],
        s["last_x"],
        s["last_y"],
        s["total"],
    )
    cut = held.shape[3] // 2
    for arrived in third:
        arrived.wait_recv()

    def add(span):
        total[span, :cut] = (
            held[x, y, span, :cut].astype(F32) + along_y[x, span].astype(F32) + last_x[span].astype(F32)
        )
        total[span, cut:] = (
            held[x, y, span, cut:].astype(F32) + along_x[y, span].astype(F32) + last_y[span].astype(F32)
        )

    over_rows(held.shape[2], add)


def reduce_plane(wires, streams):
    first = [reduce_first(wires, s) for s in streams]
    second = []
    for s, arrived in zip(streams, first):
        reduce_add(wires, s, arrived)
        second.append(reduce_second(wires, s))
    third = [reduce_third(wires, s, arrived) for s, arrived in zip(streams, second)]
    for s, arrived in zip(streams, third):
        reduce_last(wires, s, arrived)


REDUCE_KEYS = ("core", "held", "along_y", "along_x", "out_x", "out_y", "last_x", "last_y", "total")


def reduce_scratch(rows, width):
    half = width // 2
    return [
        pltpu.VMEM((2, 2, rows, width), BF16),
        pltpu.VMEM((2, 2, rows, width), BF16),
        pltpu.VMEM((2, rows, half), BF16),
        pltpu.VMEM((2, rows, half), BF16),
        pltpu.VMEM((rows, half), BF16),
        pltpu.VMEM((rows, half), BF16),
        pltpu.VMEM((rows, half), BF16),
        pltpu.VMEM((rows, half), BF16),
        pltpu.VMEM((rows, width), F32),
    ]


def block_halves(block):
    cut = block.shape[-1] // 2
    inner = (slice(None),) * (len(block.shape) - 4)
    return inner + (pl.ds(0, cut),), inner + (pl.ds(cut, cut),)


def spread_first(wires, block):
    x, y, k = wires.x, wires.y, wires.k
    low, high = block_halves(block)
    mine = block.at[(x, y, k) + low], block.at[(x, y, k) + high]
    return wires.copy(mine[0], mine[0], wires.x_next), wires.copy(mine[1], mine[1], wires.y_next)


def spread_second(wires, block, first):
    x, y, k = wires.x, wires.y, wires.k
    low, high = block_halves(block)
    for arrived in first:
        arrived.wait_recv()
    lows, highs = block.at[(slice(None), y, k) + low], block.at[(x, slice(None), k) + high]
    return wires.copy(lows, lows, wires.y_next), wires.copy(highs, highs, wires.x_next)


def spread_third(wires, block, second):
    for arrived in second:
        arrived.wait_recv()
    gathered = block.at[:, :, wires.k]
    return wires.copy(gathered, gathered, wires.k_next)


def spread_plane(wires, blocks, started=()):
    first = list(started) + [spread_first(wires, block) for block in blocks[len(started) :]]
    second = [spread_second(wires, block, arrived) for block, arrived in zip(blocks, first)]
    third = [spread_third(wires, block, arrived) for block, arrived in zip(blocks, second)]
    for arrived in third:
        arrived.wait_recv()


def comm_call(kernel, outs, scratch, wires, collective_id, name, in_specs, out_specs):
    return pl.pallas_call(
        kernel,
        out_shape=outs,
        in_specs=in_specs,
        out_specs=out_specs,
        scratch_shapes=scratch + [pltpu.SemaphoreType.DMA((wires,)), pltpu.SemaphoreType.DMA((wires,))],
        compiler_params=pltpu.CompilerParams(
            collective_id=collective_id, has_side_effects=True, vmem_limit_bytes=VMEM_LIMIT
        ),
        name=name,
    )


def enter_kernel(
    n_dp,
    groups,
    part_ref,
    bias_ref,
    rows_ref,
    image_ref,
    text_ref,
    attn_ref,
    up_ref,
    down_ref,
    mod_ref,
    rows_out,
    image_out,
    text_out,
    gates_out,
    attn_out,
    ffn_out,
    moved_out,
    mod_in,
    send_sems,
    recv_sems,
):
    wires = Wires(send_sems, recv_sems)
    dp, x, y, k, tp = wires.dp, wires.x, wires.y, wires.k, wires.tp
    count = n_dp * 2
    me = dp * 2 + x
    peers = [lax.rem(me + offset, count) for offset in range(1, count)]
    others = [(peer // 2, peer % 2, tp) for peer in peers]
    lanes = [lax.rem(tp + offset, 4) for offset in range(1, 4)]
    z_next = (lax.rem(dp + 1, n_dp), x, tp)
    wires.meet(others + [(dp, x, lane) for lane in lanes])

    sums = [wires.copy(part_ref.at[peer // 2], mod_in.at[me], other) for peer, other in zip(peers, others)]
    rows = [wires.copy(rows_ref, rows_out.at[me], other) for other in others]
    swaps = [wires.copy(attn_ref.at[1 - x, s], attn_out.at[s, dp, x], wires.x_next) for s in range(2)]
    mod_in[me] = part_ref[dp]
    rows_out[me] = rows_ref[...]
    for arrived in sums:
        arrived.wait_recv()
    ring = {(s, 0): wires.copy(attn_ref.at[x, s], attn_out.at[s, dp, x], z_next) for s in range(2)}
    total = bias_ref[...]
    for source in range(count):
        total = total + mod_in[source]
    mod_ref[tp] = total
    mods = [wires.copy(mod_ref.at[tp], mod_ref.at[tp], (dp, x, lane)) for lane in lanes]
    for arrived in mods:
        arrived.wait_recv()
    gates = []
    if groups > 1:
        gates = [
            wires.copy(mod_ref.at[:, 11], gates_out.at[dp], (lax.rem(dp + offset, groups), x, tp))
            for offset in range(1, groups)
        ]
        for lane in range(4):
            gates_out[dp, lane] = mod_ref[lane, 11]

    def pass_on(turn, side):
        for s in range(2):
            ring[s, side].wait_recv()
            if turn < n_dp - 1:
                origin = lax.rem(dp + n_dp - turn, n_dp)
                block = attn_out.at[s, origin, x if side == 0 else 1 - x]
                ring[s, side] = wires.copy(block, block, z_next)

    streams = ((image_ref, image_out), (text_ref, text_out))
    cols = ffn_out.shape[3]
    wide = ffn_out.shape[0] // 2
    held = []
    for i, weight in enumerate((up_ref, down_ref)):
        for s in range(wide):
            given = weight.at[s, :, pl.ds(pl.multiple_of((1 - x) * cols, cols), cols)]
            held.append((given, ffn_out.at[i * wide + s, x]))
    for s, arrived in enumerate(swaps):
        arrived.wait_recv()
        block = attn_out.at[s, dp, 1 - x]
        ring[s, 1] = wires.copy(block, block, z_next)
    along_x = [wires.copy(ref.at[tp], out.at[x, tp], wires.x_next) for ref, out in streams]
    pass_on(1, 0)
    along_y = []
    for (_, out), arrived in zip(streams, along_x):
        arrived.wait_recv()
        block = out.at[1 - x, tp]
        along_y.append(wires.copy(block, block, wires.y_next))
    across = []
    for _, out in streams:
        block = out.at[1 - x, tp]
        across.append(wires.copy(block, block, wires.k_next))
    later = [wires.copy(given, place, wires.x_next) for given, place in held]

    def keep_tokens(span):
        for block in range(4):
            image_out[x, block, span] = image_ref[block, span]

    def keep_weights(span):
        for s in range(2):
            attn_out[s, dp, x, span] = attn_ref[x, s, span]
        for i, weight in enumerate((up_ref, down_ref)):
            for s in range(wide):
                first, last = weight[s, span, :cols], weight[s, span, cols:]
                ffn_out[i * wide + s, x, span] = jnp.where(x == 0, first, last)
            if groups > 1:
                text_cols = cols // groups
                for peer in range(count):
                    start = (peer % 2) * cols + (peer // 2) * text_cols
                    text = weight[1, span, start : start + text_cols]
                    moved_out[peer, span, i * text_cols : (i + 1) * text_cols] = text

    over_rows(image_ref.shape[1], keep_tokens)
    over_rows(attn_ref.shape[2], keep_weights)
    for block in range(4):
        text_out[x, block] = text_ref[block]
    pass_on(1, 1)
    far = (1 - y) * 2 + k
    for (_, out), arrived in zip(streams, along_y):
        arrived.wait_recv()
        block = out.at[1 - x, far]
        across.append(wires.copy(block, block, wires.k_next))
    for turn in range(2, n_dp - 1):
        pass_on(turn, 0)
        pass_on(turn, 1)
    if n_dp > 2:
        pass_on(n_dp - 1, 0)
        pass_on(n_dp - 1, 1)
    for arrived in rows + across + later + gates:
        arrived.wait_recv()
    wires.finish()


def enter(groups, partial_mod, ada_bias, bias_rows, image, text, attn, up, down, wide):
    n_dp, kinds, slice_width = partial_mod.shape
    count = 2 * n_dp
    rows, cols = up.shape[1], up.shape[2] // 2
    width = image.shape[2]
    return comm_call(
        functools.partial(enter_kernel, n_dp, groups),
        [
            jax.ShapeDtypeStruct((4, kinds, slice_width), F32),
            jax.ShapeDtypeStruct((count,) + bias_rows.shape, F32),
            jax.ShapeDtypeStruct((2,) + image.shape, BF16),
            jax.ShapeDtypeStruct((2,) + text.shape, BF16),
            jax.ShapeDtypeStruct((groups, 4, slice_width), F32),
            jax.ShapeDtypeStruct((2, n_dp, 2) + attn.shape[2:], BF16),
            jax.ShapeDtypeStruct((2 * wide, 2, rows, cols), BF16),
            jax.ShapeDtypeStruct((2 * groups, rows, 2 * cols // groups) if groups > 1 else (1, 8, 128), BF16),
        ],
        [pltpu.VMEM((count, kinds, slice_width), F32)],
        2 * (count - 1) + 2 + 4 * n_dp + 16 + groups + 5,
        0,
        "enter",
        [VMEM_SPEC] * 8,
        [VMEM_SPEC] * 8,
    )(partial_mod, ada_bias, bias_rows, image, text, attn, up, down)


def meet_planes(wires, groups):
    planes = [(lax.rem(wires.dp + offset, groups), wires.x, wires.tp) for offset in range(1, groups)]
    wires.meet(planes + [wires.x_next, wires.y_next, wires.k_next])


def meet_groups(wires, groups, more=()):
    dp, x, tp = wires.dp, wires.x, wires.tp
    count = groups * 2
    if groups == 1:
        others = [wires.x_next]
    else:
        peers = [lax.rem(dp * 2 + x + offset, count) for offset in range(1, count)]
        others = [(peer // 2, peer % 2, tp) for peer in peers]
    wires.meet(others + [wires.y_next, wires.k_next, *more])


def start_moves(wires, groups, moved_ref, moved_out, local_sem):
    if groups == 1:
        return []
    dp, x, tp = wires.dp, wires.x, wires.tp
    count = groups * 2
    me = dp * 2 + x
    peers = [lax.rem(me + offset, count) for offset in range(1, count)]
    local = pltpu.make_async_copy(moved_ref.at[me], moved_out.at[me], local_sem)
    local.start()
    return [local] + [
        wires.copy(moved_ref.at[peer], moved_out.at[me], (peer // 2, peer % 2, tp)) for peer in peers
    ]


def end_moves(moves):
    if moves:
        moves[0].wait()
    for arrived in moves[1:]:
        arrived.wait_recv()


def middle_kernel(
    n_dp,
    groups,
    image_part,
    text_part,
    image_x,
    text_x,
    mod_ref,
    bias_ref,
    moved_ref,
    *rest,
):
    ffn_refs = rest[: n_dp - 1]
    (
        cot_ref,
        image_attention,
        text_attention,
        image_middle,
        text_middle,
        image_all,
        text_all,
        cots_all,
        moved_out,
        ffn_out,
    ) = rest[n_dp - 1 : n_dp + 9]
    scratch = rest[n_dp + 9 :]
    local_sem, send_sems, recv_sems = scratch[-3:]
    wires = Wires(send_sems, recv_sems)
    dp, x, y, k, tp = wires.dp, wires.x, wires.y, wires.k, wires.tp
    z_next = (lax.rem(dp + 1, n_dp), x, tp)
    meet_groups(wires, groups, [z_next] if groups == 1 else [])
    cots = []
    if groups > 1:
        cots_all[x, y, k, dp] = cot_ref[...]
        for offset in range(1, groups):
            block = cots_all.at[x, y, k, dp]
            cots.append(wires.copy(block, block, (lax.rem(dp + offset, groups), x, tp)))
    last = wires.copy(ffn_refs[n_dp - 2], ffn_out.at[:, lax.rem(dp + 2, n_dp)], z_next)
    size = len(REDUCE_KEYS)
    streams = [
        dict(zip(("part",) + REDUCE_KEYS, (part,) + scratch[i * size : (i + 1) * size]))
        for i, part in enumerate((image_part, text_part))
    ]

    def keep(span):
        for turn, block in enumerate(ffn_refs):
            for i in range(block.shape[0]):
                ffn_out[i, lax.rem(dp + n_dp - turn, n_dp), span] = block[i, span]

    image, text = streams
    first = reduce_first(wires, text), reduce_first(wires, image)
    reduce_add(wires, text, first[0])
    text_second = reduce_second(wires, text)
    reduce_add(wires, image, first[1])
    image_second = reduce_second(wires, image)
    for arrived in cots:
        arrived.wait_recv()
    if groups > 1:
        cots_first = spread_first(wires, cots_all)
    text_third = reduce_third(wires, text, text_second)
    image_third = reduce_third(wires, image, image_second)

    def second_rows(i, tokens, attention, middle, gathered):
        total = streams[i]["total"]

        def finish(span):
            branch = total[span] + bias_ref[i]
            attention[span] = branch
            value = tokens[span].astype(F32) + mod_ref[i, 2] * branch
            middle[span] = value
            norm, _ = normalise(value)
            gathered[x, y, k, span] = (norm * (1.0 + mod_ref[i, 4]) + mod_ref[i, 3]).astype(BF16)

        over_rows(total.shape[0], finish)

    reduce_last(wires, text, text_third)
    second_rows(1, text_x, text_attention, text_middle, text_all.at[:, :, :, dp if groups > 1 else 0])
    zs = []
    for offset in range(1, groups):
        block = text_all.at[x, y, k, dp]
        zs.append(wires.copy(block, block, (lax.rem(dp + offset, groups), x, tp)))
    if groups > 1:
        cots_second = spread_second(wires, cots_all, cots_first)
    reduce_last(wires, image, image_third)
    second_rows(0, image_x, image_attention, image_middle, image_all)
    image_first = spread_first(wires, image_all)
    for arrived in zs:
        arrived.wait_recv()
    text_first = spread_first(wires, text_all)
    moves = start_moves(wires, groups, moved_ref, moved_out, local_sem)
    thirds = [spread_third(wires, cots_all, cots_second)] if groups > 1 else []
    over_rows(ffn_out.shape[2], keep)
    image_next = spread_second(wires, image_all, image_first)
    text_next = spread_second(wires, text_all, text_first)
    thirds += [spread_third(wires, image_all, image_next), spread_third(wires, text_all, text_next)]
    for arrived in thirds:
        arrived.wait_recv()
    end_moves(moves)
    last.wait_recv()
    wires.finish()


def middle_step(groups, image_part, text_part, image_x, text_x, mod, bias, moved, ffn, cot):
    (image_rows, width), text_rows = image_x.shape, text_x.shape[0]
    outs = []
    for _ in range(2):
        outs += [jax.ShapeDtypeStruct((rows, width), F32) for rows in (image_rows, text_rows)]
    outs += [jax.ShapeDtypeStruct(image_part.shape, BF16)]
    outs += [jax.ShapeDtypeStruct((2, 2, 2, groups, text_rows, width), BF16)] * 2
    outs += [jax.ShapeDtypeStruct(moved.shape, BF16)]
    n_dp = len(ffn) + 1
    outs += [jax.ShapeDtypeStruct((ffn[0].shape[0], n_dp) + ffn[0].shape[1:], BF16)]
    return comm_call(
        functools.partial(middle_kernel, n_dp, groups),
        outs,
        reduce_scratch(image_rows, width) + reduce_scratch(text_rows, width) + [pltpu.SemaphoreType.DMA(())],
        30 + 4 * groups,
        1,
        "middle",
        [VMEM_SPEC] * 6 + [ANY_SPEC] + [VMEM_SPEC] * n_dp,
        [VMEM_SPEC] * 7 + [ANY_SPEC, VMEM_SPEC],
    )(image_part, text_part, image_x, text_x, mod, bias, moved, *ffn, cot)


def turn_kernel(
    groups,
    valid_ref,
    image_feed,
    text_feed,
    image_second,
    text_second,
    image_attention,
    text_attention,
    image_middle,
    text_middle,
    image_cot,
    text_cot,
    mod_ref,
    bias_ref,
    image_out,
    text_out,
    image_grad,
    text_grad,
    sums_ref,
    image_all,
    text_all,
    *scratch,
):
    z_out, z_in, send_sems, recv_sems = scratch[-4:]
    wires = Wires(send_sems, recv_sems)
    dp, x, y, k, tp = wires.dp, wires.x, wires.y, wires.k, wires.tp
    meet_planes(wires, groups)
    size = len(REDUCE_KEYS)
    streams = [
        dict(zip(("part",) + REDUCE_KEYS, (part,) + scratch[i * size : (i + 1) * size]))
        for i, part in enumerate((text_second, text_feed, image_second, image_feed))
    ]
    pulls, feeds = (streams[2], streams[0]), (streams[3], streams[1])
    order = [pulls[1], pulls[0], feeds[1], feeds[0]]
    rows = text_middle.shape[0]

    def to_planes(i, total):
        copies = []
        if groups > 1:
            for group in range(groups):
                z_out[i, group] = total[group * rows : (group + 1) * rows].astype(BF16)
            z_in[i, dp] = z_out[i, dp]
            for offset in range(1, groups):
                plane = lax.rem(dp + offset, groups)
                copies.append(wires.copy(z_out.at[i, plane], z_in.at[i, dp], (plane, x, tp)))
        return copies

    def from_planes(i, total, copies):
        for arrived in copies:
            arrived.wait_recv()
        if groups > 1:
            summed = z_in[i, 0].astype(F32)
            for group in range(1, groups):
                summed = summed + z_in[i, group].astype(F32)
            total[0:rows] = summed

    sums_ref[...] = jnp.zeros_like(sums_ref)
    sides = (
        (image_attention, image_middle, image_cot, image_out, image_grad, image_all),
        (text_attention, text_middle, text_cot, text_out, text_grad, text_all),
    )

    def add_sums(i, start, terms):
        for t, term in enumerate(terms):
            sums_ref[i, start + t : start + t + 1] += jnp.sum(term, axis=0, keepdims=True)

    def pull_side(i):
        attention, middle, cot, _, grad, gathered = sides[i]
        total = pulls[i]["total"]

        def finish(span):
            branch, value, arriving, pulled = attention[span], middle[span], cot[span].astype(F32), total[span]
            norm, spread = normalise(value)
            grad_middle = arriving + normalise_back(pulled * (1.0 + mod_ref[i, 4]), norm, spread)
            grad[span] = grad_middle
            low = (grad_middle * mod_ref[i, 2]).astype(BF16)
            gathered[x, y, k, span] = low
            add_sums(i, 0, (grad_middle * branch, pulled, pulled * norm))
            add_sums(i, 5, (low.astype(F32),))

        over_rows(middle.shape[0], finish)

    def feed_side(i):
        attention, middle, cot, out, _, _ = sides[i]
        total = feeds[i]["total"]

        def finish(span):
            branch, value, arriving = attention[span], middle[span], cot[span].astype(F32)
            fed = total[span] + bias_ref[i]
            gated_branch = mod_ref[i, 2] * branch
            gated_feed = mod_ref[i, 5] * fed
            result = value + gated_feed
            out[span] = result.astype(BF16)
            if i == 1:
                kept = valid_ref[span]
                result, gated_branch, gated_feed = result * kept, gated_branch * kept, gated_feed * kept
            own_feed = (arriving * mod_ref[i, 5]).astype(BF16).astype(F32)
            add_sums(i, 3, (arriving * fed, own_feed))
            add_sums(i, 6, (result * result, gated_branch * gated_branch, gated_feed * gated_feed))

        over_rows(middle.shape[0], finish)

    first = [reduce_first(wires, s) for s in order]
    pull_second = []
    for s, arrived in zip(order[:2], first[:2]):
        reduce_add(wires, s, arrived)
        pull_second.append(reduce_second(wires, s))
    for s, arrived in zip(order[2:], first[2:]):
        reduce_add(wires, s, arrived)
    pull_third = [reduce_third(wires, s, arrived) for s, arrived in zip(order[:2], pull_second)]
    feed_second = [reduce_second(wires, s) for s in order[2:]]
    reduce_last(wires, pulls[1], pull_third[0])
    planes = to_planes(0, pulls[1]["total"])
    reduce_last(wires, pulls[0], pull_third[1])
    pull_side(0)
    spread_one = [spread_first(wires, image_all)]
    from_planes(0, pulls[1]["total"], planes)
    pull_side(1)
    spread_one.append(spread_first(wires, text_all))
    feed_third = [reduce_third(wires, s, arrived) for s, arrived in zip(order[2:], feed_second)]
    spread_two = [spread_second(wires, block, arrived) for block, arrived in zip((image_all, text_all), spread_one)]
    reduce_last(wires, feeds[1], feed_third[0])
    planes = to_planes(1, feeds[1]["total"])
    reduce_last(wires, feeds[0], feed_third[1])
    spread_three = [spread_third(wires, block, arrived) for block, arrived in zip((image_all, text_all), spread_two)]
    feed_side(0)
    from_planes(1, feeds[1]["total"], planes)
    feed_side(1)
    for arrived in spread_three:
        arrived.wait_recv()
    wires.finish()


def turn_step(groups, valid, feeds, seconds, attentions, middles, cots, mod, bias):
    width = middles[0].shape[1]
    rows = [part.shape[0] for part in middles]
    outs = [jax.ShapeDtypeStruct((r, width), BF16) for r in rows]
    outs += [jax.ShapeDtypeStruct((r, width), F32) for r in rows]
    outs += [jax.ShapeDtypeStruct((2, 16, width), F32)]
    outs += [jax.ShapeDtypeStruct((2, 2, 2, r, width), BF16) for r in rows]
    scratch = []
    for r in (rows[1] * groups, rows[0]):
        scratch += reduce_scratch(r, width) + reduce_scratch(r, width)
    scratch += [pltpu.VMEM((2, groups, rows[1], width), BF16)] * 2
    return comm_call(
        functools.partial(turn_kernel, groups),
        outs,
        scratch,
        30 + 4 * groups,
        2,
        "turn",
        [VMEM_SPEC] * 13,
        [VMEM_SPEC] * 7,
    )(valid, *feeds, *seconds, *attentions, *middles, *cots, mod, bias)


PACKED = 24


def leave_kernel(
    n_dp,
    image_part,
    text_part,
    image_x,
    text_x,
    image_grad,
    text_grad,
    image_out,
    text_out,
    sums_ref,
    mod_ref,
    halves_ref,
    ffn_mine,
    out_mine,
    image_outs,
    text_outs,
    image_grads,
    text_grads,
    packed_out,
    halves_out,
    ffn_other,
    out_other,
    *scratch,
):
    send_sems, recv_sems = scratch[-2:]
    packed, packed_in, own_sums, both_halves, local_sums = scratch[-7:-2]
    wires = Wires(send_sems, recv_sems)
    dp, x, y, k, tp = wires.dp, wires.x, wires.y, wires.k, wires.tp
    me = x * 4 + tp
    peers = [lax.rem(me + offset, 8) for offset in range(1, 8)]
    planes = [lax.rem(dp + offset, n_dp) for offset in range(1, n_dp)]
    wires.meet([(dp, peer // 4, peer % 4) for peer in peers] + [(plane, x, tp) for plane in planes])

    image_outs[tp] = image_out[...]
    text_outs[tp] = text_out[...]
    both_halves[x] = halves_ref[...]
    halves = wires.copy(both_halves.at[x], both_halves.at[x], wires.x_next)
    size = len(REDUCE_KEYS)
    streams = [
        dict(zip(("part",) + REDUCE_KEYS, (part,) + scratch[i * size : (i + 1) * size]))
        for i, part in enumerate((image_part, text_part))
    ]
    reduce_plane(wires, streams)
    given = ffn_other.shape[0]
    given = pl.ds(pl.multiple_of((1 - x) * given, given), given)
    swaps = [
        wires.copy(mine.at[given], other, wires.x_next)
        for mine, other in ((ffn_mine, ffn_other), (out_mine, out_other))
    ]
    local_sums[...] = jnp.zeros_like(local_sums)
    for i, (tokens, grad, all_grads) in enumerate(
        ((image_x, image_grad, image_grads), (text_x, text_grad, text_grads))
    ):
        total = streams[i]["total"]

        def finish(span, i=i, tokens=tokens, grad=grad, all_grads=all_grads, total=total):
            pulled = total[span]
            norm, spread = normalise(tokens[span].astype(F32))
            grad_tokens = grad[span] + normalise_back(pulled * (1.0 + mod_ref[i, 1]), norm, spread)
            all_grads[tp, span] = grad_tokens.astype(BF16)
            local_sums[2 * i : 2 * i + 1] += jnp.sum(pulled, axis=0, keepdims=True)
            local_sums[2 * i + 1 : 2 * i + 2] += jnp.sum(pulled * norm, axis=0, keepdims=True)

        over_rows(total.shape[0], finish)
    wide = packed.shape[2]
    for t in range(4):
        cols = slice(t * wide, (t + 1) * wide)
        for i in range(2):
            packed[t, 6 * i : 6 * i + 2] = local_sums[2 * i : 2 * i + 2, cols]
            packed[t, 6 * i + 2 : 6 * i + 6] = sums_ref[i, 0:4, cols]
            packed[t, 12 + 5 * i : 12 + 5 * i + 5] = sums_ref[i, 4:9, cols]
        packed[t, 22:24] = jnp.zeros((2, wide), F32)
    packed_in[me] = packed[tp]
    gathers = [wires.copy(packed.at[peer % 4], packed_in.at[me], (dp, peer // 4, peer % 4)) for peer in peers]
    finals = (image_outs, text_outs, image_grads, text_grads)
    along_y = [wires.copy(final.at[tp], final.at[tp], wires.y_next) for final in finals]
    across = [wires.copy(final.at[tp], final.at[tp], wires.k_next) for final in finals]
    for arrived in gathers:
        arrived.wait_recv()
    total = packed_in[0]
    for source in range(1, 8):
        total = total + packed_in[source]
    own_sums[...] = total
    halves.wait_recv()
    for plane in planes:
        across.append(wires.copy(own_sums, packed_out.at[dp], (plane, x, tp)))
        across.append(wires.copy(both_halves, halves_out.at[dp], (plane, x, tp)))
    packed_out[dp] = total
    halves_out[dp] = both_halves[...]
    far = (1 - y) * 2 + k
    for final, arrived in zip(finals, along_y):
        arrived.wait_recv()
        across.append(wires.copy(final.at[far], final.at[far], wires.k_next))
    for arrived in across + swaps:
        arrived.wait_recv()
    wires.finish()


def leave_step(n_dp, parts, tokens, grads, outs_own, sums, mod, halves, ffn_mine, out_mine):
    width = tokens[0].shape[1]
    rows = [part.shape[0] for part in tokens]
    wide = width // 4
    outs = [jax.ShapeDtypeStruct((4, r, width), BF16) for r in rows] * 2
    outs += [
        jax.ShapeDtypeStruct((n_dp, PACKED, wide), F32),
        jax.ShapeDtypeStruct((n_dp, 2) + halves.shape, F32),
    ]
    outs += [jax.ShapeDtypeStruct((mine.shape[0] // 2, mine.shape[1]), BF16) for mine in (ffn_mine, out_mine)]
    scratch = []
    for r in rows:
        scratch += reduce_scratch(r, width)
    scratch += [
        pltpu.VMEM((4, PACKED, wide), F32),
        pltpu.VMEM((8, PACKED, wide), F32),
        pltpu.VMEM((PACKED, wide), F32),
        pltpu.VMEM((2,) + halves.shape, F32),
        pltpu.VMEM((8, width), F32),
    ]
    return comm_call(
        functools.partial(leave_kernel, n_dp),
        outs,
        scratch,
        1 + 10 + 7 + 8 + 2 * (n_dp - 1) + 6,
        3,
        "leave",
        [VMEM_SPEC] * 11 + [ANY_SPEC] * 2,
        [VMEM_SPEC] * 6 + [ANY_SPEC] * 2,
    )(*parts, *tokens, *grads, *outs_own, sums, mod, halves, ffn_mine, out_mine)


def share_kernel(part_ref, out_ref, send_sems, recv_sems):
    wires = Wires(send_sems, recv_sems)
    dp, x, tp = wires.dp, wires.x, wires.tp
    lanes = [(dp, x, lax.rem(tp + offset, 4)) for offset in range(1, 4)]
    wires.meet(lanes)
    copies = [wires.copy(part_ref, out_ref.at[tp], lane) for lane in lanes]
    out_ref[tp] = part_ref[...]
    for arrived in copies:
        arrived.wait_recv()
    wires.finish()


def share(part):
    return comm_call(
        share_kernel,
        jax.ShapeDtypeStruct((4,) + part.shape, F32),
        [],
        3,
        4,
        "share",
        [VMEM_SPEC],
        VMEM_SPEC,
    )(part)


def scatter_rows(grad):
    return lax.psum_scatter(grad, "dp", scatter_dimension=0, tiled=True)


def on_device(
    image_tokens,
    text_tokens,
    conditioning,
    ada_weight,
    ada_bias,
    qkv_weight,
    qv_bias,
    out_weight,
    out_bias,
    up_weight,
    up_bias,
    down_weight,
    down_bias,
    image_cotangent,
    text_cotangent,
):
    ctx_n, tp_n, dp_n = lax.axis_size("ctx"), lax.axis_size("tp"), lax.axis_size("dp")
    dp, ctx, tp = lax.axis_index("dp"), lax.axis_index("ctx"), lax.axis_index("tp")
    image_length, text_length, width = image_tokens.shape[1], text_tokens.shape[1], image_tokens.shape[2]
    slice_width = qkv_weight.shape[3]
    shard_rows = qkv_weight.shape[1]
    half = slice_width // ctx_n
    up_half = up_weight.shape[2] // ctx_n
    own_rows = (image_length // tp_n, TEXT_SLOTS // tp_n)
    image_all = image_length * ctx_n
    text_all = TEXT_SLOTS * ctx_n
    pad = ((0, TEXT_SLOTS - text_length), (0, 0))

    groups = dp_n if dp_n <= MOST_GROUPS else 1
    wide = 1 if groups > 1 else 2
    text_cols = up_half // groups
    text_start = ctx * up_half + (dp * text_cols if groups > 1 else 0)

    tokens = (image_tokens[0], jnp.pad(text_tokens[0], pad))
    cotangents = (image_cotangent[0], jnp.pad(text_cotangent[0], pad))

    def own(parts):
        return [lax.dynamic_slice_in_dim(part, tp * rows, rows, 0) for part, rows in zip(parts, own_rows)]

    tokens_own, cotangents_own = own(tokens), own(cotangents)
    cond_float = conditioning.astype(F32)
    activated_low = jax.nn.silu(cond_float).astype(BF16)
    partial_mod = jnp.einsum("nd,adkf->nakf", activated_low, ada_weight, preferred_element_type=F32)
    (
        mod_blocks,
        bias_blocks,
        image_blocks,
        text_blocks,
        text_gates,
        attn_full,
        ffn_mixed,
        moved,
    ) = enter(
        groups,
        partial_mod.reshape(dp_n, 12, slice_width),
        ada_bias.astype(F32).reshape(12, slice_width),
        jnp.concatenate([out_bias, down_bias], 0).astype(F32),
        *[part.reshape(tp_n, rows, width) for part, rows in zip(tokens, own_rows)],
        jnp.stack(
            [
                jnp.concatenate(
                    [qkv_weight[:, :, j, c * half : (c + 1) * half] for j in range(3)]
                    + [out_weight[:, :, c * half : (c + 1) * half]],
                    2,
                )
                for c in range(ctx_n)
            ]
        ),
        up_weight,
        down_weight,
        wide,
    )
    cotangents = (lax.optimization_barrier((cotangents[0], mod_blocks))[0], cotangents[1])
    image_other = lax.ppermute(cotangents[0], "ctx", [(0, 1), (1, 0)])
    attn_full = attn_full.reshape(2, width, 4 * half)
    ffn_blocks = [ffn_mixed.reshape(2 * wide, 2 * shard_rows, up_half)]
    around = [(i, (i + 1) % dp_n) for i in range(dp_n)]
    ffn_blocks.append(lax.ppermute(ffn_blocks[0], "dp", around))
    modulation = mod_blocks.transpose(1, 0, 2).reshape(2, 6, width)
    biases = bias_blocks.transpose(1, 0, 2).reshape(4, width)
    mod_rows = modulation[:, :, None]
    out_bias_rows, down_bias_rows = biases[:2, None], biases[2:, None]
    tokens_all = (image_blocks.reshape(image_all, width), text_blocks.reshape(text_all, width))
    qv_own = lax.dynamic_slice_in_dim(qv_bias, ctx * half, half, 2).astype(F32)
    up_bias_own = (
        lax.dynamic_slice_in_dim(up_bias[0], ctx * up_half, up_half, 0).astype(F32),
        lax.dynamic_slice_in_dim(up_bias[1], text_start, text_cols, 0).astype(F32),
    )
    slots = tp * own_rows[1] + lax.broadcasted_iota(jnp.int32, (own_rows[1], 1), 0)
    valid = jnp.broadcast_to((slots < text_length).astype(F32), (own_rows[1], width))

    own_ctx = jnp.full((1,), ctx, jnp.int32)

    def other_half(part):
        return lax.ppermute(part, "ctx", [(0, 1), (1, 0)])

    def blocks(part):
        return part.reshape(2, 2, 2, part.shape[0] // 8, width)

    qv_bias_rows = jnp.concatenate([qv_own[:, 0], jnp.zeros((2, half), F32), qv_own[:, 1]], 1)[:, None]
    normed_low, queries, keys, values, out_full = project(
        *tokens_all, mod_rows[:, :2], attn_full, qv_bias_rows
    )
    queries, ffn_blocks[1] = lax.optimization_barrier((queries, ffn_blocks[1]))
    for _ in range(dp_n - 3):
        ffn_blocks.append(lax.ppermute(ffn_blocks[-1], "dp", around))
    blended, lse, *out_parts = attend_forward(queries, keys, values, out_full, text_all, text_length)
    out_parts = [blocks(part) for part in out_parts]
    *attentions_middles, image_second, text_second, text_cots, moved_in, ffn_full = middle_step(
        groups, *out_parts, *tokens_own, mod_rows, out_bias_rows, moved, ffn_blocks, cotangents_own[1]
    )
    ffn_full = ffn_full.reshape(2 * wide, width, up_half)
    attentions, middles = attentions_middles[:2], attentions_middles[2:]
    second_low = (image_second.reshape(-1, width), text_second.reshape(-1, width))

    up_full, down_full = [(ffn_full, 0)], [(ffn_full, wide)]
    if groups > 1:
        moved_in = moved_in.reshape(width, 2 * text_cols)
        up_full.append((moved_in[None, :, :text_cols], 0))
        down_full.append((moved_in[None, :, text_cols:], 0))
        text_feed = (text_cots.reshape(-1, width), None, text_gates.reshape(groups, width))
    else:
        up_full.append((ffn_full, 1))
        down_full.append((ffn_full, 3))
        text_feed = (cotangents[1], other_half(cotangents[1]), mod_rows[1, 5])
    arrivals = ((cotangents[0], image_other, mod_rows[0, 5]), text_feed)
    feed_parts, second_parts, ffn_grads, up_bias_grads = [], [], [], []
    done = {}
    for stream in (1, 0):
        operands = (second_low[stream], *arrivals[stream], up_full[stream], down_full[stream], up_bias_own[stream])
        if groups > 1 and stream == 0:
            moved = done[1][2].reshape(dp_n * ctx_n, shard_rows, 2 * text_cols)
            *done[0], moved_in = feed_forward_moving(groups, *operands, moved)
        else:
            done[stream] = feed_forward(own_ctx, *operands)
    for stream in range(2):
        feed, pulled, grads, sums = done[stream]
        feed_parts.append(blocks(feed))
        second_parts.append(blocks(pulled))
        ffn_grads.append(grads)
        up_bias_grads.append(sums[0])
    if groups > 1:
        ffn_mine = scatter_rows(ffn_grads[0])
    else:
        ffn_mine = scatter_rows(jnp.concatenate(ffn_grads, 1))
    image_out, text_out, image_middle_grad, text_middle_grad, sums, image_attn, text_attn = turn_step(
        groups, valid, feed_parts, second_parts, attentions, middles, cotangents_own, mod_rows, down_bias_rows
    )
    attention_grad_all = (image_attn.reshape(-1, width), text_attn.reshape(-1, width))
    out_weight_grads = out_gradient(*attention_grad_all, blended)
    out_weight_grads, ffn_mine = lax.optimization_barrier((out_weight_grads, ffn_mine))
    out_mine = scatter_rows(out_weight_grads)
    grad_queries, grad_keys, grad_values = attend_backward(
        queries, keys, values, lse, *attention_grad_all, out_full, text_length
    )
    *normed_parts, qkv_weight_grads, joint_sums = unproject(
        grad_queries, grad_keys, grad_values, normed_low, attn_full, text_all
    )
    normed_parts = [blocks(part) for part in normed_parts]
    qkv_weight_grads, out_mine = lax.optimization_barrier((qkv_weight_grads, out_mine))
    qkv_mine = scatter_rows(qkv_weight_grads)

    def given(mine):
        return lax.dynamic_slice_in_dim(mine, (1 - ctx) * shard_rows, shard_rows, 0)

    qv_bias_grads = [
        jnp.concatenate([joint_sums[stream, 0, :half], joint_sums[stream, 0, 2 * half :]]) for stream in range(2)
    ]
    if groups > 1:
        up_bias_grads[1] = lax.dynamic_update_slice_in_dim(
            jnp.zeros((up_half,), F32), up_bias_grads[1], dp * text_cols, 0
        )
    halves = jnp.concatenate(
        [part.reshape(-1, slice_width) for part in (*qv_bias_grads, *up_bias_grads)], 0
    )
    image_outs, text_outs, image_grads, text_grads, packed, halves_all, ffn_other, out_other = leave_step(
        dp_n,
        normed_parts,
        tokens_own,
        (image_middle_grad, text_middle_grad),
        (image_out, text_out),
        sums,
        mod_rows,
        halves,
        ffn_mine,
        out_mine,
    )
    grad_mod_low = packed[:, :12].astype(BF16)
    ada_bias_grad = jnp.sum(grad_mod_low.astype(F32), axis=0).reshape(2, 6, slice_width)
    grad_mod_low = grad_mod_low.reshape(dp_n, 2, 6, slice_width)
    ada_weight_grad = jnp.einsum("nd,nakf->adkf", activated_low, grad_mod_low, preferred_element_type=F32)
    cond_partial = jnp.einsum("nakf,adkf->nd", grad_mod_low, ada_weight, preferred_element_type=F32)
    totals = jnp.sum(packed[:, 12:22], axis=0)
    cond_rows = jnp.pad(cond_partial, ((0, -dp_n % 2), (0, slice_width - shard_rows)))
    shared = share(jnp.concatenate([totals, cond_rows], 0))
    shared, qkv_given, image_outs, text_outs, out_other, ffn_other = lax.optimization_barrier(
        (shared, given(qkv_mine), image_outs, text_outs, out_other, ffn_other)
    )
    qkv_other = other_half(qkv_given)
    final_tokens = place_tokens((image_outs, text_outs, image_grads, text_grads), image_length, text_length)
    out_weight_grad = place_out(own_ctx, out_mine, out_other)
    if groups > 1:
        up_weight_grad, down_weight_grad = place_feed(own_ctx, ffn_mine, ffn_other, moved_in)
    else:
        kept, other = lax.dynamic_slice_in_dim(ffn_mine, ctx * shard_rows, shard_rows, 0), ffn_other
        ffn_halves = [jnp.where(ctx == c, kept, other).astype(F32) for c in range(2)]
        up_weight_grad, down_weight_grad = [
            jnp.stack(
                [
                    jnp.concatenate([part[:, c * up_half : (c + 1) * up_half] for part in ffn_halves], 1)
                    for c in (i, 2 + i)
                ]
            )
            for i in range(2)
        ]
    qkv_weight_grad = place_qkv(own_ctx, qkv_mine, qkv_other)
    cond_total = jnp.sum(shared[:, 10 : 10 + dp_n, :shard_rows], axis=0)
    cond_grad = jax.vjp(jax.nn.silu, cond_float)[1](cond_total)[0]
    full = shared[:, :10].transpose(1, 0, 2).reshape(2, 5, width)
    bias_grads = lax.dynamic_slice_in_dim(full[:, :2], (dp * ctx_n + ctx) * shard_rows, shard_rows, 2)
    squares_total = jnp.sum(full[:, 2:], axis=2).T.reshape(6)
    counts = jnp.array([image_length, text_length] * 3, F32) * (dp_n * ctx_n * width)
    root_means = jnp.sqrt(squares_total / counts)
    half_sums = jnp.sum(halves_all, axis=0)
    qv_rows = half * 2 // slice_width
    up_rows = up_half // slice_width
    qv_bias_grad = (
        half_sums[:, : 2 * qv_rows].reshape(ctx_n, 2, 2, half).transpose(1, 2, 0, 3).reshape(2, 2, slice_width)
    )
    up_bias_grad = (
        half_sums[:, 2 * qv_rows : 2 * (qv_rows + up_rows)]
        .reshape(ctx_n, 2, up_half)
        .transpose(1, 0, 2)
        .reshape(2, ctx_n * up_half)
    )
    return (
        *final_tokens,
        cond_grad,
        ada_weight_grad,
        ada_bias_grad,
        qkv_weight_grad,
        qv_bias_grad,
        out_weight_grad,
        bias_grads[:, 1],
        up_weight_grad,
        up_bias_grad,
        down_weight_grad,
        bias_grads[:, 0],
        root_means,
    )


def solution(mesh):
    rows = P(None, ("dp", "ctx"))
    tokens = P("dp", "ctx", None)
    stacked = P(None, ("dp", "ctx"), None, "tp")
    matrix = P(None, ("dp", "ctx"), "tp")
    return jax.shard_map(
        on_device,
        mesh=mesh,
        in_specs=(
            tokens,
            tokens,
            rows,
            stacked,
            P(None, None, "tp"),
            stacked,
            P(None, None, "tp"),
            matrix,
            rows,
            matrix,
            P(None, "tp"),
            matrix,
            rows,
            tokens,
            tokens,
        ),
        out_specs=(
            tokens,
            tokens,
            tokens,
            tokens,
            rows,
            stacked,
            P(None, None, "tp"),
            stacked,
            P(None, None, "tp"),
            matrix,
            rows,
            matrix,
            P(None, "tp"),
            matrix,
            rows,
            P(),
        ),
        check_vma=False,
    )
```

```python
import functools

import jax
import jax.numpy as jnp
from jax import lax
from jax.experimental import pallas as pl
from jax.experimental.pallas import tpu as pltpu
from jax.sharding import PartitionSpec as P

HEAD_DIM = 64
F32 = jnp.float32
BF16 = jnp.bfloat16
VMEM_LIMIT = 60 * 1024 * 1024
PLANE = ("ctx", "tp")
TEXT_SLOTS = 96
MOST_GROUPS = 4
QUERY_BLOCK = 256


def dot(left, right, dims=((1,), (0,))):
    return lax.dot_general(left, right, (dims, ((), ())), preferred_element_type=F32)


def local_call(kernel, steps, in_specs, outs, scratch, flops, name):
    return pl.pallas_call(
        kernel,
        grid=(steps,),
        in_specs=in_specs,
        out_specs=[spec for spec, _ in outs],
        out_shape=[shape for _, shape in outs],
        scratch_shapes=scratch,
        compiler_params=pltpu.CompilerParams(vmem_limit_bytes=VMEM_LIMIT),
        cost_estimate=pl.CostEstimate(flops=flops, bytes_accessed=flops // 256, transcendentals=0),
        name=name,
    )


def fixed(shape):
    return pl.BlockSpec(shape, lambda i: (0,) * len(shape), pipeline_mode=pl.Buffered(1))


def stepped(shape):
    return pl.BlockSpec(shape, lambda i: (i,) + (0,) * (len(shape) - 1))


def image_block(shape, last):
    return pl.BlockSpec(shape, lambda i: (jnp.minimum(i, last),) + (0,) * (len(shape) - 1))


def stream_block(shape, steps):
    return pl.BlockSpec(shape, lambda i: (i // steps,) + (0,) * (len(shape) - 1))


def padded(text):
    return jnp.concatenate([text, jnp.zeros((QUERY_BLOCK - text.shape[0], text.shape[1]), text.dtype)], 0)


def by_stream(steps, image_ref, text_ref, body):
    step = pl.program_id(0)

    @pl.when(step < steps)
    def _():
        body(image_ref[...], 0)

    @pl.when(step >= steps)
    def _():
        body(padded(text_ref[...]), 1)


def project_kernel(steps, image_ref, text_ref, mod_ref, weight_ref, bias_ref, normed_ref, q_ref, k_ref, v_ref, out_ref):
    half = q_ref.shape[1]

    def body(tokens, stream):
        norm, _ = normalise(tokens.astype(F32))
        normed = (norm * (1.0 + mod_ref[0, 1]) + mod_ref[0, 0]).astype(BF16)
        normed_ref[...] = normed
        joint = dot(normed, weight_ref[0, :, : 3 * half]) + bias_ref[0]
        q_ref[...] = joint[:, :half].astype(BF16)
        k_ref[...] = joint[:, half : 2 * half].astype(BF16)
        v_ref[...] = joint[:, 2 * half :].astype(BF16)

    by_stream(steps, image_ref, text_ref, body)

    @pl.when(lax.rem(pl.program_id(0), steps) == 0)
    def _():
        out_ref[0] = weight_ref[0, :, 3 * half :]


def project(image, text, mod, weight, bias):
    (rows, width), wide = image.shape, weight.shape[2]
    steps, half = rows // QUERY_BLOCK, wide // 4
    joint = rows + QUERY_BLOCK
    heads = [(stepped((QUERY_BLOCK, half)), jax.ShapeDtypeStruct((joint, half), BF16))] * 3
    return local_call(
        functools.partial(project_kernel, steps),
        steps + 1,
        [
            image_block((QUERY_BLOCK, width), steps - 1),
            fixed(text.shape),
            stream_block((1,) + mod.shape[1:], steps),
            stream_block((1,) + weight.shape[1:], steps),
            stream_block((1,) + bias.shape[1:], steps),
        ],
        [(stepped((QUERY_BLOCK, width)), jax.ShapeDtypeStruct((joint, width), BF16))]
        + heads
        + [(stream_block((1, width, half), steps), jax.ShapeDtypeStruct((2, width, half), BF16))],
        [],
        6 * joint * width * half,
        "project",
    )(image, text, mod, weight, bias)


def key_bias(rows, image_rows, text_rows):
    slot = lax.broadcasted_iota(jnp.int32, (rows, 1), 0)
    text_slot = slot - image_rows
    unused = jnp.logical_or(lax.rem(text_slot, TEXT_SLOTS) >= text_rows, text_slot >= 2 * TEXT_SLOTS)
    masked = jnp.logical_and(text_slot >= 0, unused)
    return jnp.where(masked, -1e30, 0.0).astype(F32)


def attend_forward_kernel(
    steps, heads, text_rows, q_ref, k_ref, v_ref, weight_ref, o_ref, lse_ref, image_ref, text_ref, vt_ref
):
    step = pl.program_id(0)

    @pl.when(step == 0)
    def _():
        vt_ref[...] = v_ref[...].T

    rows = k_ref.shape[0]
    bias = key_bias(rows, steps * QUERY_BLOCK, text_rows)
    queries_t = (q_ref[...] * HEAD_DIM ** (-0.5)).T
    outs = []
    for head in range(heads):
        span = slice(head * HEAD_DIM, (head + 1) * HEAD_DIM)
        scores = dot(k_ref[:, span], queries_t[span]) + bias
        top = jnp.max(scores, axis=0, keepdims=True)
        grown = jnp.exp(scores - top)
        total = jnp.sum(grown, axis=0, keepdims=True)
        lse_ref[head : head + 1] = top + jnp.log(total)
        outs.append(dot(vt_ref[span], grown.astype(BF16)) * (1.0 / total))
    blended = jnp.concatenate(outs, 0).T.astype(BF16)
    o_ref[...] = blended
    branch = dot(blended, weight_ref[0], ((1,), (1,))).astype(BF16)

    @pl.when(step < steps)
    def _():
        image_ref[...] = branch

    @pl.when(step >= steps)
    def _():
        text_ref[...] = branch[: text_ref.shape[0]]


def attend_forward(q, k, v, weight, text_all, text_rows):
    rows, wide = q.shape
    width = weight.shape[1]
    heads = wide // HEAD_DIM
    steps = rows // QUERY_BLOCK - 1
    return local_call(
        functools.partial(attend_forward_kernel, steps, heads, text_rows),
        steps + 1,
        [
            stepped((QUERY_BLOCK, wide)),
            fixed((rows, wide)),
            fixed((rows, wide)),
            stream_block((1, width, wide), steps),
        ],
        [
            (stepped((QUERY_BLOCK, wide)), jax.ShapeDtypeStruct((rows, wide), BF16)),
            (pl.BlockSpec((heads, QUERY_BLOCK), lambda i: (0, i)), jax.ShapeDtypeStruct((heads, rows), F32)),
            (image_block((QUERY_BLOCK, width), steps - 1), jax.ShapeDtypeStruct((steps * QUERY_BLOCK, width), BF16)),
            (pl.BlockSpec((text_all, width), lambda i: (0, 0)), jax.ShapeDtypeStruct((text_all, width), BF16)),
        ],
        [pltpu.VMEM((wide, rows), BF16)],
        4 * rows * rows * wide,
        "attend_forward",
    )(q, k, v, weight)


def out_gradient_kernel(steps, image_ref, text_ref, o_ref, dw_ref, dw_sum):
    step = pl.program_id(0)
    wide = o_ref.shape[1]

    @pl.when(step == 0)
    def _():
        dw_sum[...] = jnp.zeros_like(dw_sum)

    def add(arriving, stream):
        dw_sum[stream] += dot(arriving, o_ref[...], ((0,), (0,)))

    by_stream(steps, image_ref, text_ref, add)

    @pl.when(step == steps)
    def _():
        for stream in range(2):
            dw_ref[:, stream * wide : (stream + 1) * wide] = dw_sum[stream].astype(BF16)


def out_gradient(image, text, blended):
    rows, wide = blended.shape
    width = image.shape[1]
    steps = rows // QUERY_BLOCK - 1
    return local_call(
        functools.partial(out_gradient_kernel, steps),
        steps + 1,
        [image_block((QUERY_BLOCK, width), steps - 1), fixed(text.shape), stepped((QUERY_BLOCK, wide))],
        [(pl.BlockSpec((width, 2 * wide), lambda i: (0, 0)), jax.ShapeDtypeStruct((width, 2 * wide), BF16))],
        [pltpu.VMEM((2, width, wide), F32)],
        2 * rows * width * wide,
        "out_gradient",
    )(image, text, blended)[0]


def attend_backward_kernel(
    steps,
    heads,
    text_rows,
    q_ref,
    k_ref,
    v_ref,
    lse_ref,
    image_ref,
    text_ref,
    weight_ref,
    dq_ref,
    dk_ref,
    dv_ref,
    kt_ref,
    g_ref,
    dk_sum,
    dv_sum,
):
    step = pl.program_id(0)

    @pl.when(step == 0)
    def _():
        kt_ref[...] = k_ref[...].T
        dk_sum[...] = jnp.zeros_like(dk_sum)
        dv_sum[...] = jnp.zeros_like(dv_sum)

    def bring(arriving, stream):
        g_ref[...] = dot(arriving, weight_ref[0]).astype(BF16)

    by_stream(steps, image_ref, text_ref, bring)
    rows = k_ref.shape[0]
    bias = key_bias(rows, steps * QUERY_BLOCK, text_rows)
    queries = q_ref[...] * HEAD_DIM ** (-0.5)
    queries_t = queries.T
    grads = g_ref[...]
    grads_t = grads.T
    outs = []
    for head in range(heads):
        span = slice(head * HEAD_DIM, (head + 1) * HEAD_DIM)
        scores = dot(k_ref[:, span], queries_t[span]) + bias
        prob = jnp.exp(scores - lse_ref[head : head + 1])
        grad_prob = dot(v_ref[:, span], grads_t[span])
        weighted = prob * grad_prob
        inner = jnp.sum(weighted, axis=0, keepdims=True)
        grad_score = (weighted - prob * inner).astype(BF16)
        dv_sum[head] += dot(prob.astype(BF16), grads[:, span])
        dk_sum[head] += dot(grad_score, queries[:, span])
        outs.append(dot(kt_ref[span], grad_score) * HEAD_DIM ** (-0.5))
    dq_ref[...] = jnp.concatenate(outs, 0).T.astype(BF16)

    @pl.when(step == steps)
    def _():
        dk_ref[...] = jnp.concatenate([dk_sum[head] for head in range(heads)], 1).astype(BF16)
        dv_ref[...] = jnp.concatenate([dv_sum[head] for head in range(heads)], 1).astype(BF16)


def attend_backward(q, k, v, lse, image, text, weight, text_rows):
    rows, wide = q.shape
    width = weight.shape[1]
    heads = wide // HEAD_DIM
    steps = rows // QUERY_BLOCK - 1
    block = stepped((QUERY_BLOCK, wide))
    whole = pl.BlockSpec((rows, wide), lambda i: (0, 0))
    return local_call(
        functools.partial(attend_backward_kernel, steps, heads, text_rows),
        steps + 1,
        [
            block,
            fixed((rows, wide)),
            fixed((rows, wide)),
            pl.BlockSpec((heads, QUERY_BLOCK), lambda i: (0, i)),
            image_block((QUERY_BLOCK, width), steps - 1),
            fixed(text.shape),
            stream_block((1, width, wide), steps),
        ],
        [
            (block, jax.ShapeDtypeStruct((rows, wide), BF16)),
            (whole, jax.ShapeDtypeStruct((rows, wide), BF16)),
            (whole, jax.ShapeDtypeStruct((rows, wide), BF16)),
        ],
        [
            pltpu.VMEM((wide, rows), BF16),
            pltpu.VMEM((QUERY_BLOCK, wide), BF16),
            pltpu.VMEM((heads, rows, HEAD_DIM), F32),
            pltpu.VMEM((heads, rows, HEAD_DIM), F32),
        ],
        10 * rows * rows * wide,
        "attend_backward",
    )(q, k, v, lse, image, text, weight)


def unproject_kernel(
    steps, dq_ref, dk_ref, dv_ref, normed_ref, weight_ref, image_ref, text_ref, dw_ref, sums_ref, dw_sum
):
    step = pl.program_id(0)
    half = dq_ref.shape[1]
    stream = step // steps

    @pl.when(step == 0)
    def _():
        dw_sum[...] = jnp.zeros_like(dw_sum)
        sums_ref[...] = jnp.zeros_like(sums_ref)

    grads = jnp.concatenate([dq_ref[...], dk_ref[...], dv_ref[...]], 1)
    part = dot(grads, weight_ref[0, :, : 3 * half], ((1,), (1,))).astype(BF16)
    dw_sum[stream] += dot(normed_ref[...], grads, ((0,), (0,)))
    sums_ref[stream] += jnp.sum(grads.astype(F32), axis=0, keepdims=True)

    @pl.when(step < steps)
    def _():
        image_ref[...] = part

    @pl.when(step == steps)
    def _():
        text_ref[...] = part[: text_ref.shape[0]]
        for s in range(2):
            dw_ref[:, s * 3 * half : (s + 1) * 3 * half] = dw_sum[s].astype(BF16)


def unproject(dq, dk, dv, normed, weight, text_all):
    rows, half = dq.shape
    width = normed.shape[1]
    steps = rows // QUERY_BLOCK - 1
    block = stepped((QUERY_BLOCK, half))
    return local_call(
        functools.partial(unproject_kernel, steps),
        steps + 1,
        [
            block,
            block,
            block,
            stepped((QUERY_BLOCK, width)),
            stream_block((1,) + weight.shape[1:], steps),
        ],
        [
            (image_block((QUERY_BLOCK, width), steps - 1), jax.ShapeDtypeStruct((steps * QUERY_BLOCK, width), BF16)),
            (pl.BlockSpec((text_all, width), lambda i: (0, 0)), jax.ShapeDtypeStruct((text_all, width), BF16)),
            (pl.BlockSpec((width, 6 * half), lambda i: (0, 0)), jax.ShapeDtypeStruct((width, 6 * half), BF16)),
            (pl.BlockSpec((2, 1, 3 * half), lambda i: (0, 0, 0)), jax.ShapeDtypeStruct((2, 1, 3 * half), F32)),
        ],
        [pltpu.VMEM((2, width, 3 * half), F32)],
        12 * rows * width * half,
        "unproject",
    )(dq, dk, dv, normed, weight)


def feed_kernel(
    halves,
    ctx_ref,
    second_ref,
    cot_ref,
    other_ref,
    gate_ref,
    up_ref,
    down_ref,
    bias_ref,
    feed_ref,
    pull_ref,
    dw_ref,
    sums_ref,
    up_sum,
    down_sum,
    gate_rows,
):
    step = pl.program_id(0)
    wide = up_ref.shape[1]

    @pl.when(step == 0)
    def _():
        up_sum[...] = jnp.zeros_like(up_sum)
        down_sum[...] = jnp.zeros_like(down_sum)
        sums_ref[...] = jnp.zeros_like(sums_ref)
        groups = gate_ref.shape[0]
        if halves:
            gate_rows[...] = gate_ref[...]
        else:
            rows = gate_rows.shape[0] // (2 * groups)
            for block in range(2 * groups):
                gate = gate_ref[block % groups : block % groups + 1]
                gate_rows[block * rows : (block + 1) * rows] = jnp.broadcast_to(gate, (rows, gate.shape[1]))

    arriving = cot_ref[...]
    if halves:
        arriving = jnp.where(step // halves == ctx_ref[0], arriving, other_ref[...])
    arriving = (arriving.astype(F32) * gate_rows[...]).astype(BF16)
    second = second_ref[...]
    hidden = dot(second, up_ref[...]) + bias_ref[...]
    gelu_out, slope = gelu_parts(hidden)
    gelu_low = gelu_out.astype(BF16)
    feed_ref[...] = dot(gelu_low, down_ref[...], ((1,), (1,))).astype(BF16)
    down_sum[...] += dot(arriving, gelu_low, ((0,), (0,)))
    pulled = (dot(arriving, down_ref[...]) * slope).astype(BF16)
    sums_ref[...] += jnp.sum(pulled.astype(F32), axis=0, keepdims=True)
    up_sum[...] += dot(second, pulled, ((0,), (0,)))
    pull_ref[...] = dot(pulled, up_ref[...], ((1,), (1,))).astype(BF16)

    @pl.when(step == pl.num_programs(0) - 1)
    def _():
        dw_ref[:, :wide] = up_sum[...].astype(BF16)
        dw_ref[:, wide:] = down_sum[...].astype(BF16)


def feed_forward(ctx, second, cot, other, gate, up, down, bias):
    (up, up_at), (down, down_at) = up, down
    (rows, width), wide, groups = second.shape, up.shape[2], gate.shape[0]
    if other is None:
        block_rows, halves, gate_rows = 2 * TEXT_SLOTS // 4 * groups, 0, 2 * TEXT_SLOTS // 4 * groups
        other, last = cot[:8], 0
        cot_spec = pl.BlockSpec((block_rows, width), lambda i, c: (i, 0))
        other_spec = pl.BlockSpec((8, width), lambda i, c: (0, 0))
    else:
        block_rows = min(QUERY_BLOCK, cot.shape[0])
        halves, gate_rows = cot.shape[0] // block_rows, 1
        last = halves - 1
        cot_spec = pl.BlockSpec((block_rows, width), lambda i, c: (jnp.clip(i - c[0] * halves, 0, last), 0))
        other_spec = pl.BlockSpec((block_rows, width), lambda i, c: (jnp.clip(i - (1 - c[0]) * halves, 0, last), 0))
    block = pl.BlockSpec((block_rows, width), lambda i, c: (i, 0))

    def once(shape):
        return pl.BlockSpec(shape, lambda i, c: (0, 0), pipeline_mode=pl.Buffered(1))

    flops = 12 * rows * width * wide
    return pl.pallas_call(
        functools.partial(feed_kernel, halves),
        grid_spec=pltpu.PrefetchScalarGridSpec(
            num_scalar_prefetch=1,
            grid=(rows // block_rows,),
            in_specs=[
                block,
                cot_spec,
                other_spec,
                once(gate.shape),
                pl.BlockSpec(
                    (None,) + up.shape[1:], lambda i, c: (up_at, 0, 0), pipeline_mode=pl.Buffered(1)
                ),
                pl.BlockSpec(
                    (None,) + down.shape[1:], lambda i, c: (down_at, 0, 0), pipeline_mode=pl.Buffered(1)
                ),
                once((1, wide)),
            ],
            out_specs=[
                block,
                block,
                pl.BlockSpec((width, 2 * wide), lambda i, c: (0, 0)),
                pl.BlockSpec((1, wide), lambda i, c: (0, 0)),
            ],
            scratch_shapes=[pltpu.VMEM((width, wide), F32)] * 2 + [pltpu.VMEM((gate_rows, width), F32)],
        ),
        out_shape=[
            jax.ShapeDtypeStruct((rows, width), BF16),
            jax.ShapeDtypeStruct((rows, width), BF16),
            jax.ShapeDtypeStruct((width, 2 * wide), BF16),
            jax.ShapeDtypeStruct((1, wide), F32),
        ],
        compiler_params=pltpu.CompilerParams(vmem_limit_bytes=VMEM_LIMIT),
        cost_estimate=pl.CostEstimate(flops=flops, bytes_accessed=flops // 256, transcendentals=0),
        name="feed_forward",
    )(ctx, second, cot, other, gate, up, down, bias.reshape(1, wide))


def feed_moving_kernel(
    groups,
    halves,
    second_ref,
    own_ref,
    other_ref,
    gate_ref,
    up_ref,
    down_ref,
    bias_ref,
    moved_ref,
    feed_ref,
    pull_ref,
    dw_ref,
    sums_ref,
    moved_out,
    up_sum,
    down_sum,
    local_sem,
    send_sems,
    recv_sems,
):
    step = pl.program_id(0)
    dp, x, tp = lax.axis_index("dp"), lax.axis_index("ctx"), lax.axis_index("tp")
    wide = up_ref.shape[1]
    block_rows = second_ref.shape[0]
    count = groups * 2
    me = dp * 2 + x
    peers = [lax.rem(me + offset, count) for offset in range(1, count)]
    devices = [(peer // 2, peer % 2, tp) for peer in peers]
    local = pltpu.make_async_copy(moved_ref.at[me], moved_out.at[me], local_sem)
    moves = [
        pltpu.make_async_remote_copy(
            src_ref=moved_ref.at[peer],
            dst_ref=moved_out.at[me],
            send_sem=send_sems.at[i],
            recv_sem=recv_sems.at[i],
            device_id=device,
            device_id_type=MESH,
        )
        for i, (peer, device) in enumerate(zip(peers, devices))
    ]

    @pl.when(step == 0)
    def _():
        barrier = pltpu.get_barrier_semaphore()
        for device in devices:
            pl.semaphore_signal(barrier, inc=1, device_id=device, device_id_type=MESH)
        pl.semaphore_wait(barrier, len(devices))
        local.start()
        for move in moves:
            move.start()
        up_sum[...] = jnp.zeros_like(up_sum)
        down_sum[...] = jnp.zeros_like(down_sum)
        sums_ref[...] = jnp.zeros_like(sums_ref)

    rows = pl.ds(pl.multiple_of(lax.rem(step, halves) * block_rows, block_rows), block_rows)
    arriving = jnp.where(step // halves == x, own_ref[rows], other_ref[rows])
    arriving = (arriving.astype(F32) * gate_ref[...]).astype(BF16)
    second = second_ref[...]
    hidden = dot(second, up_ref[...]) + bias_ref[...]
    gelu_out, slope = gelu_parts(hidden)
    gelu_low = gelu_out.astype(BF16)
    feed_ref[...] = dot(gelu_low, down_ref[...], ((1,), (1,))).astype(BF16)
    down_sum[...] += dot(arriving, gelu_low, ((0,), (0,)))
    pulled = (dot(arriving, down_ref[...]) * slope).astype(BF16)
    sums_ref[...] += jnp.sum(pulled.astype(F32), axis=0, keepdims=True)
    up_sum[...] += dot(second, pulled, ((0,), (0,)))
    pull_ref[...] = dot(pulled, up_ref[...], ((1,), (1,))).astype(BF16)

    @pl.when(step == pl.num_programs(0) - 1)
    def _():
        dw_ref[:, :wide] = up_sum[...].astype(BF16)
        dw_ref[:, wide:] = down_sum[...].astype(BF16)
        local.wait()
        for move in moves:
            move.wait()


def feed_forward_moving(groups, second, own, other, gate, up, down, bias, moved):
    (up, up_at), (down, down_at) = up, down
    (rows, width), wide = second.shape, up.shape[2]
    block_rows = min(QUERY_BLOCK, own.shape[0])
    block = stepped((block_rows, width))
    peers = 2 * groups - 1

    def weight(shape, place):
        return pl.BlockSpec((None,) + shape[1:], lambda i: (place, 0, 0), pipeline_mode=pl.Buffered(1))

    return pl.pallas_call(
        functools.partial(feed_moving_kernel, groups, own.shape[0] // block_rows),
        grid=(rows // block_rows,),
        in_specs=[
            block,
            fixed(own.shape),
            fixed(other.shape),
            fixed(gate.shape),
            weight(up.shape, up_at),
            weight(down.shape, down_at),
            fixed((1, wide)),
            pl.BlockSpec(memory_space=pl.ANY),
        ],
        out_specs=[
            block,
            block,
            pl.BlockSpec((width, 2 * wide), lambda i: (0, 0)),
            pl.BlockSpec((1, wide), lambda i: (0, 0)),
            pl.BlockSpec(memory_space=pl.ANY),
        ],
        out_shape=[
            jax.ShapeDtypeStruct((rows, width), BF16),
            jax.ShapeDtypeStruct((rows, width), BF16),
            jax.ShapeDtypeStruct((width, 2 * wide), BF16),
            jax.ShapeDtypeStruct((1, wide), F32),
            jax.ShapeDtypeStruct(moved.shape, BF16),
        ],
        scratch_shapes=[pltpu.VMEM((width, wide), F32)] * 2
        + [
            pltpu.SemaphoreType.DMA(()),
            pltpu.SemaphoreType.DMA((peers,)),
            pltpu.SemaphoreType.DMA((peers,)),
        ],
        compiler_params=pltpu.CompilerParams(
            collective_id=5, has_side_effects=True, vmem_limit_bytes=VMEM_LIMIT
        ),
        name="feed_moving",
    )(second, own, other, gate, up, down, bias.reshape(1, wide), moved)


def place_feed_kernel(ctx_ref, mine_ref, other_ref, moved_ref, up_ref, down_ref):
    ctx = ctx_ref[0]
    cols = mine_ref.shape[2] // 2
    text_cols = moved_ref.shape[2] // 2
    groups = moved_ref.shape[0] // 2

    def place(span):
        kept, other = mine_ref[ctx, span], other_ref[span]
        for c in range(2):
            part = jnp.where(ctx == c, kept, other).astype(F32)
            up_ref[0, span, c * cols : (c + 1) * cols] = part[:, :cols]
            down_ref[0, span, c * cols : (c + 1) * cols] = part[:, cols:]
            for group in range(groups):
                start = c * cols + group * text_cols
                text = moved_ref[group * 2 + c, span].astype(F32)
                up_ref[1, span, start : start + text_cols] = text[:, :text_cols]
                down_ref[1, span, start : start + text_cols] = text[:, text_cols:]

    over_rows(other_ref.shape[0], place)


def place_feed(ctx, mine, other, moved):
    rows, cols = other.shape
    shape = jax.ShapeDtypeStruct((2, rows, cols), F32)
    return pl.pallas_call(
        place_feed_kernel,
        in_specs=[pl.BlockSpec(memory_space=pltpu.SMEM)] + [pl.BlockSpec(memory_space=pltpu.VMEM)] * 3,
        out_specs=[pl.BlockSpec(memory_space=pltpu.VMEM)] * 2,
        out_shape=[shape, shape],
        compiler_params=pltpu.CompilerParams(vmem_limit_bytes=VMEM_LIMIT),
        name="place_feed",
    )(ctx, mine.reshape(2, rows, cols), other, moved)


def place_tokens_kernel(image_out, text_out, image_grad, text_grad, *outs):
    for source, place in zip((image_out, image_grad), outs[::2]):
        rows = source.shape[1]
        for block in range(source.shape[0]):
            place[0, block * rows : (block + 1) * rows] = source[block]
    for source, place in zip((text_out, text_grad), outs[1::2]):
        rows, length = source.shape[1], place.shape[1]
        for block in range(source.shape[0]):
            used = min(rows, length - block * rows)
            place[0, block * rows : block * rows + used] = source[block, :used]


def place_tokens(parts, image_length, text_length):
    shapes = [
        jax.ShapeDtypeStruct((1, length, parts[0].shape[2]), BF16) for length in (image_length, text_length) * 2
    ]
    return pl.pallas_call(
        place_tokens_kernel,
        in_specs=[pl.BlockSpec(memory_space=pltpu.VMEM)] * 4,
        out_specs=[pl.BlockSpec(memory_space=pltpu.VMEM)] * 4,
        out_shape=shapes,
        compiler_params=pltpu.CompilerParams(vmem_limit_bytes=VMEM_LIMIT),
        name="place_tokens",
    )(*parts)


def place_heads_kernel(kinds, ctx_ref, mine_ref, other_ref, out_ref):
    ctx = ctx_ref[0]
    half = out_ref.shape[3] // 2

    def place(span):
        kept, other = mine_ref[ctx, span], other_ref[span]
        for c in range(2):
            part = jnp.where(ctx == c, kept, other).astype(F32)
            for s in range(2):
                for j in range(kinds):
                    start = (kinds * s + j) * half
                    out_ref[s, j, span, c * half : (c + 1) * half] = part[:, start : start + half]

    over_rows(other_ref.shape[0], place)


def place_heads(kinds, ctx, mine, other):
    rows, cols = other.shape
    return pl.pallas_call(
        functools.partial(place_heads_kernel, kinds),
        in_specs=[pl.BlockSpec(memory_space=pltpu.SMEM)] + [pl.BlockSpec(memory_space=pltpu.VMEM)] * 2,
        out_specs=pl.BlockSpec(memory_space=pltpu.VMEM),
        out_shape=jax.ShapeDtypeStruct((2, kinds, rows, cols // kinds), F32),
        compiler_params=pltpu.CompilerParams(vmem_limit_bytes=VMEM_LIMIT),
        name="place_heads",
    )(ctx, mine.reshape(2, rows, cols), other)


def place_all_kernel(ctx_ref, out_mine, out_other, ffn_mine, ffn_other, moved, *rest):
    tokens, (out_ref, up_ref, down_ref), placed = rest[:4], rest[4:7], rest[7:]
    place_heads_kernel(1, ctx_ref, out_mine, out_other, out_ref)
    place_feed_kernel(ctx_ref, ffn_mine, ffn_other, moved, up_ref, down_ref)
    place_tokens_kernel(*tokens, *placed)


def place_all(ctx, out_mine, out_other, ffn_mine, ffn_other, moved, tokens, image_length, text_length):
    rows, out_cols = out_other.shape
    cols = ffn_other.shape[1]
    vmem = pl.BlockSpec(memory_space=pltpu.VMEM)
    out, up, down, *placed = pl.pallas_call(
        place_all_kernel,
        in_specs=[pl.BlockSpec(memory_space=pltpu.SMEM)] + [vmem] * 9,
        out_specs=[vmem] * 7,
        out_shape=[
            jax.ShapeDtypeStruct((2, 1, rows, out_cols), F32),
            jax.ShapeDtypeStruct((2, rows, cols), F32),
            jax.ShapeDtypeStruct((2, rows, cols), F32),
        ]
        + [jax.ShapeDtypeStruct((1, n, tokens[0].shape[2]), BF16) for n in (image_length, text_length) * 2],
        compiler_params=pltpu.CompilerParams(vmem_limit_bytes=VMEM_LIMIT),
        name="place_all",
    )(ctx, out_mine.reshape(2, rows, out_cols), out_other, ffn_mine.reshape(2, rows, cols), ffn_other, moved, *tokens)
    return out[:, 0], up, down, placed


def place_qkv(ctx, mine, other):
    return place_heads(3, ctx, mine, other).transpose(0, 2, 1, 3)


def place_out(ctx, mine, other):
    return place_heads(1, ctx, mine, other)[:, 0]


def normalise(inputs):
    centred = inputs - jnp.mean(inputs, axis=-1, keepdims=True)
    spread = lax.rsqrt(jnp.mean(centred * centred, axis=-1, keepdims=True) + 1e-06)
    return centred * spread, spread


def normalise_back(grad_norm, norm, spread):
    return spread * (
        grad_norm
        - jnp.mean(grad_norm, axis=-1, keepdims=True)
        - norm * jnp.mean(grad_norm * norm, axis=-1, keepdims=True)
    )


def gelu_parts(hidden):
    root = 0.7978845608028654
    square = hidden * hidden
    bent = jnp.tanh(hidden * (root + root * 0.044715 * square))
    half = 0.5 * (1.0 + bent)
    slope = half + 0.5 * hidden * (1.0 - bent * bent) * (root + 3.0 * root * 0.044715 * square)
    return hidden * half, slope


MESH = pl.DeviceIdType.MESH
VMEM_SPEC = pl.BlockSpec(memory_space=pltpu.VMEM)
ANY_SPEC = pl.BlockSpec(memory_space=pl.ANY)


class Wires:
    def __init__(self, send_sems, recv_sems):
        self.dp, self.x, self.tp = lax.axis_index("dp"), lax.axis_index("ctx"), lax.axis_index("tp")
        self.y, self.k = self.tp // 2, self.tp % 2
        self.x_next = (self.dp, 1 - self.x, self.tp)
        self.y_next = (self.dp, self.x, (1 - self.y) * 2 + self.k)
        self.k_next = (self.dp, self.x, self.y * 2 + 1 - self.k)
        self.send_sems, self.recv_sems, self.used = send_sems, recv_sems, 0
        self.started = []

    def copy(self, source, target, device):
        wire = pltpu.make_async_remote_copy(
            src_ref=source,
            dst_ref=target,
            send_sem=self.send_sems.at[self.used],
            recv_sem=self.recv_sems.at[self.used],
            device_id=device,
            device_id_type=MESH,
        )
        self.used += 1
        wire.start()
        self.started.append(wire)
        return wire

    def meet(self, devices):
        barrier = pltpu.get_barrier_semaphore()
        for device in devices:
            pl.semaphore_signal(barrier, inc=1, device_id=device, device_id_type=MESH)
        pl.semaphore_wait(barrier, len(devices))

    def finish(self):
        for wire in self.started:
            wire.wait_send()


def row_step(rows):
    return 32 if rows % 32 == 0 else rows


def over_rows(rows, body):
    step = row_step(rows)
    if step == rows:
        body(slice(0, rows))
        return

    def one(index, carry):
        body(pl.ds(pl.multiple_of(index * step, step), step))
        return carry

    lax.fori_loop(0, rows // step, one, 0)


def reduce_first(wires, s):
    return wires.copy(s["part"].at[:, :, 1 - wires.k], s["core"], wires.k_next)


def reduce_add(wires, s, arrived):
    k = wires.k
    part, core, held = s["part"], s["core"], s["held"]
    arrived.wait_recv()
    for i in range(2):
        for j in range(2):

            def add(span, i=i, j=j):
                held[i, j, span] = (part[i, j, k, span].astype(F32) + core[i, j, span].astype(F32)).astype(BF16)

            over_rows(part.shape[3], add)


def reduce_second(wires, s):
    held = s["held"]
    cut = held.shape[3] // 2
    return (
        wires.copy(held.at[:, 1 - wires.y, :, pl.ds(0, cut)], s["along_y"], wires.y_next),
        wires.copy(held.at[1 - wires.x, :, :, pl.ds(cut, cut)], s["along_x"], wires.x_next),
    )


def reduce_third(wires, s, second):
    x, y = wires.x, wires.y
    held, along_y, along_x, out_x, out_y = s["held"], s["along_y"], s["along_x"], s["out_x"], s["out_y"]
    cut = held.shape[3] // 2
    for arrived in second:
        arrived.wait_recv()

    def add(span):
        out_x[span] = (held[1 - x, y, span, :cut].astype(F32) + along_y[1 - x, span].astype(F32)).astype(BF16)
        out_y[span] = (held[x, 1 - y, span, cut:].astype(F32) + along_x[1 - y, span].astype(F32)).astype(BF16)

    over_rows(held.shape[2], add)
    return (
        wires.copy(out_x, s["last_x"], wires.x_next),
        wires.copy(out_y, s["last_y"], wires.y_next),
    )


def reduce_last(wires, s, third):
    x, y = wires.x, wires.y
    held, along_y, along_x, last_x, last_y, total = (
        s["held"],
        s["along_y"],
        s["along_x"],
        s["last_x"],
        s["last_y"],
        s["total"],
    )
    cut = held.shape[3] // 2
    for arrived in third:
        arrived.wait_recv()

    def add(span):
        total[span, :cut] = (
            held[x, y, span, :cut].astype(F32) + along_y[x, span].astype(F32) + last_x[span].astype(F32)
        )
        total[span, cut:] = (
            held[x, y, span, cut:].astype(F32) + along_x[y, span].astype(F32) + last_y[span].astype(F32)
        )

    over_rows(held.shape[2], add)


def reduce_plane(wires, streams):
    first = [reduce_first(wires, s) for s in streams]
    second = []
    for s, arrived in zip(streams, first):
        reduce_add(wires, s, arrived)
        second.append(reduce_second(wires, s))
    third = [reduce_third(wires, s, arrived) for s, arrived in zip(streams, second)]
    for s, arrived in zip(streams, third):
        reduce_last(wires, s, arrived)


REDUCE_KEYS = ("core", "held", "along_y", "along_x", "out_x", "out_y", "last_x", "last_y", "total")


def reduce_scratch(rows, width):
    half = width // 2
    return [
        pltpu.VMEM((2, 2, rows, width), BF16),
        pltpu.VMEM((2, 2, rows, width), BF16),
        pltpu.VMEM((2, rows, half), BF16),
        pltpu.VMEM((2, rows, half), BF16),
        pltpu.VMEM((rows, half), BF16),
        pltpu.VMEM((rows, half), BF16),
        pltpu.VMEM((rows, half), BF16),
        pltpu.VMEM((rows, half), BF16),
        pltpu.VMEM((rows, width), F32),
    ]


def block_halves(block):
    cut = block.shape[-1] // 2
    inner = (slice(None),) * (len(block.shape) - 4)
    return inner + (pl.ds(0, cut),), inner + (pl.ds(cut, cut),)


def spread_first(wires, block):
    x, y, k = wires.x, wires.y, wires.k
    low, high = block_halves(block)
    mine = block.at[(x, y, k) + low], block.at[(x, y, k) + high]
    return wires.copy(mine[0], mine[0], wires.x_next), wires.copy(mine[1], mine[1], wires.y_next)


def spread_second(wires, block, first):
    x, y, k = wires.x, wires.y, wires.k
    low, high = block_halves(block)
    for arrived in first:
        arrived.wait_recv()
    lows, highs = block.at[(slice(None), y, k) + low], block.at[(x, slice(None), k) + high]
    return wires.copy(lows, lows, wires.y_next), wires.copy(highs, highs, wires.x_next)


def spread_third(wires, block, second):
    for arrived in second:
        arrived.wait_recv()
    gathered = block.at[:, :, wires.k]
    return wires.copy(gathered, gathered, wires.k_next)


def spread_plane(wires, blocks, started=()):
    first = list(started) + [spread_first(wires, block) for block in blocks[len(started) :]]
    second = [spread_second(wires, block, arrived) for block, arrived in zip(blocks, first)]
    third = [spread_third(wires, block, arrived) for block, arrived in zip(blocks, second)]
    for arrived in third:
        arrived.wait_recv()


def comm_call(kernel, outs, scratch, wires, collective_id, name, in_specs, out_specs):
    return pl.pallas_call(
        kernel,
        out_shape=outs,
        in_specs=in_specs,
        out_specs=out_specs,
        scratch_shapes=scratch + [pltpu.SemaphoreType.DMA((wires,)), pltpu.SemaphoreType.DMA((wires,))],
        compiler_params=pltpu.CompilerParams(
            collective_id=collective_id, has_side_effects=True, vmem_limit_bytes=VMEM_LIMIT
        ),
        name=name,
    )


def enter_kernel(
    n_dp,
    groups,
    part_ref,
    bias_ref,
    rows_ref,
    image_ref,
    text_ref,
    attn_ref,
    up_ref,
    down_ref,
    mod_ref,
    rows_out,
    image_out,
    text_out,
    gates_out,
    attn_out,
    ffn_out,
    moved_out,
    mod_in,
    send_sems,
    recv_sems,
):
    wires = Wires(send_sems, recv_sems)
    dp, x, y, k, tp = wires.dp, wires.x, wires.y, wires.k, wires.tp
    count = n_dp * 2
    me = dp * 2 + x
    peers = [lax.rem(me + offset, count) for offset in range(1, count)]
    others = [(peer // 2, peer % 2, tp) for peer in peers]
    lanes = [lax.rem(tp + offset, 4) for offset in range(1, 4)]
    z_next = (lax.rem(dp + 1, n_dp), x, tp)
    wires.meet(others + [(dp, x, lane) for lane in lanes])

    sums = [wires.copy(part_ref.at[peer // 2], mod_in.at[me], other) for peer, other in zip(peers, others)]
    rows = [wires.copy(rows_ref, rows_out.at[me], other) for other in others]
    swaps = [wires.copy(attn_ref.at[1 - x, s], attn_out.at[s, dp, x], wires.x_next) for s in range(2)]
    mod_in[me] = part_ref[dp]
    rows_out[me] = rows_ref[...]
    for arrived in sums:
        arrived.wait_recv()
    ring = {(s, 0): wires.copy(attn_ref.at[x, s], attn_out.at[s, dp, x], z_next) for s in range(2)}
    total = bias_ref[...]
    for source in range(count):
        total = total + mod_in[source]
    mod_ref[tp] = total
    mods = [wires.copy(mod_ref.at[tp], mod_ref.at[tp], (dp, x, lane)) for lane in lanes]
    for arrived in mods:
        arrived.wait_recv()
    gates = []
    if groups > 1:
        gates = [
            wires.copy(mod_ref.at[:, 11], gates_out.at[dp], (lax.rem(dp + offset, groups), x, tp))
            for offset in range(1, groups)
        ]
        for lane in range(4):
            gates_out[dp, lane] = mod_ref[lane, 11]

    def pass_on(turn, side):
        for s in range(2):
            ring[s, side].wait_recv()
            if turn < n_dp - 1:
                origin = lax.rem(dp + n_dp - turn, n_dp)
                block = attn_out.at[s, origin, x if side == 0 else 1 - x]
                ring[s, side] = wires.copy(block, block, z_next)

    streams = ((image_ref, image_out), (text_ref, text_out))
    cols = ffn_out.shape[3]
    wide = ffn_out.shape[0] // 2
    held = []
    for i, weight in enumerate((up_ref, down_ref)):
        for s in range(wide):
            given = weight.at[s, :, pl.ds(pl.multiple_of((1 - x) * cols, cols), cols)]
            held.append((given, ffn_out.at[i * wide + s, x]))
    for s, arrived in enumerate(swaps):
        arrived.wait_recv()
        block = attn_out.at[s, dp, 1 - x]
        ring[s, 1] = wires.copy(block, block, z_next)
    along_x = [wires.copy(ref.at[tp], out.at[x, tp], wires.x_next) for ref, out in streams]
    pass_on(1, 0)
    along_y = []
    for (_, out), arrived in zip(streams, along_x):
        arrived.wait_recv()
        block = out.at[1 - x, tp]
        along_y.append(wires.copy(block, block, wires.y_next))
    across = []
    for _, out in streams:
        block = out.at[1 - x, tp]
        across.append(wires.copy(block, block, wires.k_next))
    later = [wires.copy(given, place, wires.x_next) for given, place in held]

    def keep_tokens(span):
        for block in range(4):
            image_out[x, block, span] = image_ref[block, span]

    def keep_weights(span):
        for s in range(2):
            attn_out[s, dp, x, span] = attn_ref[x, s, span]
        for i, weight in enumerate((up_ref, down_ref)):
            for s in range(wide):
                first, last = weight[s, span, :cols], weight[s, span, cols:]
                ffn_out[i * wide + s, x, span] = jnp.where(x == 0, first, last)
            if groups > 1:
                text_cols = cols // groups
                for peer in range(count):
                    start = (peer % 2) * cols + (peer // 2) * text_cols
                    text = weight[1, span, start : start + text_cols]
                    moved_out[peer, span, i * text_cols : (i + 1) * text_cols] = text

    over_rows(image_ref.shape[1], keep_tokens)
    over_rows(attn_ref.shape[2], keep_weights)
    for block in range(4):
        text_out[x, block] = text_ref[block]
    pass_on(1, 1)
    far = (1 - y) * 2 + k
    for (_, out), arrived in zip(streams, along_y):
        arrived.wait_recv()
        block = out.at[1 - x, far]
        across.append(wires.copy(block, block, wires.k_next))
    for turn in range(2, n_dp - 1):
        pass_on(turn, 0)
        pass_on(turn, 1)
    if n_dp > 2:
        pass_on(n_dp - 1, 0)
        pass_on(n_dp - 1, 1)
    for arrived in rows + across + later + gates:
        arrived.wait_recv()
    wires.finish()


def enter(groups, partial_mod, ada_bias, bias_rows, image, text, attn, up, down, wide):
    n_dp, kinds, slice_width = partial_mod.shape
    count = 2 * n_dp
    rows, cols = up.shape[1], up.shape[2] // 2
    width = image.shape[2]
    return comm_call(
        functools.partial(enter_kernel, n_dp, groups),
        [
            jax.ShapeDtypeStruct((4, kinds, slice_width), F32),
            jax.ShapeDtypeStruct((count,) + bias_rows.shape, F32),
            jax.ShapeDtypeStruct((2,) + image.shape, BF16),
            jax.ShapeDtypeStruct((2,) + text.shape, BF16),
            jax.ShapeDtypeStruct((groups, 4, slice_width), F32),
            jax.ShapeDtypeStruct((2, n_dp, 2) + attn.shape[2:], BF16),
            jax.ShapeDtypeStruct((2 * wide, 2, rows, cols), BF16),
            jax.ShapeDtypeStruct((2 * groups, rows, 2 * cols // groups) if groups > 1 else (1, 8, 128), BF16),
        ],
        [pltpu.VMEM((count, kinds, slice_width), F32)],
        2 * (count - 1) + 2 + 4 * n_dp + 16 + groups + 5,
        0,
        "enter",
        [VMEM_SPEC] * 8,
        [VMEM_SPEC] * 8,
    )(partial_mod, ada_bias, bias_rows, image, text, attn, up, down)


def meet_planes(wires, groups):
    planes = [(lax.rem(wires.dp + offset, groups), wires.x, wires.tp) for offset in range(1, groups)]
    wires.meet(planes + [wires.x_next, wires.y_next, wires.k_next])


def meet_groups(wires, groups, more=()):
    dp, x, tp = wires.dp, wires.x, wires.tp
    count = groups * 2
    if groups == 1:
        others = [wires.x_next]
    else:
        peers = [lax.rem(dp * 2 + x + offset, count) for offset in range(1, count)]
        others = [(peer // 2, peer % 2, tp) for peer in peers]
    wires.meet(others + [wires.y_next, wires.k_next, *more])


def start_moves(wires, groups, moved_ref, moved_out, local_sem):
    if groups == 1:
        return []
    dp, x, tp = wires.dp, wires.x, wires.tp
    count = groups * 2
    me = dp * 2 + x
    peers = [lax.rem(me + offset, count) for offset in range(1, count)]
    local = pltpu.make_async_copy(moved_ref.at[me], moved_out.at[me], local_sem)
    local.start()
    return [local] + [
        wires.copy(moved_ref.at[peer], moved_out.at[me], (peer // 2, peer % 2, tp)) for peer in peers
    ]


def end_moves(moves):
    if moves:
        moves[0].wait()
    for arrived in moves[1:]:
        arrived.wait_recv()


def middle_kernel(
    n_dp,
    groups,
    image_part,
    text_part,
    image_x,
    text_x,
    mod_ref,
    bias_ref,
    moved_ref,
    *rest,
):
    ffn_refs = rest[: n_dp - 1]
    (
        cot_ref,
        image_attention,
        text_attention,
        image_middle,
        text_middle,
        image_all,
        text_all,
        cots_all,
        moved_out,
        ffn_out,
    ) = rest[n_dp - 1 : n_dp + 9]
    scratch = rest[n_dp + 9 :]
    local_sem, send_sems, recv_sems = scratch[-3:]
    wires = Wires(send_sems, recv_sems)
    dp, x, y, k, tp = wires.dp, wires.x, wires.y, wires.k, wires.tp
    z_next = (lax.rem(dp + 1, n_dp), x, tp)
    meet_groups(wires, groups, [z_next] if groups == 1 else [])
    cots = []
    if groups > 1:
        cots_all[x, y, k, dp] = cot_ref[...]
        for offset in range(1, groups):
            block = cots_all.at[x, y, k, dp]
            cots.append(wires.copy(block, block, (lax.rem(dp + offset, groups), x, tp)))
    last = wires.copy(ffn_refs[n_dp - 2], ffn_out.at[:, lax.rem(dp + 2, n_dp)], z_next)
    size = len(REDUCE_KEYS)
    streams = [
        dict(zip(("part",) + REDUCE_KEYS, (part,) + scratch[i * size : (i + 1) * size]))
        for i, part in enumerate((image_part, text_part))
    ]

    def keep(span):
        for turn, block in enumerate(ffn_refs):
            for i in range(block.shape[0]):
                ffn_out[i, lax.rem(dp + n_dp - turn, n_dp), span] = block[i, span]

    image, text = streams
    first = reduce_first(wires, text), reduce_first(wires, image)
    reduce_add(wires, text, first[0])
    text_second = reduce_second(wires, text)
    reduce_add(wires, image, first[1])
    image_second = reduce_second(wires, image)
    for arrived in cots:
        arrived.wait_recv()
    if groups > 1:
        cots_first = spread_first(wires, cots_all)
    text_third = reduce_third(wires, text, text_second)
    image_third = reduce_third(wires, image, image_second)

    def second_rows(i, tokens, attention, middle, gathered):
        total = streams[i]["total"]

        def finish(span):
            branch = total[span] + bias_ref[i]
            attention[span] = branch
            value = tokens[span].astype(F32) + mod_ref[i, 2] * branch
            middle[span] = value
            norm, _ = normalise(value)
            gathered[x, y, k, span] = (norm * (1.0 + mod_ref[i, 4]) + mod_ref[i, 3]).astype(BF16)

        over_rows(total.shape[0], finish)

    reduce_last(wires, text, text_third)
    second_rows(1, text_x, text_attention, text_middle, text_all.at[:, :, :, dp if groups > 1 else 0])
    zs = []
    for offset in range(1, groups):
        block = text_all.at[x, y, k, dp]
        zs.append(wires.copy(block, block, (lax.rem(dp + offset, groups), x, tp)))
    if groups > 1:
        cots_second = spread_second(wires, cots_all, cots_first)
    reduce_last(wires, image, image_third)
    second_rows(0, image_x, image_attention, image_middle, image_all)
    image_first = spread_first(wires, image_all)
    for arrived in zs:
        arrived.wait_recv()
    text_first = spread_first(wires, text_all)
    moves = start_moves(wires, groups, moved_ref, moved_out, local_sem)
    thirds = [spread_third(wires, cots_all, cots_second)] if groups > 1 else []
    over_rows(ffn_out.shape[2], keep)
    image_next = spread_second(wires, image_all, image_first)
    text_next = spread_second(wires, text_all, text_first)
    thirds += [spread_third(wires, image_all, image_next), spread_third(wires, text_all, text_next)]
    for arrived in thirds:
        arrived.wait_recv()
    end_moves(moves)
    last.wait_recv()
    wires.finish()


def middle_step(groups, image_part, text_part, image_x, text_x, mod, bias, moved, ffn, cot):
    (image_rows, width), text_rows = image_x.shape, text_x.shape[0]
    outs = []
    for _ in range(2):
        outs += [jax.ShapeDtypeStruct((rows, width), F32) for rows in (image_rows, text_rows)]
    outs += [jax.ShapeDtypeStruct(image_part.shape, BF16)]
    outs += [jax.ShapeDtypeStruct((2, 2, 2, groups, text_rows, width), BF16)] * 2
    outs += [jax.ShapeDtypeStruct(moved.shape, BF16)]
    n_dp = len(ffn) + 1
    outs += [jax.ShapeDtypeStruct((ffn[0].shape[0], n_dp) + ffn[0].shape[1:], BF16)]
    return comm_call(
        functools.partial(middle_kernel, n_dp, groups),
        outs,
        reduce_scratch(image_rows, width) + reduce_scratch(text_rows, width) + [pltpu.SemaphoreType.DMA(())],
        30 + 4 * groups,
        1,
        "middle",
        [VMEM_SPEC] * 6 + [ANY_SPEC] + [VMEM_SPEC] * n_dp,
        [VMEM_SPEC] * 7 + [ANY_SPEC, VMEM_SPEC],
    )(image_part, text_part, image_x, text_x, mod, bias, moved, *ffn, cot)


def turn_kernel(
    groups,
    valid_ref,
    image_feed,
    text_feed,
    image_second,
    text_second,
    image_attention,
    text_attention,
    image_middle,
    text_middle,
    image_cot,
    text_cot,
    mod_ref,
    bias_ref,
    image_out,
    text_out,
    image_grad,
    text_grad,
    sums_ref,
    image_all,
    text_all,
    *scratch,
):
    z_out, z_in, send_sems, recv_sems = scratch[-4:]
    wires = Wires(send_sems, recv_sems)
    dp, x, y, k, tp = wires.dp, wires.x, wires.y, wires.k, wires.tp
    meet_planes(wires, groups)
    size = len(REDUCE_KEYS)
    streams = [
        dict(zip(("part",) + REDUCE_KEYS, (part,) + scratch[i * size : (i + 1) * size]))
        for i, part in enumerate((text_second, text_feed, image_second, image_feed))
    ]
    pulls, feeds = (streams[2], streams[0]), (streams[3], streams[1])
    order = [pulls[1], pulls[0], feeds[1], feeds[0]]
    rows = text_middle.shape[0]

    def to_planes(i, total):
        copies = []
        if groups > 1:
            for group in range(groups):
                z_out[i, group] = total[group * rows : (group + 1) * rows].astype(BF16)
            z_in[i, dp] = z_out[i, dp]
            for offset in range(1, groups):
                plane = lax.rem(dp + offset, groups)
                copies.append(wires.copy(z_out.at[i, plane], z_in.at[i, dp], (plane, x, tp)))
        return copies

    def from_planes(i, total, copies):
        for arrived in copies:
            arrived.wait_recv()
        if groups > 1:
            summed = z_in[i, 0].astype(F32)
            for group in range(1, groups):
                summed = summed + z_in[i, group].astype(F32)
            total[0:rows] = summed

    sums_ref[...] = jnp.zeros_like(sums_ref)
    sides = (
        (image_attention, image_middle, image_cot, image_out, image_grad, image_all),
        (text_attention, text_middle, text_cot, text_out, text_grad, text_all),
    )

    def add_sums(i, start, terms):
        for t, term in enumerate(terms):
            sums_ref[i, start + t : start + t + 1] += jnp.sum(term, axis=0, keepdims=True)

    def pull_side(i):
        attention, middle, cot, _, grad, gathered = sides[i]
        total = pulls[i]["total"]

        def finish(span):
            branch, value, arriving, pulled = attention[span], middle[span], cot[span].astype(F32), total[span]
            norm, spread = normalise(value)
            grad_middle = arriving + normalise_back(pulled * (1.0 + mod_ref[i, 4]), norm, spread)
            grad[span] = grad_middle
            low = (grad_middle * mod_ref[i, 2]).astype(BF16)
            gathered[x, y, k, span] = low
            add_sums(i, 0, (grad_middle * branch, pulled, pulled * norm))
            add_sums(i, 5, (low.astype(F32),))

        over_rows(middle.shape[0], finish)

    def feed_side(i):
        attention, middle, cot, out, _, _ = sides[i]
        total = feeds[i]["total"]

        def finish(span):
            branch, value, arriving = attention[span], middle[span], cot[span].astype(F32)
            fed = total[span] + bias_ref[i]
            gated_branch = mod_ref[i, 2] * branch
            gated_feed = mod_ref[i, 5] * fed
            result = value + gated_feed
            out[span] = result.astype(BF16)
            if i == 1:
                kept = valid_ref[span]
                result, gated_branch, gated_feed = result * kept, gated_branch * kept, gated_feed * kept
            own_feed = (arriving * mod_ref[i, 5]).astype(BF16).astype(F32)
            add_sums(i, 3, (arriving * fed, own_feed))
            add_sums(i, 6, (result * result, gated_branch * gated_branch, gated_feed * gated_feed))

        over_rows(middle.shape[0], finish)

    first = [reduce_first(wires, s) for s in order]
    pull_second = []
    for s, arrived in zip(order[:2], first[:2]):
        reduce_add(wires, s, arrived)
        pull_second.append(reduce_second(wires, s))
    for s, arrived in zip(order[2:], first[2:]):
        reduce_add(wires, s, arrived)
    pull_third = [reduce_third(wires, s, arrived) for s, arrived in zip(order[:2], pull_second)]
    feed_second = [reduce_second(wires, s) for s in order[2:]]
    reduce_last(wires, pulls[1], pull_third[0])
    planes = to_planes(0, pulls[1]["total"])
    reduce_last(wires, pulls[0], pull_third[1])
    pull_side(0)
    spread_one = [spread_first(wires, image_all)]
    from_planes(0, pulls[1]["total"], planes)
    pull_side(1)
    spread_one.append(spread_first(wires, text_all))
    feed_third = [reduce_third(wires, s, arrived) for s, arrived in zip(order[2:], feed_second)]
    spread_two = [spread_second(wires, block, arrived) for block, arrived in zip((image_all, text_all), spread_one)]
    reduce_last(wires, feeds[1], feed_third[0])
    planes = to_planes(1, feeds[1]["total"])
    reduce_last(wires, feeds[0], feed_third[1])
    spread_three = [spread_third(wires, block, arrived) for block, arrived in zip((image_all, text_all), spread_two)]
    feed_side(0)
    from_planes(1, feeds[1]["total"], planes)
    feed_side(1)
    for arrived in spread_three:
        arrived.wait_recv()
    wires.finish()


def turn_step(groups, valid, feeds, seconds, attentions, middles, cots, mod, bias):
    width = middles[0].shape[1]
    rows = [part.shape[0] for part in middles]
    outs = [jax.ShapeDtypeStruct((r, width), BF16) for r in rows]
    outs += [jax.ShapeDtypeStruct((r, width), F32) for r in rows]
    outs += [jax.ShapeDtypeStruct((2, 16, width), F32)]
    outs += [jax.ShapeDtypeStruct((2, 2, 2, r, width), BF16) for r in rows]
    scratch = []
    for r in (rows[1] * groups, rows[0]):
        scratch += reduce_scratch(r, width) + reduce_scratch(r, width)
    scratch += [pltpu.VMEM((2, groups, rows[1], width), BF16)] * 2
    return comm_call(
        functools.partial(turn_kernel, groups),
        outs,
        scratch,
        30 + 4 * groups,
        2,
        "turn",
        [VMEM_SPEC] * 13,
        [VMEM_SPEC] * 7,
    )(valid, *feeds, *seconds, *attentions, *middles, *cots, mod, bias)


PACKED = 24


def leave_kernel(
    n_dp,
    image_part,
    text_part,
    image_x,
    text_x,
    image_grad,
    text_grad,
    image_out,
    text_out,
    sums_ref,
    mod_ref,
    halves_ref,
    ffn_mine,
    out_mine,
    image_outs,
    text_outs,
    image_grads,
    text_grads,
    packed_out,
    halves_out,
    ffn_other,
    out_other,
    *scratch,
):
    send_sems, recv_sems = scratch[-2:]
    packed, packed_in, own_sums, both_halves, local_sums = scratch[-7:-2]
    wires = Wires(send_sems, recv_sems)
    dp, x, y, k, tp = wires.dp, wires.x, wires.y, wires.k, wires.tp
    me = x * 4 + tp
    peers = [lax.rem(me + offset, 8) for offset in range(1, 8)]
    planes = [lax.rem(dp + offset, n_dp) for offset in range(1, n_dp)]
    wires.meet([(dp, peer // 4, peer % 4) for peer in peers] + [(plane, x, tp) for plane in planes])

    image_outs[tp] = image_out[...]
    text_outs[tp] = text_out[...]
    both_halves[x] = halves_ref[...]
    halves = wires.copy(both_halves.at[x], both_halves.at[x], wires.x_next)
    size = len(REDUCE_KEYS)
    streams = [
        dict(zip(("part",) + REDUCE_KEYS, (part,) + scratch[i * size : (i + 1) * size]))
        for i, part in enumerate((image_part, text_part))
    ]
    reduce_plane(wires, streams)
    given = ffn_other.shape[0]
    given = pl.ds(pl.multiple_of((1 - x) * given, given), given)
    swaps = [
        wires.copy(mine.at[given], other, wires.x_next)
        for mine, other in ((ffn_mine, ffn_other), (out_mine, out_other))
    ]
    local_sums[...] = jnp.zeros_like(local_sums)
    for i, (tokens, grad, all_grads) in enumerate(
        ((image_x, image_grad, image_grads), (text_x, text_grad, text_grads))
    ):
        total = streams[i]["total"]

        def finish(span, i=i, tokens=tokens, grad=grad, all_grads=all_grads, total=total):
            pulled = total[span]
            norm, spread = normalise(tokens[span].astype(F32))
            grad_tokens = grad[span] + normalise_back(pulled * (1.0 + mod_ref[i, 1]), norm, spread)
            all_grads[tp, span] = grad_tokens.astype(BF16)
            local_sums[2 * i : 2 * i + 1] += jnp.sum(pulled, axis=0, keepdims=True)
            local_sums[2 * i + 1 : 2 * i + 2] += jnp.sum(pulled * norm, axis=0, keepdims=True)

        over_rows(total.shape[0], finish)
    wide = packed.shape[2]
    for t in range(4):
        cols = slice(t * wide, (t + 1) * wide)
        for i in range(2):
            packed[t, 6 * i : 6 * i + 2] = local_sums[2 * i : 2 * i + 2, cols]
            packed[t, 6 * i + 2 : 6 * i + 6] = sums_ref[i, 0:4, cols]
            packed[t, 12 + 5 * i : 12 + 5 * i + 5] = sums_ref[i, 4:9, cols]
        packed[t, 22:24] = jnp.zeros((2, wide), F32)
    packed_in[me] = packed[tp]
    gathers = [wires.copy(packed.at[peer % 4], packed_in.at[me], (dp, peer // 4, peer % 4)) for peer in peers]
    finals = (image_outs, text_outs, image_grads, text_grads)
    along_y = [wires.copy(final.at[tp], final.at[tp], wires.y_next) for final in finals]
    across = [wires.copy(final.at[tp], final.at[tp], wires.k_next) for final in finals]
    for arrived in gathers:
        arrived.wait_recv()
    total = packed_in[0]
    for source in range(1, 8):
        total = total + packed_in[source]
    own_sums[...] = total
    halves.wait_recv()
    for plane in planes:
        across.append(wires.copy(own_sums, packed_out.at[dp], (plane, x, tp)))
        across.append(wires.copy(both_halves, halves_out.at[dp], (plane, x, tp)))
    packed_out[dp] = total
    halves_out[dp] = both_halves[...]
    far = (1 - y) * 2 + k
    for final, arrived in zip(finals, along_y):
        arrived.wait_recv()
        across.append(wires.copy(final.at[far], final.at[far], wires.k_next))
    for arrived in across + swaps:
        arrived.wait_recv()
    wires.finish()


def leave_step(n_dp, parts, tokens, grads, outs_own, sums, mod, halves, ffn_mine, out_mine):
    width = tokens[0].shape[1]
    rows = [part.shape[0] for part in tokens]
    wide = width // 4
    outs = [jax.ShapeDtypeStruct((4, r, width), BF16) for r in rows] * 2
    outs += [
        jax.ShapeDtypeStruct((n_dp, PACKED, wide), F32),
        jax.ShapeDtypeStruct((n_dp, 2) + halves.shape, F32),
    ]
    outs += [jax.ShapeDtypeStruct((mine.shape[0] // 2, mine.shape[1]), BF16) for mine in (ffn_mine, out_mine)]
    scratch = []
    for r in rows:
        scratch += reduce_scratch(r, width)
    scratch += [
        pltpu.VMEM((4, PACKED, wide), F32),
        pltpu.VMEM((8, PACKED, wide), F32),
        pltpu.VMEM((PACKED, wide), F32),
        pltpu.VMEM((2,) + halves.shape, F32),
        pltpu.VMEM((8, width), F32),
    ]
    return comm_call(
        functools.partial(leave_kernel, n_dp),
        outs,
        scratch,
        1 + 10 + 7 + 8 + 2 * (n_dp - 1) + 6,
        3,
        "leave",
        [VMEM_SPEC] * 11 + [ANY_SPEC] * 2,
        [VMEM_SPEC] * 6 + [ANY_SPEC] * 2,
    )(*parts, *tokens, *grads, *outs_own, sums, mod, halves, ffn_mine, out_mine)


def share_kernel(part_ref, out_ref, send_sems, recv_sems):
    wires = Wires(send_sems, recv_sems)
    dp, x, tp = wires.dp, wires.x, wires.tp
    lanes = [(dp, x, lax.rem(tp + offset, 4)) for offset in range(1, 4)]
    wires.meet(lanes)
    copies = [wires.copy(part_ref, out_ref.at[tp], lane) for lane in lanes]
    out_ref[tp] = part_ref[...]
    for arrived in copies:
        arrived.wait_recv()
    wires.finish()


def share(part):
    return comm_call(
        share_kernel,
        jax.ShapeDtypeStruct((4,) + part.shape, F32),
        [],
        3,
        4,
        "share",
        [VMEM_SPEC],
        VMEM_SPEC,
    )(part)


def scatter_rows(grad):
    return lax.psum_scatter(grad, "dp", scatter_dimension=0, tiled=True)


def on_device(
    image_tokens,
    text_tokens,
    conditioning,
    ada_weight,
    ada_bias,
    qkv_weight,
    qv_bias,
    out_weight,
    out_bias,
    up_weight,
    up_bias,
    down_weight,
    down_bias,
    image_cotangent,
    text_cotangent,
):
    ctx_n, tp_n, dp_n = lax.axis_size("ctx"), lax.axis_size("tp"), lax.axis_size("dp")
    dp, ctx, tp = lax.axis_index("dp"), lax.axis_index("ctx"), lax.axis_index("tp")
    image_length, text_length, width = image_tokens.shape[1], text_tokens.shape[1], image_tokens.shape[2]
    slice_width = qkv_weight.shape[3]
    shard_rows = qkv_weight.shape[1]
    half = slice_width // ctx_n
    up_half = up_weight.shape[2] // ctx_n
    own_rows = (image_length // tp_n, TEXT_SLOTS // tp_n)
    image_all = image_length * ctx_n
    text_all = TEXT_SLOTS * ctx_n
    pad = ((0, TEXT_SLOTS - text_length), (0, 0))

    groups = dp_n if dp_n <= MOST_GROUPS else 1
    wide = 1 if groups > 1 else 2
    text_cols = up_half // groups
    text_start = ctx * up_half + (dp * text_cols if groups > 1 else 0)

    tokens = (image_tokens[0], jnp.pad(text_tokens[0], pad))
    cotangents = (image_cotangent[0], jnp.pad(text_cotangent[0], pad))

    def own(parts):
        return [lax.dynamic_slice_in_dim(part, tp * rows, rows, 0) for part, rows in zip(parts, own_rows)]

    tokens_own, cotangents_own = own(tokens), own(cotangents)
    cond_float = conditioning.astype(F32)
    activated_low = jax.nn.silu(cond_float).astype(BF16)
    partial_mod = jnp.einsum("nd,adkf->nakf", activated_low, ada_weight, preferred_element_type=F32)
    (
        mod_blocks,
        bias_blocks,
        image_blocks,
        text_blocks,
        text_gates,
        attn_full,
        ffn_mixed,
        moved,
    ) = enter(
        groups,
        partial_mod.reshape(dp_n, 12, slice_width),
        ada_bias.astype(F32).reshape(12, slice_width),
        jnp.concatenate([out_bias, down_bias], 0).astype(F32),
        *[part.reshape(tp_n, rows, width) for part, rows in zip(tokens, own_rows)],
        jnp.stack(
            [
                jnp.concatenate(
                    [qkv_weight[:, :, j, c * half : (c + 1) * half] for j in range(3)]
                    + [out_weight[:, :, c * half : (c + 1) * half]],
                    2,
                )
                for c in range(ctx_n)
            ]
        ),
        up_weight,
        down_weight,
        wide,
    )
    cotangents = (lax.optimization_barrier((cotangents[0], mod_blocks))[0], cotangents[1])
    image_other = lax.ppermute(cotangents[0], "ctx", [(0, 1), (1, 0)])
    attn_full = attn_full.reshape(2, width, 4 * half)
    ffn_blocks = [ffn_mixed.reshape(2 * wide, 2 * shard_rows, up_half)]
    around = [(i, (i + 1) % dp_n) for i in range(dp_n)]
    ffn_blocks.append(lax.ppermute(ffn_blocks[0], "dp", around))
    modulation = mod_blocks.transpose(1, 0, 2).reshape(2, 6, width)
    biases = bias_blocks.transpose(1, 0, 2).reshape(4, width)
    mod_rows = modulation[:, :, None]
    out_bias_rows, down_bias_rows = biases[:2, None], biases[2:, None]
    tokens_all = (image_blocks.reshape(image_all, width), text_blocks.reshape(text_all, width))
    qv_own = lax.dynamic_slice_in_dim(qv_bias, ctx * half, half, 2).astype(F32)
    up_bias_own = (
        lax.dynamic_slice_in_dim(up_bias[0], ctx * up_half, up_half, 0).astype(F32),
        lax.dynamic_slice_in_dim(up_bias[1], text_start, text_cols, 0).astype(F32),
    )
    slots = tp * own_rows[1] + lax.broadcasted_iota(jnp.int32, (own_rows[1], 1), 0)
    valid = jnp.broadcast_to((slots < text_length).astype(F32), (own_rows[1], width))

    own_ctx = jnp.full((1,), ctx, jnp.int32)

    def other_half(part):
        return lax.ppermute(part, "ctx", [(0, 1), (1, 0)])

    def blocks(part):
        return part.reshape(2, 2, 2, part.shape[0] // 8, width)

    qv_bias_rows = jnp.concatenate([qv_own[:, 0], jnp.zeros((2, half), F32), qv_own[:, 1]], 1)[:, None]
    normed_low, queries, keys, values, out_full = project(
        *tokens_all, mod_rows[:, :2], attn_full, qv_bias_rows
    )
    queries, ffn_blocks[1] = lax.optimization_barrier((queries, ffn_blocks[1]))
    for _ in range(dp_n - 3):
        ffn_blocks.append(lax.ppermute(ffn_blocks[-1], "dp", around))
    blended, lse, *out_parts = attend_forward(queries, keys, values, out_full, text_all, text_length)
    out_parts = [blocks(part) for part in out_parts]
    *attentions_middles, image_second, text_second, text_cots, moved_in, ffn_full = middle_step(
        groups, *out_parts, *tokens_own, mod_rows, out_bias_rows, moved, ffn_blocks, cotangents_own[1]
    )
    ffn_full = ffn_full.reshape(2 * wide, width, up_half)
    attentions, middles = attentions_middles[:2], attentions_middles[2:]
    second_low = (image_second.reshape(-1, width), text_second.reshape(-1, width))

    up_full, down_full = [(ffn_full, 0)], [(ffn_full, wide)]
    if groups > 1:
        moved_in = moved_in.reshape(width, 2 * text_cols)
        up_full.append((moved_in[None, :, :text_cols], 0))
        down_full.append((moved_in[None, :, text_cols:], 0))
        text_feed = (text_cots.reshape(-1, width), None, text_gates.reshape(groups, width))
    else:
        up_full.append((ffn_full, 1))
        down_full.append((ffn_full, 3))
        text_feed = (cotangents[1], other_half(cotangents[1]), mod_rows[1, 5])
    arrivals = ((cotangents[0], image_other, mod_rows[0, 5]), text_feed)
    feed_parts, second_parts, ffn_grads, up_bias_grads = [], [], [], []
    done = {}
    for stream in (1, 0):
        operands = (second_low[stream], *arrivals[stream], up_full[stream], down_full[stream], up_bias_own[stream])
        if groups > 1 and stream == 0:
            moved = done[1][2].reshape(dp_n * ctx_n, shard_rows, 2 * text_cols)
            *done[0], moved_in = feed_forward_moving(groups, *operands, moved)
        else:
            done[stream] = feed_forward(own_ctx, *operands)
    for stream in range(2):
        feed, pulled, grads, sums = done[stream]
        feed_parts.append(blocks(feed))
        second_parts.append(blocks(pulled))
        ffn_grads.append(grads)
        up_bias_grads.append(sums[0])
    if groups > 1:
        ffn_mine = scatter_rows(ffn_grads[0])
    else:
        ffn_mine = scatter_rows(jnp.concatenate(ffn_grads, 1))
    image_out, text_out, image_middle_grad, text_middle_grad, sums, image_attn, text_attn = turn_step(
        groups, valid, feed_parts, second_parts, attentions, middles, cotangents_own, mod_rows, down_bias_rows
    )
    attention_grad_all = (image_attn.reshape(-1, width), text_attn.reshape(-1, width))
    out_weight_grads = out_gradient(*attention_grad_all, blended)
    out_weight_grads, ffn_mine = lax.optimization_barrier((out_weight_grads, ffn_mine))
    out_mine = scatter_rows(out_weight_grads)
    grad_queries, grad_keys, grad_values = attend_backward(
        queries, keys, values, lse, *attention_grad_all, out_full, text_length
    )
    *normed_parts, qkv_weight_grads, joint_sums = unproject(
        grad_queries, grad_keys, grad_values, normed_low, attn_full, text_all
    )
    normed_parts = [blocks(part) for part in normed_parts]
    qkv_weight_grads, out_mine = lax.optimization_barrier((qkv_weight_grads, out_mine))
    qkv_mine = scatter_rows(qkv_weight_grads)

    def given(mine):
        return lax.dynamic_slice_in_dim(mine, (1 - ctx) * shard_rows, shard_rows, 0)

    qv_bias_grads = [
        jnp.concatenate([joint_sums[stream, 0, :half], joint_sums[stream, 0, 2 * half :]]) for stream in range(2)
    ]
    if groups > 1:
        up_bias_grads[1] = lax.dynamic_update_slice_in_dim(
            jnp.zeros((up_half,), F32), up_bias_grads[1], dp * text_cols, 0
        )
    halves = jnp.concatenate(
        [part.reshape(-1, slice_width) for part in (*qv_bias_grads, *up_bias_grads)], 0
    )
    image_outs, text_outs, image_grads, text_grads, packed, halves_all, ffn_other, out_other = leave_step(
        dp_n,
        normed_parts,
        tokens_own,
        (image_middle_grad, text_middle_grad),
        (image_out, text_out),
        sums,
        mod_rows,
        halves,
        ffn_mine,
        out_mine,
    )
    grad_mod_low = packed[:, :12].astype(BF16)
    ada_bias_grad = jnp.sum(grad_mod_low.astype(F32), axis=0).reshape(2, 6, slice_width)
    grad_mod_low = grad_mod_low.reshape(dp_n, 2, 6, slice_width)
    ada_weight_grad = jnp.einsum("nd,nakf->adkf", activated_low, grad_mod_low, preferred_element_type=F32)
    cond_partial = jnp.einsum("nakf,adkf->nd", grad_mod_low, ada_weight, preferred_element_type=F32)
    totals = jnp.sum(packed[:, 12:22], axis=0)
    cond_rows = jnp.pad(cond_partial, ((0, -dp_n % 2), (0, slice_width - shard_rows)))
    shared = share(jnp.concatenate([totals, cond_rows], 0))
    shared, qkv_given, image_outs, text_outs, out_other, ffn_other = lax.optimization_barrier(
        (shared, given(qkv_mine), image_outs, text_outs, out_other, ffn_other)
    )
    qkv_other = other_half(qkv_given)
    last_tokens = (image_outs, text_outs, image_grads, text_grads)
    if groups > 1:
        out_weight_grad, up_weight_grad, down_weight_grad, final_tokens = place_all(
            own_ctx, out_mine, out_other, ffn_mine, ffn_other, moved_in, last_tokens, image_length, text_length
        )
    else:
        final_tokens = place_tokens(last_tokens, image_length, text_length)
        out_weight_grad = place_out(own_ctx, out_mine, out_other)
        kept, other = lax.dynamic_slice_in_dim(ffn_mine, ctx * shard_rows, shard_rows, 0), ffn_other
        ffn_halves = [jnp.where(ctx == c, kept, other).astype(F32) for c in range(2)]
        up_weight_grad, down_weight_grad = [
            jnp.stack(
                [
                    jnp.concatenate([part[:, c * up_half : (c + 1) * up_half] for part in ffn_halves], 1)
                    for c in (i, 2 + i)
                ]
            )
            for i in range(2)
        ]
    qkv_weight_grad = place_qkv(own_ctx, qkv_mine, qkv_other)
    cond_total = jnp.sum(shared[:, 10 : 10 + dp_n, :shard_rows], axis=0)
    cond_grad = jax.vjp(jax.nn.silu, cond_float)[1](cond_total)[0]
    full = shared[:, :10].transpose(1, 0, 2).reshape(2, 5, width)
    bias_grads = lax.dynamic_slice_in_dim(full[:, :2], (dp * ctx_n + ctx) * shard_rows, shard_rows, 2)
    squares_total = jnp.sum(full[:, 2:], axis=2).T.reshape(6)
    counts = jnp.array([image_length, text_length] * 3, F32) * (dp_n * ctx_n * width)
    root_means = jnp.sqrt(squares_total / counts)
    half_sums = jnp.sum(halves_all, axis=0)
    qv_rows = half * 2 // slice_width
    up_rows = up_half // slice_width
    qv_bias_grad = (
        half_sums[:, : 2 * qv_rows].reshape(ctx_n, 2, 2, half).transpose(1, 2, 0, 3).reshape(2, 2, slice_width)
    )
    up_bias_grad = (
        half_sums[:, 2 * qv_rows : 2 * (qv_rows + up_rows)]
        .reshape(ctx_n, 2, up_half)
        .transpose(1, 0, 2)
        .reshape(2, ctx_n * up_half)
    )
    return (
        *final_tokens,
        cond_grad,
        ada_weight_grad,
        ada_bias_grad,
        qkv_weight_grad,
        qv_bias_grad,
        out_weight_grad,
        bias_grads[:, 1],
        up_weight_grad,
        up_bias_grad,
        down_weight_grad,
        bias_grads[:, 0],
        root_means,
    )


def solution(mesh):
    rows = P(None, ("dp", "ctx"))
    tokens = P("dp", "ctx", None)
    stacked = P(None, ("dp", "ctx"), None, "tp")
    matrix = P(None, ("dp", "ctx"), "tp")
    return jax.shard_map(
        on_device,
        mesh=mesh,
        in_specs=(
            tokens,
            tokens,
            rows,
            stacked,
            P(None, None, "tp"),
            stacked,
            P(None, None, "tp"),
            matrix,
            rows,
            matrix,
            P(None, "tp"),
            matrix,
            rows,
            tokens,
            tokens,
        ),
        out_specs=(
            tokens,
            tokens,
            tokens,
            tokens,
            rows,
            stacked,
            P(None, None, "tp"),
            stacked,
            P(None, None, "tp"),
            matrix,
            rows,
            matrix,
            P(None, "tp"),
            matrix,
            rows,
            P(),
        ),
        check_vma=False,
    )
```
